32 devices in a mesh: seq: 4 (over z), fsdp: 8 (over y, x, core).
Axes of the slice: x: 2, y: 2, z: 4, core: 2. Of those that a mesh axis runs over, the one named last changes fastest.
Arguments:
- tokens: bfloat16 [8, 2048, 512], P('fsdp', 'seq'), may hold values from -6 to 6
- memory: bfloat16 [8, 1024, 512], P('fsdp', 'seq'), may hold values from -6 to 6
- cotangent: bfloat16 [8, 2048, 512], P('fsdp', 'seq'), may hold values from -6 to 6
- w_query: bfloat16 [512, 512], P('fsdp'), may hold values from -0.375 to 0.375
- w_key: bfloat16 [512, 512], P('fsdp'), may hold values from -0.375 to 0.375
- w_value: bfloat16 [512, 512], P('fsdp'), may hold values from -0.25 to 0.25
- w_output: bfloat16 [512, 512], P('fsdp'), may hold values from -1.5 to 1.5
- b_query: bfloat16 [512], P('fsdp'), may hold values from -1.5 to 1.5
- b_value: bfloat16 [512], P('fsdp'), may hold values from -1.5 to 1.5
- b_output: bfloat16 [512], P('fsdp'), may hold values from -1.5 to 1.5
- gain_attend: bfloat16 [512], P('fsdp'), may hold values from 0.25 to 1.75
- shift_attend: bfloat16 [512], P('fsdp'), may hold values from -1.5 to 1.5
- u_query: bfloat16 [512, 512], P('fsdp'), may hold values from -0.375 to 0.375
- u_key: bfloat16 [512, 512], P('fsdp'), may hold values from -0.375 to 0.375
- u_value: bfloat16 [512, 512], P('fsdp'), may hold values from -0.25 to 0.25
- u_output: bfloat16 [512, 512], P('fsdp'), may hold values from -1.5 to 1.5
- c_query: bfloat16 [512], P('fsdp'), may hold values from -1.5 to 1.5
- c_value: bfloat16 [512], P('fsdp'), may hold values from -1.5 to 1.5
- c_output: bfloat16 [512], P('fsdp'), may hold values from -1.5 to 1.5
- gain_cross: bfloat16 [512], P('fsdp'), may hold values from 0.25 to 1.75
- shift_cross: bfloat16 [512], P('fsdp'), may hold values from -1.5 to 1.5
- w_expand: bfloat16 [512, 2048], P('fsdp'), may hold values from -0.25 to 0.25
- b_expand: bfloat16 [2048], P('fsdp'), may hold values from -1.5 to 1.5
- w_reduce: bfloat16 [2048, 512], P('fsdp'), may hold values from -0.1875 to 0.1875
- b_reduce: bfloat16 [512], P('fsdp'), may hold values from -1.5 to 1.5
- gain_feed: bfloat16 [512], P('fsdp'), may hold values from 0.25 to 1.75
- shift_feed: bfloat16 [512], P('fsdp'), may hold values from -1.5 to 1.5
Outputs:
- layer_out: bfloat16 [8, 2048, 512], P('fsdp', 'seq')
- grad_tokens: float32 [8, 2048, 512], P('fsdp', 'seq')
- grad_memory: float32 [8, 1024, 512], P('fsdp', 'seq')
- dw_query: float32 [512, 512], P('fsdp')
- dw_key: float32 [512, 512], P('fsdp')
- dw_value: float32 [512, 512], P('fsdp')
- dw_output: float32 [512, 512], P('fsdp')
- db_query: float32 [512], P('fsdp')
- db_value: float32 [512], P('fsdp')
- db_output: float32 [512], P('fsdp')
- dgain_attend: float32 [512], P('fsdp')
- dshift_attend: float32 [512], P('fsdp')
- du_query: float32 [512, 512], P('fsdp')
- du_key: float32 [512, 512], P('fsdp')
- du_value: float32 [512, 512], P('fsdp')
- du_output: float32 [512, 512], P('fsdp')
- dc_query: float32 [512], P('fsdp')
- dc_value: float32 [512], P('fsdp')
- dc_output: float32 [512], P('fsdp')
- dgain_cross: float32 [512], P('fsdp')
- dshift_cross: float32 [512], P('fsdp')
- dw_expand: float32 [512, 2048], P('fsdp')
- db_expand: float32 [2048], P('fsdp')
- dw_reduce: float32 [2048, 512], P('fsdp')
- db_reduce: float32 [512], P('fsdp')
- dgain_feed: float32 [512], P('fsdp')
- dshift_feed: float32 [512], P('fsdp')
The draws below stay inside these ranges and needn't reach their ends.
All inputs are finite; a program needn't handle non-finite values.
Results may differ from the reference program's by a relative error of at most 0.025.
The reference program's roundings to bfloat16 on the way count: a program that leaves them out, or rounds other values in their place, can miss the bound.
Values may be sent and summed in bfloat16 or wider, within the bound.
No kernel may reach another device: no remote copies, remote signals or barrier semaphores. Data moves between devices by JAX's collectives and lax.ppermute only.
A program may use at most 128 MiB of HBM per device.

```python
import jax
import jax.numpy as jnp
from jax import lax

D = 512
H = 8
HD = 64
FF = 2048
SEQS = 8
LEN = 2048
MEM = 1024


def spiked(values, rng, source, target, blocks, factor):
    def block_of(dim):
        return (jnp.arange(values.shape[dim]) // (values.shape[dim] // blocks)).reshape((-1,) + (1,) * (values.ndim - 1 - dim))

    first = jax.random.permutation(rng, blocks)[block_of(target)]
    second = (block_of(target) + blocks // 2) % blocks
    return jnp.where((block_of(source) == first) | (block_of(source) == second), factor * values, values)


def steps_of(key, dims, cuts, smallest, top_value):
    level, own = 1.0, jax.random.fold_in(key, 6)
    for position, parts in cuts:
        heights = jnp.exp(jax.random.uniform(jax.random.fold_in(own, position), (parts,), jnp.float32, smallest / len(cuts), top_value / len(cuts)))
        level = level * jnp.repeat(heights, dims[position] // parts).reshape([-1 if axis == position else 1 for axis in range(len(dims))])
    return level


def centred(own_key, shape, scale, reach, cuts=(), kind=jnp.bfloat16):
    drawn = jax.random.normal(own_key, shape, jnp.float32) * scale
    if len(cuts) > 0:
        drawn = steps_of(own_key, shape, cuts, -0.22, 0.18) * drawn
    return jnp.clip(drawn, min=-reach, max=reach).astype(kind)


def gaussian_with(own_key, extent, scale, reach, split, heavy, dtype=jnp.bfloat16):
    values = scale * jax.random.normal(own_key, extent, jnp.float32)
    if split:
        values = values * steps_of(own_key, extent, split, -0.22, 0.18)
    return jnp.clip(spiked(values, jax.random.fold_in(own_key, 3), *heavy), -reach, reach).astype(dtype)


def setup_inputs(seed: int = 0) -> dict:
    splits = jax.random.split(jax.random.key(seed), 28)
    tokens = centred(splits[0], (SEQS, LEN, D), 1.0, 6.0, ((0, 8), (1, 4)))
    memory = centred(splits[1], (SEQS, MEM, D), 1.0, 6.0, ((0, 8), (1, 4)))
    cotangent = gaussian_with(splits[2], (SEQS, LEN, D), 1.0, 6.0, ((0, 8), (1, 4)), (0, 2, 8, 2.0))
    w_query = centred(splits[3], (D, D), (D // 2) ** -0.5, 0.375, ((0, 8),))
    w_key = centred(splits[4], (D, D), (D // 2) ** -0.5, 0.375, ((0, 8),))
    w_value = centred(splits[5], (D, D), D ** -0.5, 0.25, ((0, 8),))
    w_output = centred(splits[6], (D, D), (max(1, D * 64 // LEN)) ** -0.5, 1.5, ((0, 8),))
    b_query = centred(splits[7], (D,), 0.3, 1.5, ((0, 8),))
    b_value = centred(splits[8], (D,), 0.3, 1.5, ((0, 8),))
    b_output = centred(splits[9], (D,), 0.3, 1.5, ((0, 8),))
    gain_attend = jnp.clip(1.0 + 0.15 * jax.random.normal(splits[10], (D,), jnp.float32), 0.25, 1.75).astype(jnp.bfloat16)
    shift_attend = centred(splits[11], (D,), 0.3, 1.5, ((0, 8),))
    u_query = centred(splits[12], (D, D), (D // 2) ** -0.5, 0.375, ((0, 8),))
    u_key = centred(splits[13], (D, D), (D // 2) ** -0.5, 0.375, ((0, 8),))
    u_value = centred(splits[14], (D, D), D ** -0.5, 0.25, ((0, 8),))
    u_output = centred(splits[15], (D, D), (max(1, D * 32 // MEM)) ** -0.5, 1.5, ((0, 8),))
    c_query = centred(splits[16], (D,), 0.3, 1.5, ((0, 8),))
    c_value = centred(splits[17], (D,), 0.3, 1.5, ((0, 8),))
    c_output = centred(splits[18], (D,), 0.3, 1.5, ((0, 8),))
    gain_cross = jnp.clip(1.0 + 0.15 * jax.random.normal(splits[19], (D,), jnp.float32), 0.25, 1.75).astype(jnp.bfloat16)
    shift_cross = centred(splits[20], (D,), 0.3, 1.5, ((0, 8),))
    w_expand = centred(splits[21], (D, FF), D ** -0.5, 0.25, ((0, 8),))
    b_expand = centred(splits[22], (FF,), 0.3, 1.5, ((0, 8),))
    w_reduce = centred(splits[23], (FF, D), (FF // 2) ** -0.5, 0.1875, ((0, 8),))
    b_reduce = centred(splits[24], (D,), 0.3, 1.5, ((0, 8),))
    gain_feed = jnp.clip(1.0 + 0.15 * jax.random.normal(splits[25], (D,), jnp.float32), 0.25, 1.75).astype(jnp.bfloat16)
    shift_feed = centred(splits[26], (D,), 0.3, 1.5, ((0, 8),))
    return {"tokens": tokens, "memory": memory, "cotangent": cotangent, "w_query": w_query, "w_key": w_key, "w_value": w_value, "w_output": w_output, "b_query": b_query, "b_value": b_value, "b_output": b_output, "gain_attend": gain_attend, "shift_attend": shift_attend, "u_query": u_query, "u_key": u_key, "u_value": u_value, "u_output": u_output, "c_query": c_query, "c_value": c_value, "c_output": c_output, "gain_cross": gain_cross, "shift_cross": shift_cross, "w_expand": w_expand, "b_expand": b_expand, "w_reduce": w_reduce, "b_reduce": b_reduce, "gain_feed": gain_feed, "shift_feed": shift_feed}


@jax.custom_vjp
def low(v):
    return lax.optimization_barrier(v.astype(jnp.bfloat16)).astype(jnp.float32)

@jax.custom_vjp
def low_back(v):
    return v

def low_keep(v):
    return (low(v), None)

def low_pass(kept, grad):
    return (grad,)

def back_keep(v):
    return (v, None)

def back_low(kept, grad):
    return (low(grad),)
low.defvjp(low_keep, low_pass)
low_back.defvjp(back_keep, back_low)
EPS = 1e-05
HIGH = lax.Precision.HIGHEST

def dense(left, right):
    return jnp.dot(left, right, precision=HIGH, preferred_element_type=jnp.float32)

def both_ways(value):
    return low(low_back(value))

def norm_rows(hidden, gain, shift):
    centre = lax.optimization_barrier(jnp.mean(hidden, axis=-1, keepdims=True))
    offset = hidden - centre
    spread = lax.optimization_barrier(jnp.mean(offset * offset, axis=-1, keepdims=True))
    return offset * lax.rsqrt(spread + EPS) * gain + shift

def attention(queries, keys_all, values_all):
    length = queries.shape[0]
    count = keys_all.shape[0]
    block = min(512, length)
    scale = HD ** (-0.5)
    keys_h = keys_all.reshape(count, H, HD)
    values_h = values_all.reshape(count, H, HD)

    def one_block(q_block):
        q_heads = q_block.reshape(block, H, HD)
        scores = low_back(jnp.einsum('bhd,khd->hbk', q_heads, keys_h, precision=HIGH) * scale)
        top = lax.optimization_barrier(jnp.max(scores, axis=-1, keepdims=True))
        expo = jnp.exp(scores - top)
        probs = low(expo / lax.optimization_barrier(jnp.sum(expo, axis=-1, keepdims=True)))
        mixed = jnp.einsum('hbk,khd->bhd', probs, values_h, precision=HIGH)
        return mixed.reshape(block, H * HD)
    outs = lax.map(jax.checkpoint(one_block), queries.reshape(length // block, block, H * HD))
    return outs.reshape(length, H * HD)

def forward(params, rows_in, mem_in):
    w_query, w_key, w_value, w_output, b_query, b_value, b_output, gain_attend, shift_attend, u_query, u_key, u_value, u_output, c_query, c_value, c_output, gain_cross, shift_cross, w_expand, b_expand, w_reduce, b_reduce, gain_feed, shift_feed = params
    queries = both_ways(dense(rows_in, w_query) + b_query)
    keys_in = both_ways(dense(rows_in, w_key))
    values_in = both_ways(dense(rows_in, w_value) + b_value)
    attended = both_ways(attention(queries, keys_in, values_in))
    branch_one = low_back(dense(attended, w_output) + b_output)
    first = norm_rows(rows_in + branch_one, gain_attend, shift_attend)
    first_low = low(first)
    cross_queries = both_ways(dense(first_low, u_query) + c_query)
    mem_keys = both_ways(dense(mem_in, u_key))
    mem_values = both_ways(dense(mem_in, u_value) + c_value)
    cross_attended = both_ways(attention(cross_queries, mem_keys, mem_values))
    branch_two = low_back(dense(cross_attended, u_output) + c_output)
    second = norm_rows(first + branch_two, gain_cross, shift_cross)
    second_low = low(second)
    pre_act = low_back(dense(second_low, w_expand) + b_expand)
    act_low = low(jax.nn.gelu(pre_act, approximate=True))
    branch_three = low_back(dense(act_low, w_reduce) + b_reduce)
    return norm_rows(second + branch_three, gain_feed, shift_feed)

def reference(tokens, memory, cotangent, w_query, w_key, w_value, w_output, b_query, b_value, b_output, gain_attend, shift_attend, u_query, u_key, u_value, u_output, c_query, c_value, c_output, gain_cross, shift_cross, w_expand, b_expand, w_reduce, b_reduce, gain_feed, shift_feed):
    params = tuple((item.astype(jnp.float32) for item in (w_query, w_key, w_value, w_output, b_query, b_value, b_output, gain_attend, shift_attend, u_query, u_key, u_value, u_output, c_query, c_value, c_output, gain_cross, shift_cross, w_expand, b_expand, w_reduce, b_reduce, gain_feed, shift_feed)))

    def one_sequence(totals, items):
        rows_in, mem_in, upstream = items
        result, backward = jax.vjp(forward, params, rows_in.astype(jnp.float32), mem_in.astype(jnp.float32))
        grad_params, grad_rows, grad_mem = backward(upstream.astype(jnp.float32))
        totals = tuple((left + right for left, right in zip(totals, grad_params)))
        return (totals, (result.astype(jnp.bfloat16), grad_rows, grad_mem))
    zeros = tuple((jnp.zeros_like(item) for item in params))
    totals, (layer_out, grad_tokens, grad_memory) = lax.scan(one_sequence, zeros, (tokens, memory, cotangent))
    return (layer_out, grad_tokens, grad_memory) + totals
```

```python
import functools

import jax
import jax.numpy as jnp
from jax import lax
from jax.experimental import pallas as pl
from jax.experimental.pallas import tpu as pltpu
from jax.sharding import PartitionSpec as P

HD = 64
D = 512
EPS = 1e-05
SCALE = HD ** (-0.5)
BF = jnp.bfloat16
F32 = jnp.float32

B_QUERY, B_VALUE, B_OUTPUT, GAIN_A, SHIFT_A = 0, 1, 2, 3, 4
C_QUERY, C_VALUE, C_OUTPUT, GAIN_B, SHIFT_B = 5, 6, 7, 8, 9
B_REDUCE, GAIN_C, SHIFT_C, B_EXPAND = 10, 11, 12, 13
N_VEC = 17
VEC_ROWS = 32

AT_EXPAND, AT_WO, AT_UQ, AT_UK, AT_UV, AT_UO = 4, 8, 9, 10, 11, 12


def dot(a, b, ca, cb):
    return lax.dot_general(a, b, (((ca,), (cb,)), ((), ())), preferred_element_type=F32)


def params(mib=56):
    return pltpu.CompilerParams(vmem_limit_bytes=mib << 20)


def cost(flops, nbytes, trans=0):
    return pl.CostEstimate(flops=flops, bytes_accessed=nbytes, transcendentals=trans)


def shape(dims, dtype):
    return jax.ShapeDtypeStruct(dims, dtype)


def whole(x):
    nd = x.ndim
    return pl.BlockSpec(x.shape, lambda i: (0,) * nd)


def norm(hidden):
    centre = jnp.mean(hidden, axis=-1, keepdims=True)
    offset = hidden - centre
    spread = jnp.mean(offset * offset, axis=-1, keepdims=True)
    r = lax.rsqrt(spread + EPS)
    return offset * r, r


def norm_back(e, gain, n, r):
    t = e * gain
    return r * (t - jnp.mean(t, axis=-1, keepdims=True) - n * jnp.mean(t * n, axis=-1, keepdims=True))


def total(x):
    return jnp.sum(x, axis=0, keepdims=True)


def square(ref):
    return ref[...].reshape(-1, ref.shape[-1])


def assemble_kernel(rows, f_ref, own, r1, r2, r3, *rest):
    outs, sems = rest[:-1], rest[-1]
    f = f_ref[0]
    c = lax.rem(f, 2)
    a = 2 + 2 * c
    b = 4 - 2 * c
    n = own.shape[0]
    pieces = (
        (own, 0, 0), (r1, 0, a), (r2, 0, b), (r2, n, 6),
        (r3, 0, 1), (r3, n, b + 1), (r3, 2 * n, a + 1), (r3, 3 * n, 7),
    )
    copies = []
    for j, (src, base, off) in enumerate(pieces):
        at = pl.multiple_of(jnp.bitwise_xor(f, off) * rows, rows)
        for k, out in enumerate(outs):
            copy = pltpu.make_async_copy(
                src.at[pl.ds(base + k * rows, rows), :], out.at[pl.ds(at, rows), :], sems.at[j, k]
            )
            copy.start()
            copies.append(copy)
    for copy in copies:
        copy.wait()


def assemble(f, rows, count, own, r1, r2, r3):
    anyspec = pl.BlockSpec(memory_space=pl.ANY)
    return pl.pallas_call(
        functools.partial(assemble_kernel, rows),
        in_specs=[pl.BlockSpec(memory_space=pltpu.SMEM)] + [anyspec] * 4,
        out_specs=[anyspec] * count,
        out_shape=[shape((8 * rows, D), BF)] * count,
        scratch_shapes=[pltpu.SemaphoreType.DMA((8, count))],
        name="assemble",
    )(f.reshape(1).astype(jnp.int32), own, r1, r2, r3)


def project_kernel(n, *refs):
    chunks = refs[:n]
    wq, wk, wv, vec, q_ref, k_ref, v_ref = refs[n:]
    bq = vec[B_QUERY : B_QUERY + 1, :]
    bv = vec[B_VALUE : B_VALUE + 1, :]
    for i, chunk in enumerate(chunks):
        x = chunk[...]
        m = x.shape[0]
        if i == 0:
            q_ref[...] = (dot(x, wq[...], 1, 0) + bq).astype(BF)
        k_ref[pl.ds(i * m, m), :] = dot(x, wk[...], 1, 0).astype(BF)
        v_ref[pl.ds(i * m, m), :] = (dot(x, wv[...], 1, 0) + bv).astype(BF)


def project(chunks, wq, wk, wv, vec):
    m = chunks[0].shape[0]
    n = len(chunks)
    return pl.pallas_call(
        functools.partial(project_kernel, n),
        out_shape=[shape((m, D), BF), shape((n * m, D), BF), shape((n * m, D), BF)],
        compiler_params=params(),
        cost_estimate=cost(2 * (2 * n + 1) * m * D * D, 4 * n * m * D * 2),
        name="project",
    )(*chunks, wq, wk, wv, vec)


def project_memory_kernel(n, *refs):
    chunks = refs[:n]
    uk, uv, vec, k_ref, v_ref = refs[n:]
    cv = vec[C_VALUE : C_VALUE + 1, :]
    for i, chunk in enumerate(chunks):
        x = chunk[...]
        m = x.shape[0]
        k_ref[pl.ds(i * m, m), :] = dot(x, square(uk), 1, 0).astype(BF)
        v_ref[pl.ds(i * m, m), :] = (dot(x, square(uv), 1, 0) + cv).astype(BF)


def project_memory(chunks, bulk, vec):
    m = chunks[0].shape[0]
    n = len(chunks)
    (uk, uk_spec), (uv, uv_spec) = bulk(AT_UK), bulk(AT_UV)
    return pl.pallas_call(
        functools.partial(project_memory_kernel, n),
        grid=(1,),
        in_specs=[whole(c) for c in chunks] + [uk_spec, uv_spec, whole(vec)],
        out_specs=[pl.BlockSpec((n * m, D), lambda i: (0, 0))] * 2,
        out_shape=[shape((n * m, D), BF)] * 2,
        compiler_params=params(),
        cost_estimate=cost(4 * n * m * D * D, 4 * n * m * D * 2),
        name="project_memory",
    )(*chunks, uk, uv, vec)


def attend_kernel(block, q_ref, k_ref, v_ref, o_ref, lse_ref):
    lane = lax.broadcasted_iota(jnp.int32, (block, 128), 1) < HD
    k = k_ref[...]
    v = v_ref[...]
    for i in range(q_ref.shape[0] // block):
        rows = pl.ds(i * block, block)
        q = q_ref[rows, :] * BF(SCALE)
        outs = []
        for a in range(2):
            qm = jnp.where(lane == (a == 0), q, jnp.zeros_like(q))
            s = dot(qm, k, 1, 1)
            top = jnp.max(s, axis=1, keepdims=True)
            p = jnp.exp(s - top)
            count = jnp.sum(p, axis=1, keepdims=True)
            outs.append(dot(p.astype(BF), v, 1, 0) / count)
            lse = jnp.broadcast_to(top + jnp.log(count), (block, 128))
            lse_ref[a, :, rows] = lse.T[:8]
        o_ref[rows, :] = jnp.where(lane, outs[0], outs[1]).astype(BF)


def attend(q, k, v):
    n, kv = q.shape[0], k.shape[0]
    pairs = D // 128

    def cols(m):
        return pl.BlockSpec((m, 128), lambda h: (0, h))

    return pl.pallas_call(
        functools.partial(attend_kernel, 256),
        grid=(pairs,),
        in_specs=[cols(n), cols(kv), cols(kv)],
        out_specs=[cols(n), pl.BlockSpec((2, 8, n), lambda h: (h, 0, 0))],
        out_shape=[shape((n, D), BF), shape((2 * pairs, 8, n), F32)],
        compiler_params=params(),
        cost_estimate=cost(16 * n * kv * D, 4 * kv * D, 8 * n * kv),
        name="attend",
    )(q, k, v)


def attend_back_kernel(block, q_ref, k_ref, v_ref, g_ref, o_ref, lse_ref, dq_ref, dk_ref, dv_ref):
    n, kv = q_ref.shape[0], k_ref.shape[0]
    g = g_ref[...]
    q = q_ref[...] * BF(SCALE)
    lane = lax.broadcasted_iota(jnp.int32, (n, 128), 1) < HD
    go = (g.astype(F32) * o_ref[...].astype(F32)).T
    delta = [jnp.sum(go[HD * a : HD * a + HD], axis=0, keepdims=True) for a in range(2)]
    zero = jnp.zeros_like(q)
    qm = [jnp.where(lane == (a == 0), q, zero) for a in range(2)]
    gm = [jnp.where(lane == (a == 0), g, zero) for a in range(2)]
    top_half = lax.broadcasted_iota(jnp.int32, (128, n), 0) < HD
    dqt = jnp.zeros((128, n), F32)
    for j in range(kv // block):
        rows = pl.ds(j * block, block)
        k = k_ref[rows, :]
        v = v_ref[rows, :]
        dk = jnp.zeros((block, 128), F32)
        dv = jnp.zeros((block, 128), F32)
        dqs = []
        for a in range(2):
            p = jnp.exp(dot(k, qm[a], 1, 1) - lse_ref[a, 0:1, :])
            dp = dot(v, gm[a], 1, 1)
            ds = (p * (dp - delta[a])).astype(BF)
            dv = dv + dot(p.astype(BF), gm[a], 1, 0)
            dk = dk + dot(ds, qm[a], 1, 0)
            dqs.append(dot(k, ds, 0, 0))
        dqt = dqt + jnp.where(top_half, dqs[0], dqs[1])
        dk_ref[rows, :] = dk.astype(BF)
        dv_ref[rows, :] = dv.astype(BF)
    dq_ref[...] = (dqt.T * SCALE).astype(BF)


def attend_back(q, k, v, g, o, lse):
    n, kv = q.shape[0], k.shape[0]
    pairs = D // 128

    def cols(m):
        return pl.BlockSpec((m, 128), lambda h: (0, h))

    return pl.pallas_call(
        functools.partial(attend_back_kernel, 1024),
        grid=(pairs,),
        in_specs=[cols(n), cols(kv), cols(kv), cols(n), cols(n)]
        + [pl.BlockSpec((2, 8, n), lambda h: (h, 0, 0))],
        out_specs=[cols(n), cols(kv), cols(kv)],
        out_shape=[shape((n, D), BF), shape((kv, D), BF), shape((kv, D), BF)],
        compiler_params=params(),
        cost_estimate=cost(40 * n * kv * D, 8 * kv * D, 8 * n * kv),
        name="attend_back",
    )(q, k, v, g, o, lse)


def after_self_kernel(o, x, wo, uq, vec, n_ref, r_ref, low_ref, cq_ref):
    def v(i):
        return vec[i : i + 1, :]

    sum_one = x[...].astype(F32) + dot(o[...], square(wo), 1, 0) + v(B_OUTPUT)
    n, r = norm(sum_one)
    low = (n * v(GAIN_A) + v(SHIFT_A)).astype(BF)
    n_ref[...] = n
    r_ref[...] = jnp.broadcast_to(r, r_ref.shape)
    low_ref[...] = low
    cq_ref[...] = (dot(low, square(uq), 1, 0) + v(C_QUERY)).astype(BF)


def after_self(o, x, bulk, vec):
    (wo, wo_spec), (uq, uq_spec) = bulk(AT_WO), bulk(AT_UQ)
    m = x.shape[0]
    outs = [shape((m, D), F32), shape((m, 128), F32), shape((m, D), BF), shape((m, D), BF)]
    return pl.pallas_call(
        after_self_kernel,
        grid=(1,),
        in_specs=[whole(o), whole(x), wo_spec, uq_spec, whole(vec)],
        out_specs=[whole(s) for s in outs],
        out_shape=outs,
        compiler_params=params(),
        cost_estimate=cost(4 * m * D * D, 12 * m * D),
        name="after_self",
    )(o, x, wo, uq, vec)


GELU_C = 0.7978845608028654
GELU_A = 0.044715


def feed_kernel(ca, n1, cot, e0, e1, e2, e3, wred_ref, uo, vec,
                out_ref, two_ref, catt_ref, dexp_ref, dred_ref, duo_ref, dvec_ref):
    def v(i):
        return vec[i : i + 1, :]

    expand = (e0, e1, e2, e3)
    wred = square(wred_ref)
    first = n1[...] * v(GAIN_A) + v(SHIFT_A)
    sum_two = first + dot(ca[...], square(uo), 1, 0) + v(C_OUTPUT)
    n2, r2 = norm(sum_two)
    second = n2 * v(GAIN_B) + v(SHIFT_B)
    low = second.astype(BF)
    sum_three = second + v(B_REDUCE)
    acts, slopes = [], []
    for j in range(4):
        pre = dot(low, square(expand[j]), 1, 0) + v(B_EXPAND + j)
        sq = pre * pre
        t = jnp.tanh(GELU_C * (pre + GELU_A * (sq * pre)))
        half = 0.5 * (1.0 + t)
        act = (pre * half).astype(BF)
        slope = half + 0.5 * pre * (1.0 - t * t) * (GELU_C * (1.0 + 3.0 * GELU_A * sq))
        acts.append(act)
        slopes.append(slope)
        sum_three = sum_three + dot(act, wred[j * D : (j + 1) * D], 1, 0)
    n3, r3 = norm(sum_three)
    out_ref[...] = (n3 * v(GAIN_C) + v(SHIFT_C)).astype(BF)
    e = cot[...].astype(F32)
    d_three = norm_back(e, v(GAIN_C), n3, r3)
    branch = d_three.astype(BF)
    dvec_ref[0:1, :] = total(branch.astype(F32))
    dvec_ref[1:2, :] = total(e * n3)
    dvec_ref[2:3, :] = total(e)
    second_grad = d_three
    for j in range(4):
        d_act = dot(branch, wred[j * D : (j + 1) * D], 1, 1)
        d_pre = (d_act * slopes[j]).astype(BF)
        dvec_ref[3 + j : 4 + j, :] = total(d_pre.astype(F32))
        dexp_ref[j * D : (j + 1) * D, :] = dot(low, d_pre, 0, 0).astype(BF)
        dred_ref[j * D : (j + 1) * D, :] = dot(acts[j], branch, 0, 0).astype(BF)
        second_grad = second_grad + dot(d_pre, square(expand[j]), 1, 1)
    d_two = norm_back(second_grad, v(GAIN_B), n2, r2)
    two_ref[...] = d_two
    cross = d_two.astype(BF)
    dvec_ref[7:8, :] = total(second_grad * n2)
    dvec_ref[8:9, :] = total(second_grad)
    dvec_ref[9:10, :] = total(cross.astype(F32))
    duo_ref[...] = dot(ca[...], cross, 0, 0).astype(BF)
    catt_ref[...] = dot(cross, square(uo), 1, 1).astype(BF)


def feed(ca, n1, cot, bulk, wred, vec):
    m = ca.shape[0]
    arrays, specs = [ca, n1, cot], [whole(ca), whole(n1), whole(cot)]
    for j in range(4):
        w, s = bulk(AT_EXPAND + j)
        arrays.append(w)
        specs.append(s)
    for w, s in (wred, bulk(AT_UO), (vec, whole(vec))):
        arrays.append(w)
        specs.append(s)
    outs = [
        shape((m, D), BF), shape((m, D), F32), shape((m, D), BF),
        shape((4 * D, D), BF), shape((4 * D, D), BF), shape((D, D), BF), shape((16, D), F32),
    ]
    return pl.pallas_call(
        feed_kernel,
        grid=(1,),
        in_specs=specs,
        out_specs=[whole(s) for s in outs],
        out_shape=outs,
        compiler_params=params(),
        cost_estimate=cost(2 * 27 * m * D * D, 24 * m * D * 4, 4 * m * D),
        name="feed",
    )(*arrays)


def after_cross_back_kernel(count, *refs):
    mems = refs[:count]
    (gq, gk, gv, low, o, two, n1, r1, uq, uk, uv, wo, vec,
     one_ref, att_ref, dw_ref, mine_ref, rest_ref, dvec_ref) = refs[count:]
    gain = vec[GAIN_A : GAIN_A + 1, :]
    m = mems[0].shape[0]
    for i in range(count):
        rows = pl.ds(i * m, m)
        part = dot(gk[rows, :], square(uk), 1, 1) + dot(gv[rows, :], square(uv), 1, 1)
        if i == 0:
            mine_ref[...] = part
        else:
            rest_ref[pl.ds((i - 1) * m, m), :] = part.astype(BF)
    first_grad = two[...] + dot(gq[...], square(uq), 1, 1)
    n = n1[...]
    d_one = norm_back(first_grad, gain, n, r1[:, 0:1])
    one_ref[...] = d_one
    low_one = d_one.astype(BF)
    att_ref[...] = dot(low_one, square(wo), 1, 1).astype(BF)
    dvec_ref[0:1, :] = total(gq[...].astype(F32))
    dvec_ref[1:2, :] = total(gv[...].astype(F32))
    dvec_ref[2:3, :] = total(first_grad * n)
    dvec_ref[3:4, :] = total(first_grad)
    dvec_ref[4:5, :] = total(low_one.astype(F32))
    dw_ref[0:D, :] = dot(low[...], gq[...], 0, 0).astype(BF)
    dk = jnp.zeros((D, D), F32)
    dv = jnp.zeros((D, D), F32)
    for i in range(count):
        rows = pl.ds(i * m, m)
        dk = dk + dot(mems[i][...], gk[rows, :], 0, 0)
        dv = dv + dot(mems[i][...], gv[rows, :], 0, 0)
    dw_ref[D : 2 * D, :] = dk.astype(BF)
    dw_ref[2 * D : 3 * D, :] = dv.astype(BF)
    dw_ref[3 * D : 4 * D, :] = dot(o[...], low_one, 0, 0).astype(BF)


def after_cross_back(mems, gq, gk, gv, low, o, two, n1, r1, bulk, vec):
    m = gq.shape[0]
    k = mems[0].shape[0]
    count = len(mems)
    arrays = list(mems) + [gq, gk, gv, low, o, two, n1, r1]
    specs = [whole(a) for a in arrays]
    for at in (AT_UQ, AT_UK, AT_UV, AT_WO):
        w, s = bulk(at)
        arrays.append(w)
        specs.append(s)
    arrays.append(vec)
    specs.append(whole(vec))
    outs = [
        shape((m, D), F32), shape((m, D), BF), shape((4 * D, D), BF),
        shape((k, D), F32), shape(((count - 1) * k, D), BF), shape((8, D), F32),
    ]
    return pl.pallas_call(
        functools.partial(after_cross_back_kernel, count),
        grid=(1,),
        in_specs=specs,
        out_specs=[whole(s) for s in outs],
        out_shape=outs,
        compiler_params=params(),
        cost_estimate=cost(2 * 12 * m * D * D, 20 * m * D * 4),
        name="after_cross_back",
    )(*arrays)


def last_kernel(count, *refs):
    chunks = refs[:count]
    gq, gk, gv, one, wq, wk, wv, dw_ref, mine_ref, rest_ref, dvec_ref = refs[count:]
    m = chunks[0].shape[0]
    for i in reversed(range(count)):
        rows = pl.ds(i * m, m)
        part = dot(gk[rows, :], wk[...], 1, 1) + dot(gv[rows, :], wv[...], 1, 1)
        if i == 0:
            mine_ref[...] = part + one[...] + dot(gq[...], wq[...], 1, 1)
        else:
            rest_ref[pl.ds((i - 1) * m, m), :] = part.astype(BF)
    dvec_ref[0:1, :] = total(gq[...].astype(F32))
    dvec_ref[1:2, :] = total(gv[...].astype(F32))
    dw_ref[0:D, :] = dot(chunks[0][...], gq[...], 0, 0).astype(BF)
    dk = jnp.zeros((D, D), F32)
    dv = jnp.zeros((D, D), F32)
    for i in range(count):
        rows = pl.ds(i * m, m)
        dk = dk + dot(chunks[i][...], gk[rows, :], 0, 0)
        dv = dv + dot(chunks[i][...], gv[rows, :], 0, 0)
    dw_ref[D : 2 * D, :] = dk.astype(BF)
    dw_ref[2 * D : 3 * D, :] = dv.astype(BF)


def last(chunks, gq, gk, gv, one, wq, wk, wv):
    m = gq.shape[0]
    count = len(chunks)
    outs = [shape((3 * D, D), BF), shape((m, D), F32), shape(((count - 1) * m, D), BF), shape((8, D), F32)]
    return pl.pallas_call(
        functools.partial(last_kernel, count),
        out_shape=outs,
        compiler_params=params(),
        cost_estimate=cost(2 * 18 * m * D * D, 20 * m * D * 4),
        name="last",
    )(*chunks, gq, gk, gv, one, wq, wk, wv)


ENDS_IN = ((1, 0), (2, 3))
ENDS_OUT = ((0, 1), (3, 2))
MIDDLE = ((1, 2), (2, 1))
PAIRS = ((0, 1), (1, 0), (2, 3), (3, 2))
ACROSS = ((0, 2), (2, 0), (1, 3), (3, 1))


def over_seq(x, pairs):
    return lax.ppermute(x, "seq", pairs)


def gather_line(own):
    z = lax.axis_index("seq")
    middle = (z == 1) | (z == 2)
    a = over_seq(own, PAIRS)
    b = over_seq(own, MIDDLE)
    d = over_seq(a, MIDDLE)
    c = over_seq(b, ENDS_IN)
    e = over_seq(d, ENDS_IN)
    return a, jnp.where(middle, b, c), jnp.where(middle, d, e)


def scatter_line(mine, one, two, three):
    def add(p, r):
        return (p.astype(F32) + r.astype(F32)).astype(BF)

    e = over_seq(three, ENDS_OUT)
    c = over_seq(two, ENDS_OUT)
    d = over_seq(add(three, e), MIDDLE)
    b = over_seq(add(two, c), MIDDLE)
    a = over_seq(add(one, d), PAIRS)
    return mine + a.astype(F32) + b.astype(F32)


def swap_core():
    return [(i, i ^ 1) for i in range(8)]


def swap_first():
    return [(i, i ^ (4 if i & 1 else 2)) for i in range(8)]


def swap_second():
    return [(i, i ^ (2 if i & 1 else 4)) for i in range(8)]


def gather_plane(own):
    r1 = lax.ppermute(own, "fsdp", swap_first())
    both = jnp.concatenate([own, r1])
    r2 = lax.ppermute(both, "fsdp", swap_second())
    r3 = lax.ppermute(jnp.concatenate([both, r2]), "fsdp", swap_core())
    return r1, r2, r3


def reduce_plane(blocks, f):
    c = lax.rem(f, 2)
    x = lax.rem(f // 2, 2)
    y = f // 4

    def pick(parity):
        return jnp.concatenate(
            [lax.dynamic_index_in_dim(b.reshape(4, 2, *b.shape[1:]), parity, 1, False) for b in blocks], 1
        )

    got = lax.ppermute(pick(1 - c), "fsdp", swap_core())
    u = pick(c).astype(F32) + got.astype(F32)

    def at(i):
        return lax.dynamic_index_in_dim(u, i, 0, False)

    even = c == 0
    keep0 = jnp.where(even, x, 2 * y)
    keep1 = jnp.where(even, 2 + x, 2 * y + 1)
    send0 = jnp.where(even, 1 - x, 2 * (1 - y))
    send1 = jnp.where(even, 3 - x, 3 - 2 * y)
    out = jnp.stack([at(send0), at(send1)]).astype(BF)
    got = lax.ppermute(out, "fsdp", swap_first())
    v0 = at(keep0) + got[0].astype(F32)
    v1 = at(keep1) + got[1].astype(F32)
    own = jnp.where(even, y, x) == 0
    got = lax.ppermute(jnp.where(own, v1, v0).astype(BF), "fsdp", swap_second())
    return jnp.where(own, v0, v1) + got.astype(F32)


def reduce_all(blocks, f, size):
    if size == 8:
        part = reduce_plane(blocks, f)
    else:
        part = lax.psum_scatter(
            jnp.concatenate(blocks, 1), "fsdp", scatter_dimension=0, tiled=False
        ).astype(F32)
    part = part.astype(BF)
    got = over_seq(part, PAIRS)
    half = (part.astype(F32) + got.astype(F32)).astype(BF)
    got = over_seq(half, ACROSS)
    return half.astype(F32) + got.astype(F32)


def on_device(size, tokens, memory, cotangent,
              w_query, w_key, w_value, w_output, b_query, b_value, b_output, gain_attend, shift_attend,
              u_query, u_key, u_value, u_output, c_query, c_value, c_output, gain_cross, shift_cross,
              w_expand, b_expand, w_reduce, b_reduce, gain_feed, shift_feed):
    rows = w_query.shape[0]
    f = lax.axis_index("fsdp")
    x = tokens[0]
    mem = memory[0]

    vectors = (b_query, b_value, b_output, gain_attend, shift_attend, c_query, c_value, c_output,
               gain_cross, shift_cross, b_reduce, gain_feed, shift_feed)
    table = jnp.concatenate([jnp.stack(vectors), b_expand.reshape(4, rows)])
    table = jnp.pad(table, ((0, VEC_ROWS - N_VEC), (0, D - rows)))
    first = jnp.concatenate([w_query, w_key, w_value, table])
    pack = jnp.concatenate(
        [w_reduce] + [w_expand[:, j * D : (j + 1) * D] for j in range(4)]
        + [w_output, u_query, u_key, u_value, u_output]
    )
    chunks = (x,) + gather_line(x)
    if size == 8:
        r1, r2, r3 = gather_plane(first)
        wq, wk, wv = assemble(f, rows, 3, first, r1, r2, r3)
        n = first.shape[0]
        tables = [first, r1, r2[:n], r2[n:]] + [r3[i * n : (i + 1) * n] for i in range(4)]
        tables = jnp.stack([t[3 * rows : 3 * rows + N_VEC, :rows] for t in tables])
        c = lax.rem(f, 2)
        a, b = 2 + 2 * c, 4 - 2 * c
        offsets = jnp.stack([0 * c, a, b, 6 + 0 * c, 1 + 0 * c, b + 1, a + 1, 7 + 0 * c])
        pick = (jnp.arange(8)[:, None] == (offsets ^ f)[None, :]).astype(BF)
        tables = jnp.einsum("gd,dkl->gkl", pick, tables, preferred_element_type=F32)
    else:
        g = lax.all_gather(first, "fsdp", axis=0, tiled=False)
        wq, wk, wv = [g[:, i * rows : (i + 1) * rows].reshape(D, D) for i in range(3)]
        tables = g[:, 3 * rows : 3 * rows + N_VEC, :rows].astype(F32)
    vec = jnp.concatenate(
        [tables[:, :B_EXPAND].transpose(1, 0, 2).reshape(B_EXPAND, D), tables[:, B_EXPAND:].reshape(4, D)]
    )
    vec = jnp.pad(vec, ((0, VEC_ROWS - N_VEC), (0, 0)))

    everything = lax.all_gather(pack, "fsdp", axis=0, tiled=False)

    def bulk(at, count=1):
        if rows % 16 == 0:
            return everything, pl.BlockSpec((size, count * rows, D), lambda i: (0, at // count, 0))
        w = everything[:, at * rows : (at + count) * rows].reshape(1, count * D, D)
        return w, whole(w)

    q, k, v = project(chunks, wq, wk, wv, vec)
    o, lse = attend(q, k, v)
    mems = (mem,) + gather_line(mem)
    mk, mv = project_memory(mems, bulk, vec)
    n1, r_one, low, cq = after_self(o, x, bulk, vec)
    ca, cross_lse = attend(cq, mk, mv)
    layer_out, d_two, d_catt, d_exp, d_red, d_uo, dvec_feed = feed(
        ca, n1, cotangent[0], bulk, bulk(0, 4), vec
    )

    def by_owner(stack, count):
        s = stack.reshape(count, size, rows, D)
        return s.transpose(1, 0, 2, 3).reshape(size, count * rows, D)

    sum_feed = reduce_all([d_red.reshape(size, 4 * rows, D), by_owner(d_exp, 4), by_owner(d_uo, 1)], f, size)
    gq, gk, gv = attend_back(cq, mk, mv, d_catt, ca, cross_lse)
    d_one, d_att, d_mid, mem_mine, mem_rest, dvec_mid = after_cross_back(
        mems, gq, gk, gv, low, o, d_two, n1, r_one, bulk, vec
    )
    m = mem.shape[0]
    grad_mem = scatter_line(mem_mine, mem_rest[:m], mem_rest[m : 2 * m], mem_rest[2 * m :])
    sum_mid = reduce_all([by_owner(d_mid, 4)], f, size)
    gq, gk, gv = attend_back(q, k, v, d_att, o, lse)
    d_last, tok_mine, tok_rest, dvec_last = last(chunks, gq, gk, gv, d_one, wq, wk, wv)
    m = x.shape[0]
    grad_tok = scatter_line(tok_mine, tok_rest[:m], tok_rest[m : 2 * m], tok_rest[2 * m :])
    dvec = jnp.concatenate([
        dvec_last[0:2], dvec_mid[4:5], dvec_mid[2:4], dvec_mid[0:2], dvec_feed[9:10],
        dvec_feed[7:9], dvec_feed[0:3],
    ])
    dtab = jnp.concatenate([
        dvec.reshape(B_EXPAND, size, rows).transpose(1, 0, 2),
        dvec_feed[3:7].reshape(size, 4, rows),
    ], 1)
    dtab = jnp.pad(dtab, ((0, 0), (0, VEC_ROWS - N_VEC), (0, D - rows))).astype(BF)
    sum_last = reduce_all([by_owner(d_last, 3), dtab], f, size)

    vecs = sum_last[3 * rows : 3 * rows + N_VEC, :rows]
    dw_reduce = sum_feed[: 4 * rows]
    dw_expand = jnp.concatenate([sum_feed[(4 + j) * rows : (5 + j) * rows] for j in range(4)], 1)
    du_output = sum_feed[8 * rows :]
    du_query, du_key, du_value, dw_output = [sum_mid[i * rows : (i + 1) * rows] for i in range(4)]
    dw_query, dw_key, dw_value = [sum_last[i * rows : (i + 1) * rows] for i in range(3)]
    return (
        layer_out[None], grad_tok[None], grad_mem[None],
        dw_query, dw_key, dw_value, dw_output, vecs[0], vecs[1], vecs[2], vecs[3], vecs[4],
        du_query, du_key, du_value, du_output, vecs[5], vecs[6], vecs[7], vecs[8], vecs[9],
        dw_expand, vecs[B_EXPAND:].reshape(4 * rows), dw_reduce, vecs[10], vecs[11], vecs[12],
    )


def solution(mesh):
    rows = P("fsdp", "seq", None)
    mat, vec = P("fsdp", None), P("fsdp")
    weights = (mat,) * 4 + (vec,) * 5 + (mat,) * 4 + (vec,) * 5 + (mat, vec, mat, vec, vec, vec)
    return jax.shard_map(
        functools.partial(on_device, mesh.shape["fsdp"]),
        mesh=mesh,
        in_specs=(rows,) * 3 + weights,
        out_specs=(rows,) * 3 + weights,
        check_vma=False,
    )
```

```python
import functools

import jax
import jax.numpy as jnp
from jax import lax
from jax.experimental import pallas as pl
from jax.experimental.pallas import tpu as pltpu
from jax.sharding import PartitionSpec as P

HD = 64
D = 512
EPS = 1e-05
SCALE = HD ** (-0.5)
BF = jnp.bfloat16
F32 = jnp.float32

B_QUERY, B_VALUE, B_OUTPUT, GAIN_A, SHIFT_A = 0, 1, 2, 3, 4
C_QUERY, C_VALUE, C_OUTPUT, GAIN_B, SHIFT_B = 5, 6, 7, 8, 9
B_REDUCE, GAIN_C, SHIFT_C, B_EXPAND = 10, 11, 12, 13
N_VEC = 17
VEC_ROWS = 32

AT_EXPAND, AT_WO, AT_UQ, AT_UK, AT_UV, AT_UO = 4, 8, 9, 10, 11, 12


def dot(a, b, ca, cb):
    return lax.dot_general(a, b, (((ca,), (cb,)), ((), ())), preferred_element_type=F32)


def params(mib=14):
    return pltpu.CompilerParams(vmem_limit_bytes=mib << 20)


def cost(flops, nbytes, trans=0):
    return pl.CostEstimate(flops=flops // 100, bytes_accessed=nbytes // 100, transcendentals=0)


def shape(dims, dtype):
    return jax.ShapeDtypeStruct(dims, dtype)


def whole(x):
    nd = len(x.shape)
    return pl.BlockSpec(x.shape, lambda i: (0,) * nd, pipeline_mode=pl.Buffered(1))


def norm(hidden):
    centre = jnp.mean(hidden, axis=-1, keepdims=True)
    offset = hidden - centre
    spread = jnp.mean(offset * offset, axis=-1, keepdims=True)
    r = lax.rsqrt(spread + EPS)
    return offset * r, r


def norm_back(e, gain, n, r):
    t = e * gain
    return r * (t - jnp.mean(t, axis=-1, keepdims=True) - n * jnp.mean(t * n, axis=-1, keepdims=True))


def total(x):
    return jnp.sum(x, axis=0, keepdims=True)


def square(ref):
    return ref[...].reshape(-1, ref.shape[-1])


def any_space():
    return pl.BlockSpec(memory_space=pltpu.HBM)


def in_hbm(*arrays):
    return [pltpu.with_memory_space_constraint(a, pltpu.HBM) for a in arrays]


class Bulk:
    def __init__(self, array, size):
        self.array = in_hbm(array)[0]
        self.by_owner = size == 8

    def scratch(self, wanted):
        shapes = []
        for count in (c for _, c in wanted):
            shapes.append(pltpu.VMEM((8, count * D // 8, D) if self.by_owner else (count, D, D), BF))
        return shapes + [pltpu.SemaphoreType.DMA((len(wanted),))]

    def copies(self, wanted, ref, scratch):
        out = []
        for i, (at, count) in enumerate(wanted):
            if self.by_owner:
                src = ref.at[:, pl.ds(at * D // 8, count * D // 8), :]
            else:
                src = ref.at[pl.ds(at, count)]
            out.append(pltpu.make_async_copy(src, scratch[i], scratch[-1].at[i]))
        return out


def sums_out(size, rows, count, late=False):
    if size == 8 and late:
        return [shape((4, rows, D), BF)] * 2
    if size == 8:
        return [shape((8, rows, D), BF)]
    return [shape((count * D, D), BF)]


def emit(size, f_ref, outs, block, at, value):
    value = value.astype(BF)
    if size != 8:
        outs[0][block * D : (block + 1) * D, :] = value
        return
    if len(outs) == 1:
        if at is None:
            outs[0][2 * block : 2 * block + 2, 0 : D // 2, :] = value.reshape(2, D // 2, D)
        else:
            outs[0][:, at : at + D // 8, :] = value.reshape(8, D // 8, D)
        return
    even = lax.rem(f_ref[0], 2) == 0
    if at is None:
        v = value.reshape(2, D // 2, D)
        outs[0][block, 0 : D // 2, :] = jnp.where(even, v[1], v[0])
        outs[1][block, 0 : D // 2, :] = jnp.where(even, v[0], v[1])
    else:
        v = value.reshape(4, 2, D // 8, D)
        outs[0][:, at : at + D // 8, :] = jnp.where(even, v[:, 1], v[:, 0])
        outs[1][:, at : at + D // 8, :] = jnp.where(even, v[:, 0], v[:, 1])


def head_rows(g, o):
    n = g.shape[0]
    t = (g.astype(F32) * o.astype(F32)).T
    s = jnp.sum(t.reshape(D // HD, HD, n), axis=1, keepdims=True)
    return jnp.broadcast_to(s, (D // HD, 8, n))


def assemble_kernel(rows, f_ref, own, r1, r2, r3, *rest):
    outs, sems = rest[:-1], rest[-1]
    f = f_ref[0]
    c = lax.rem(f, 2)
    a = 2 + 2 * c
    b = 4 - 2 * c
    n = own.shape[0]
    pieces = (
        (own, 0, 0), (r1, 0, a), (r2, 0, b), (r2, n, 6),
        (r3, 0, 1), (r3, n, b + 1), (r3, 2 * n, a + 1), (r3, 3 * n, 7),
    )
    copies = []
    for j, (src, base, off) in enumerate(pieces):
        at = pl.multiple_of(jnp.bitwise_xor(f, off) * rows, rows)
        for k, out in enumerate(outs):
            copy = pltpu.make_async_copy(
                src.at[pl.ds(base + k * rows, rows), :], out.at[pl.ds(at, rows), :], sems.at[j, k]
            )
            copy.start()
            copies.append(copy)
    for copy in copies:
        copy.wait()


def assemble(f, rows, count, own, r1, r2, r3):
    anyspec = pl.BlockSpec(memory_space=pl.ANY)
    return pl.pallas_call(
        functools.partial(assemble_kernel, rows),
        in_specs=[pl.BlockSpec(memory_space=pltpu.SMEM)] + [anyspec] * 4,
        out_shape=[shape((8 * rows, D), BF)] * count,
        scratch_shapes=[pltpu.SemaphoreType.DMA((8, count))],
        compiler_params=params(6),
        name="assemble",
    )(f.reshape(1).astype(jnp.int32), own, r1, r2, r3)


def project_kernel(n, with_q, *refs):
    chunks = refs[:n]
    wq, wk, wv, vec = refs[n : n + 4]
    outs = refs[n + 4 :]
    k_ref, v_ref = outs[-2:]
    bv = vec[B_VALUE : B_VALUE + 1, :]
    for i, chunk in enumerate(chunks):
        x = chunk[...]
        m = x.shape[0]
        if i == 0 and with_q:
            outs[0][...] = (dot(x, wq[...], 1, 0) + vec[B_QUERY : B_QUERY + 1, :]).astype(BF)
        k_ref[pl.ds(i * m, m), :] = dot(x, wk[...], 1, 0).astype(BF)
        v_ref[pl.ds(i * m, m), :] = (dot(x, wv[...], 1, 0) + bv).astype(BF)


def project(chunks, with_q, wq, wk, wv, vec):
    m = chunks[0].shape[0]
    n = len(chunks)
    outs = [pltpu.HBM((n * m, D), BF)] * 2
    if with_q:
        outs = [pltpu.HBM((m, D), BF)] + outs
    chunks = in_hbm(*chunks)
    return pl.pallas_call(
        functools.partial(project_kernel, n, with_q),
        out_shape=outs,
        compiler_params=params(),
        cost_estimate=cost(4 * n * m * D * D, 4 * n * m * D * 2),
        name="project",
    )(*chunks, wq, wk, wv, vec)


def project_memory_kernel(bulk, own, rest, w_ref, vec, x_ref, k_ref, v_ref, uk, uv, sem):
    copies = bulk.copies(((AT_UK, 1), (AT_UV, 1)), w_ref, (uk, uv, sem))
    for copy in copies:
        copy.start()
    cv = vec[C_VALUE : C_VALUE + 1, :]
    m = own.shape[0]
    x_ref[0:m, :] = own[...]
    x_ref[m:, :] = rest[...]
    for copy in copies:
        copy.wait()
    x = x_ref[...]
    k_ref[...] = dot(x, square(uk), 1, 0).astype(BF)
    v_ref[...] = (dot(x, square(uv), 1, 0) + cv).astype(BF)


def project_memory(own, rest, bulk, vec):
    n = own.shape[0] + rest.shape[0]
    return pl.pallas_call(
        functools.partial(project_memory_kernel, bulk),
        grid=(1,),
        in_specs=[whole(own), whole(rest), any_space(), whole(vec)],
        out_specs=[pl.BlockSpec((n, D), lambda i: (0, 0))] * 3,
        out_shape=[pltpu.HBM((n, D), BF)] * 3,
        scratch_shapes=bulk.scratch(((AT_UK, 1), (AT_UV, 1))),
        compiler_params=params(),
        cost_estimate=cost(4 * n * D * D, 10 * n * D),
        name="project_memory",
    )(own, rest, bulk.array, vec)


def attend_kernel(block, parts, q_ref, *refs):
    o_ref, lse_ref = refs[-2:]
    lane = lax.broadcasted_iota(jnp.int32, (block, 128), 1) < HD
    k = jnp.concatenate([r[...] for r in refs[:parts]])
    v = jnp.concatenate([r[...] for r in refs[parts : 2 * parts]])
    for i in range(q_ref.shape[0] // block):
        rows = pl.ds(i * block, block)
        q = q_ref[rows, :] * BF(SCALE)
        outs = []
        for a in range(2):
            qm = jnp.where(lane == (a == 0), q, jnp.zeros_like(q))
            s = dot(qm, k, 1, 1)
            top = jnp.max(s, axis=1, keepdims=True)
            p = jnp.exp(s - top)
            count = jnp.sum(p, axis=1, keepdims=True)
            outs.append(dot(p.astype(BF), v, 1, 0) / count)
            lse = jnp.broadcast_to(top + jnp.log(count), (block, 128))
            lse_ref[a, :, rows] = lse.T[:8]
        o_ref[rows, :] = jnp.where(lane, outs[0], outs[1]).astype(BF)


def attend(q, ks, vs):
    n, kv = q.shape[0], sum(k.shape[0] for k in ks)
    pairs = D // 128

    def cols(m):
        return pl.BlockSpec((m, 128), lambda h: (0, h))

    q, *kv_arrays = in_hbm(q, *ks, *vs)
    return pl.pallas_call(
        functools.partial(attend_kernel, 256, len(ks)),
        grid=(pairs,),
        in_specs=[cols(n)] + [cols(a.shape[0]) for a in ks] * 2,
        out_specs=[cols(n), pl.BlockSpec((2, 8, n), lambda h: (h, 0, 0))],
        out_shape=[shape((n, D), BF), pltpu.HBM((2 * pairs, 8, n), F32)],
        compiler_params=params(),
        cost_estimate=cost(16 * n * kv * D, 4 * kv * D, 8 * n * kv),
        name="attend",
    )(q, *kv_arrays)


def attend_back_kernel(first, bulk, q_ref, g_ref, delta_ref, lse_ref, k_ref, v_ref, *refs):
    h = pl.program_id(0)
    *refs, dk_all, dv_all, wk_ref, wv_ref, sem = refs
    if bulk is None:
        *weights, = refs[:2]
        refs = refs[2:]
        copies = [pltpu.make_async_copy(weights[i], (wk_ref, wv_ref)[i], sem.at[i]) for i in range(2)]
    else:
        copies = bulk.copies(((AT_UK, 1), (AT_UV, 1)), refs[0], (wk_ref, wv_ref, sem))
        refs = refs[1:]

    @pl.when(h == 0)
    def _():
        for copy in copies:
            copy.start()

    if not first:
        acc_ref, *refs = refs
    p_ref, dqt_ref, dk_ref, dv_ref = refs
    n = q_ref.shape[0]
    g = g_ref[...]
    q = q_ref[...] * BF(SCALE)
    k = k_ref[...]
    v = v_ref[...]
    lane = lax.broadcasted_iota(jnp.int32, (n, 128), 1) < HD
    zero = jnp.zeros_like(q)
    dk = jnp.zeros(k.shape, F32)
    dv = jnp.zeros(k.shape, F32)
    dqs = []
    for a in range(2):
        qm = jnp.where(lane == (a == 0), q, zero)
        gm = jnp.where(lane == (a == 0), g, zero)
        p = jnp.exp(dot(k, qm, 1, 1) - lse_ref[a, 0:1, :])
        dp = dot(v, gm, 1, 1)
        ds = (p * (dp - delta_ref[a, 0:1, :])).astype(BF)
        dv = dv + dot(p.astype(BF), gm, 1, 0)
        dk = dk + dot(ds, qm, 1, 0)
        dqs.append(dot(k, ds, 0, 0))
    top_half = lax.broadcasted_iota(jnp.int32, (128, n), 0) < HD
    dqt = jnp.where(top_half, dqs[0], dqs[1])
    if not first:
        dqt = dqt + acc_ref[...]
    dqt_ref[...] = dqt
    dk = dk.astype(BF)
    dv = dv.astype(BF)
    dk_ref[...] = dk
    dv_ref[...] = dv
    for i in range(D // 128):

        @pl.when(h == i)
        def _(i=i):
            dk_all[:, i * 128 : (i + 1) * 128] = dk
            dv_all[:, i * 128 : (i + 1) * 128] = dv

    @pl.when(h == pl.num_programs(0) - 1)
    def _():
        for copy in copies:
            copy.wait()
        p_ref[...] = (dot(dk_all[...], square(wk_ref), 1, 1) + dot(dv_all[...], square(wv_ref), 1, 1)).astype(
            p_ref.dtype
        )


def attend_back(q, g, delta, lse, k, v, at, m, weights, acc, dtype):
    n = q.shape[0]
    pairs = D // 128
    bulk = weights if isinstance(weights, Bulk) else None
    weights = weights if bulk is None else (bulk.array,)

    def cols(rows, i=0):
        return pl.BlockSpec((rows, 128), lambda h: (i, h))

    by_head = pl.BlockSpec((2, 8, n), lambda h: (h, 0, 0))
    acc_spec = pl.BlockSpec((128, n), lambda h: (h, 0))
    first = acc is None
    arrays = in_hbm(q, g, delta, lse, k, v, *weights, *([] if first else [acc]))
    shapes = [pltpu.VMEM((m, D), BF)] * 2
    shapes += bulk.scratch(((AT_UK, 1), (AT_UV, 1))) if bulk else (
        [pltpu.VMEM((D, D), BF)] * 2 + [pltpu.SemaphoreType.DMA((2,))]
    )
    return pl.pallas_call(
        functools.partial(attend_back_kernel, first, bulk),
        grid=(pairs,),
        in_specs=[cols(n), cols(n), by_head, by_head, cols(m, at), cols(m, at)]
        + [any_space()] * len(weights)
        + ([] if first else [acc_spec]),
        out_specs=[pl.BlockSpec((m, D), lambda h: (0, 0)), acc_spec, cols(m), cols(m)],
        out_shape=[shape((m, D), dtype), pltpu.HBM((D, n), F32), pltpu.HBM((m, D), BF), pltpu.HBM((m, D), BF)],
        scratch_shapes=shapes,
        compiler_params=params(),
        cost_estimate=cost(44 * n * m * D, 12 * m * D, 8 * n * m),
        name="attend_back",
    )(*arrays)


def after_self_kernel(bulk, o, x, w_ref, vec, n_ref, r_ref, low_ref, cq_ref, wo, uq, sem):
    copies = bulk.copies(((AT_WO, 1), (AT_UQ, 1)), w_ref, (wo, uq, sem))
    for copy in copies:
        copy.start()

    def v(i):
        return vec[i : i + 1, :]

    copies[0].wait()
    sum_one = x[...].astype(F32) + dot(o[...], square(wo), 1, 0) + v(B_OUTPUT)
    n, r = norm(sum_one)
    low = (n * v(GAIN_A) + v(SHIFT_A)).astype(BF)
    n_ref[...] = n
    r_ref[...] = jnp.broadcast_to(r, r_ref.shape)
    low_ref[...] = low
    copies[1].wait()
    cq_ref[...] = (dot(low, square(uq), 1, 0) + v(C_QUERY)).astype(BF)


def after_self(o, x, bulk, vec):
    m = x.shape[0]
    outs = [shape((m, D), F32), shape((m, 128), F32), shape((m, D), BF), pltpu.HBM((m, D), BF)]
    return pl.pallas_call(
        functools.partial(after_self_kernel, bulk),
        grid=(1,),
        in_specs=[whole(o), whole(x), any_space(), whole(vec)],
        out_specs=[whole(s) for s in outs],
        out_shape=outs,
        scratch_shapes=bulk.scratch(((AT_WO, 1), (AT_UQ, 1))),
        compiler_params=params(),
        cost_estimate=cost(4 * m * D * D, 12 * m * D),
        name="after_self",
    )(o, x, bulk.array, vec)


GELU_C = 0.7978845608028654
GELU_A = 0.044715


FEED_WEIGHTS = ((AT_UO, 1),) + tuple((AT_EXPAND + j, 1) for j in range(4)) + ((0, 4),)


def feed_kernel(size, bulk, f_ref, ca, n1, cot, w_ref, vec,
                out_ref, two_ref, catt_ref, delta_ref, dvec_ref, *refs):
    sums, (uo, *expand, wred_ref, sem) = refs[:-7], refs[-7:]
    copies = bulk.copies(FEED_WEIGHTS, w_ref, (uo, *expand, wred_ref, sem))
    for copy in copies:
        copy.start()

    def v(i):
        return vec[i : i + 1, :]

    copies[0].wait()
    first = n1[...] * v(GAIN_A) + v(SHIFT_A)
    sum_two = first + dot(ca[...], square(uo), 1, 0) + v(C_OUTPUT)
    n2, r2 = norm(sum_two)
    second = n2 * v(GAIN_B) + v(SHIFT_B)
    low = second.astype(BF)
    sum_three = second + v(B_REDUCE)
    acts, slopes = [], []
    for copy in copies[1:]:
        copy.wait()
    wred = square(wred_ref)
    for j in range(4):
        pre = dot(low, square(expand[j]), 1, 0) + v(B_EXPAND + j)
        sq = pre * pre
        t = jnp.tanh(GELU_C * (pre + GELU_A * (sq * pre)))
        half = 0.5 * (1.0 + t)
        act = (pre * half).astype(BF)
        slope = half + 0.5 * pre * (1.0 - t * t) * (GELU_C * (1.0 + 3.0 * GELU_A * sq))
        acts.append(act)
        slopes.append(slope)
        sum_three = sum_three + dot(act, wred[j * D : (j + 1) * D], 1, 0)
    n3, r3 = norm(sum_three)
    out_ref[...] = (n3 * v(GAIN_C) + v(SHIFT_C)).astype(BF)
    e = cot[...].astype(F32)
    d_three = norm_back(e, v(GAIN_C), n3, r3)
    branch = d_three.astype(BF)
    dvec_ref[0:1, :] = total(branch.astype(F32))
    dvec_ref[1:2, :] = total(e * n3)
    dvec_ref[2:3, :] = total(e)
    second_grad = d_three
    for j in range(4):
        d_act = dot(branch, wred[j * D : (j + 1) * D], 1, 1)
        d_pre = (d_act * slopes[j]).astype(BF)
        dvec_ref[3 + j : 4 + j, :] = total(d_pre.astype(F32))
        emit(size, f_ref, sums, j, None, dot(acts[j], branch, 0, 0))
        emit(size, f_ref, sums, 4 + j, (4 + j) * D // 8, dot(low, d_pre, 0, 0))
        second_grad = second_grad + dot(d_pre, square(expand[j]), 1, 1)
    d_two = norm_back(second_grad, v(GAIN_B), n2, r2)
    two_ref[...] = d_two
    cross = d_two.astype(BF)
    dvec_ref[7:8, :] = total(second_grad * n2)
    dvec_ref[8:9, :] = total(second_grad)
    dvec_ref[9:10, :] = total(cross.astype(F32))
    emit(size, f_ref, sums, 8, D, dot(ca[...], cross, 0, 0))
    att = dot(cross, square(uo), 1, 1).astype(BF)
    catt_ref[...] = att
    delta_ref[...] = head_rows(att, ca[...])


def smem():
    return pl.BlockSpec(memory_space=pltpu.SMEM)


def feed(size, f, ca, n1, cot, bulk, vec):
    m = ca.shape[0]
    outs = [
        shape((m, D), BF), shape((m, D), F32), pltpu.HBM((m, D), BF), pltpu.HBM((D // HD, 8, m), F32),
        shape((16, D), F32),
    ] + sums_out(size, 9 * D // 8, 9)
    return pl.pallas_call(
        functools.partial(feed_kernel, size, bulk),
        grid=(1,),
        in_specs=[smem(), whole(ca), whole(n1), whole(cot), any_space(), whole(vec)],
        out_specs=[whole(s) for s in outs],
        out_shape=outs,
        scratch_shapes=bulk.scratch(FEED_WEIGHTS),
        compiler_params=params(34),
        cost_estimate=cost(2 * 27 * m * D * D, 24 * m * D * 4, 4 * m * D),
        name="feed",
    )(f, ca, n1, cot, bulk.array, vec)


def after_cross_back_kernel(size, bulk, f_ref, dqt, k0, k1, v0, v1, mem, low, o, two, n1, r1, w_ref, vec,
                            one_ref, att_ref, delta_ref, dvec_ref, *refs):
    sums, (uq, wo, sem) = refs[:-3], refs[-3:]
    copies = bulk.copies(((AT_UQ, 1), (AT_WO, 1)), w_ref, (uq, wo, sem))
    for copy in copies:
        copy.start()
    gain = vec[GAIN_A : GAIN_A + 1, :]
    gq = (dqt[...].T * SCALE).astype(BF)
    for copy in copies:
        copy.wait()
    first_grad = two[...] + dot(gq, square(uq), 1, 1)
    n = n1[...]
    d_one = norm_back(first_grad, gain, n, r1[:, 0:1])
    one_ref[...] = d_one
    low_one = d_one.astype(BF)
    att = dot(low_one, square(wo), 1, 1).astype(BF)
    att_ref[...] = att
    delta_ref[...] = head_rows(att, o[...])
    m = k0.shape[0]
    dvec_ref[0:1, :] = total(gq.astype(F32))
    dvec_ref[1:2, :] = total(first_grad * n)
    dvec_ref[2:3, :] = total(first_grad)
    dvec_ref[3:4, :] = total(low_one.astype(F32))
    dvec_ref[4:5, :] = total(v0[...].astype(F32)) + total(v1[...].astype(F32))
    r = D // 8
    emit(size, f_ref, sums, 0, 0, dot(low[...], gq, 0, 0))
    emit(size, f_ref, sums, 1, r, dot(mem[0:m, :], k0[...], 0, 0) + dot(mem[m:, :], k1[...], 0, 0))
    emit(size, f_ref, sums, 2, 2 * r, dot(mem[0:m, :], v0[...], 0, 0) + dot(mem[m:, :], v1[...], 0, 0))
    emit(size, f_ref, sums, 3, 3 * r, dot(o[...], low_one, 0, 0))


def after_cross_back(size, f, dqt, ks, vs, mem, low, o, two, n1, r1, bulk, vec):
    m = low.shape[0]
    arrays = in_hbm(dqt, *ks, *vs, mem) + [low, o, two, n1, r1]
    outs = [shape((m, D), F32), pltpu.HBM((m, D), BF), pltpu.HBM((D // HD, 8, m), F32), shape((8, D), F32)]
    outs += sums_out(size, 4 * D // 8, 4, True)
    return pl.pallas_call(
        functools.partial(after_cross_back_kernel, size, bulk),
        grid=(1,),
        in_specs=[smem()] + [whole(a) for a in arrays] + [any_space(), whole(vec)],
        out_specs=[whole(s) for s in outs],
        out_shape=outs,
        scratch_shapes=bulk.scratch(((AT_UQ, 1), (AT_WO, 1))),
        compiler_params=params(24),
        cost_estimate=cost(2 * 8 * m * D * D, 14 * m * D * 4),
        name="after_cross_back",
    )(f, *arrays, bulk.array, vec)


def last_kernel(size, count, f_ref, dqt, *refs):
    ks, vs, xs = refs[:count], refs[count : 2 * count], refs[2 * count : 3 * count]
    feed, mid, gq_ref = refs[3 * count : 3 * count + 3]
    *sums, table = refs[3 * count + 3 :]
    gq = (dqt[...].T * SCALE).astype(BF)
    gq_ref[...] = gq
    r = D // 8
    emit(size, f_ref, sums, 0, 0, dot(xs[0][...], gq, 0, 0))
    for i, parts in ((1, ks), (2, vs)):
        acc = dot(xs[0][...], parts[0][...], 0, 0)
        for x, p in zip(xs[1:], parts[1:]):
            acc = acc + dot(x[...], p[...], 0, 0)
        emit(size, f_ref, sums, i, i * r, acc)
    table[...] = jnp.zeros_like(table)
    table[B_QUERY : B_QUERY + 1, :] = total(gq.astype(F32))
    dbv = total(vs[0][...].astype(F32))
    for v in vs[1:]:
        dbv = dbv + total(v[...].astype(F32))
    table[B_VALUE : B_VALUE + 1, :] = dbv
    for at, src, i in (
        (B_OUTPUT, mid, 3), (GAIN_A, mid, 1), (SHIFT_A, mid, 2), (C_QUERY, mid, 0), (C_VALUE, mid, 4),
        (C_OUTPUT, feed, 9), (GAIN_B, feed, 7), (SHIFT_B, feed, 8),
        (B_REDUCE, feed, 0), (GAIN_C, feed, 1), (SHIFT_C, feed, 2),
    ):
        table[at : at + 1, :] = src[i : i + 1, :]
    if size != 8:
        table[B_EXPAND : B_EXPAND + 4, :] = feed[3:7, :]
        return
    rows = table[0:16, :].astype(BF)
    for chip in range(4):
        wide = jnp.broadcast_to(feed[3 + chip : 4 + chip, :], (16, D)).astype(BF)
        for s in sums:
            s[chip, 3 * r : 3 * r + 16, :] = jnp.zeros((16, D), BF)
            s[chip, 3 * r : 3 * r + 16, 0:128] = rows[:, chip * 128 : (chip + 1) * 128]
            s[chip, 3 * r + 16 : 3 * r + 32, :] = wide


def last(size, f, dqt, ks, vs, xs, feed, mid):
    m = xs[0].shape[0]
    count = len(xs)
    arrays = [f, *in_hbm(dqt, *ks, *vs, *xs), feed, mid]
    outs = [shape((m, D), BF)] + sums_out(size, 3 * D // 8 + 32, 3, True) + [shape((VEC_ROWS, D), F32)]
    return pl.pallas_call(
        functools.partial(last_kernel, size, count),
        grid=(1,),
        in_specs=[smem()] + [whole(a) for a in arrays[1:]],
        out_specs=[whole(s) for s in outs],
        out_shape=outs,
        compiler_params=params(),
        cost_estimate=cost(2 * 9 * m * D * D, 14 * m * D * 2),
        name="last",
    )(*arrays)


def own_rows_kernel(gq, part, one, wq, out):
    out[...] = part[...] + one[...] + dot(gq[...], wq[...], 1, 1)


def own_rows(gq, part, one, wq):
    return pl.pallas_call(
        own_rows_kernel,
        out_shape=shape(part.shape, F32),
        compiler_params=params(),
        cost_estimate=cost(2 * part.shape[0] * D * D, 4 * part.shape[0] * D * 4),
        name="own_rows",
    )(gq, part, one, wq)


def fold_kernel(t_ref, *refs):
    acc = refs[0][...].astype(F32)
    for r in refs[1:-1]:
        acc = acc + r[...].astype(F32)
    refs[-1][...] = acc.astype(BF)


def fold(table, base, count, arrays):
    n = arrays[0].shape[1]
    width = len(arrays)

    def spec(k):
        return pl.BlockSpec((1, n, D), lambda j, t: (t[base + j * width + k], 0, 0))

    return pl.pallas_call(
        fold_kernel,
        grid_spec=pltpu.PrefetchScalarGridSpec(
            num_scalar_prefetch=1,
            grid=(count,),
            in_specs=[spec(k) for k in range(width)],
            out_specs=pl.BlockSpec((1, n, D), lambda j, t: (j, 0, 0)),
        ),
        out_shape=shape((count, n, D), BF),
        compiler_params=params(6),
        name="fold",
    )(table, *arrays)


def start_rows(arrays, out, sems):
    copies = []
    at = 0
    for ref in arrays:
        rows = ref.shape[0]
        for j in range(ref.shape[1] // D):
            copies.append(pltpu.make_async_copy(
                ref.at[:, pl.ds(j * D, D)], out.at[pl.ds(at, rows), :], sems.at[len(copies)]
            ))
            copies[-1].start()
            at += rows
    return copies


def pack_kernel(*refs):
    *arrays, out, sems = refs
    for copy in start_rows(arrays, out, sems):
        copy.wait()


def pack_plain(arrays):
    return jnp.concatenate([a[:, i : i + D] for a in arrays for i in range(0, a.shape[1], D)])


def pack_rows(arrays):
    if arrays[0].shape[0] % 16:
        return pack_plain(arrays)
    pieces = sum(a.shape[1] // D for a in arrays)
    rows = sum(a.shape[0] * a.shape[1] // D for a in arrays)
    return pl.pallas_call(
        pack_kernel,
        in_specs=[any_space()] * len(arrays),
        out_shape=shape((rows, D), BF),
        scratch_shapes=[pltpu.SemaphoreType.DMA((pieces,))],
        compiler_params=params(4),
        name="pack_rows",
    )(*in_hbm(*arrays))


def table_kernel(rows, count, *refs):
    arrays, refs = refs[:count], refs[count:]
    *vectors, expand, out, scratch, sems = refs
    copies = start_rows(arrays, out, sems)
    scratch[...] = jnp.zeros_like(scratch)
    for i, ref in enumerate(vectors):
        scratch[i : i + 1, 0:rows] = ref[...].astype(F32)
    for j in range(4):
        scratch[B_EXPAND + j : B_EXPAND + j + 1, 0:rows] = expand[:, j * rows : (j + 1) * rows].astype(F32)
    out[len(copies) * rows :, :] = scratch[...].astype(BF)
    for copy in copies:
        copy.wait()


def pack_first(arrays, vectors, expand):
    rows = vectors[0].shape[0]
    plain = rows % 16 != 0
    used = [] if plain else arrays
    out = pl.pallas_call(
        functools.partial(table_kernel, rows, len(used)),
        in_specs=[any_space()] * len(used) + [pl.BlockSpec(memory_space=pltpu.VMEM)] * (len(vectors) + 1),
        out_shape=shape((len(used) * rows + VEC_ROWS, D), BF),
        scratch_shapes=[pltpu.VMEM((VEC_ROWS, D), F32), pltpu.SemaphoreType.DMA((len(arrays),))],
        compiler_params=params(4),
        name="pack_first",
    )(*in_hbm(*used), *[v.reshape(1, -1) for v in vectors], expand.reshape(1, -1))
    return pack_plain([*arrays, out]) if plain else out


ENDS_IN = ((1, 0), (2, 3))
ENDS_OUT = ((0, 1), (3, 2))
MIDDLE = ((1, 2), (2, 1))
PAIRS = ((0, 1), (1, 0), (2, 3), (3, 2))
ACROSS = ((0, 2), (2, 0), (1, 3), (3, 1))


def over_seq(x, pairs):
    return lax.ppermute(x, "seq", pairs)


def after(x, *deps):
    return lax.optimization_barrier((x,) + deps)[0]


def gather_line(own):
    z = lax.axis_index("seq")
    middle = (z == 1) | (z == 2)
    a = over_seq(own, PAIRS)
    b = over_seq(own, MIDDLE)
    d = over_seq(a, MIDDLE)
    c = over_seq(b, ENDS_IN)
    e = over_seq(d, ENDS_IN)
    return a, jnp.where(middle, b, c), jnp.where(middle, d, e), (a, d, e)


def gather_line_after(own, steps, last_dep):
    z = lax.axis_index("seq")
    middle = (z == 1) | (z == 2)
    out = over_seq(after(own, steps[1]), ENDS_OUT)
    mid = over_seq(after(jnp.concatenate([own, out]), steps[2]), MIDDLE)
    inward = over_seq(after(jnp.concatenate([own, mid]), last_dep), ENDS_IN)
    return jnp.where(middle, jnp.concatenate([out, mid]), inward)


def add(p, r):
    return (p.astype(F32) + r.astype(F32)).astype(BF)


def swap_core():
    return [(i, i ^ 1) for i in range(8)]


def swap_first():
    return [(i, i ^ (4 if i & 1 else 2)) for i in range(8)]


def swap_second():
    return [(i, i ^ (2 if i & 1 else 4)) for i in range(8)]


def gather_plane(own):
    r1 = lax.ppermute(own, "fsdp", swap_first())
    both = jnp.concatenate([own, r1])
    r2 = lax.ppermute(both, "fsdp", swap_second())
    r3 = lax.ppermute(jnp.concatenate([both, r2]), "fsdp", swap_core())
    return r1, r2, r3


def fold_table(f):
    c = lax.rem(f, 2)
    x = lax.rem(f // 2, 2)
    y = f // 4
    even = c == 0
    send0 = jnp.where(even, 1 - x, 2 * (1 - y))
    send1 = jnp.where(even, 3 - x, 3 - 2 * y)
    keep0 = jnp.where(even, x, 2 * y)
    keep1 = jnp.where(even, 2 + x, 2 * y + 1)
    own = jnp.where(even, y, x)
    mine = jnp.where(own == 0, keep0, keep1)
    other = jnp.where(own == 0, keep1, keep0)
    zero = 0 * own
    return jnp.stack([send0, send0, send1, send1, other, other, 1 - own, mine, mine, own, zero]).astype(jnp.int32)


class PlaneReduce:
    def __init__(self, table, sums):
        self.table = table
        self.keep = sums[1]
        self.got = [lax.ppermute(sums[0], "fsdp", swap_core())]

    def second(self, *deps):
        out = fold(self.table, 0, 2, [after(self.keep, *deps), self.got[0]])
        self.got.append(lax.ppermute(out, "fsdp", swap_first()))

    def third(self, *deps):
        out = fold(self.table, 4, 1, [after(self.keep, *deps)] + self.got)
        self.got.append(lax.ppermute(out, "fsdp", swap_second()))

    def end(self, *deps):
        return fold(self.table, 7, 1, [after(self.keep, *deps)] + self.got)[0]


class PlainReduce:
    def __init__(self, table, sums):
        self.got = [lax.psum_scatter(sums, "fsdp", scatter_dimension=0, tiled=False)]

    def second(self, *deps):
        pass

    third = second

    def end(self, *deps):
        return self.got[0]


def on_device(size, tokens, memory, cotangent,
              w_query, w_key, w_value, w_output, b_query, b_value, b_output, gain_attend, shift_attend,
              u_query, u_key, u_value, u_output, c_query, c_value, c_output, gain_cross, shift_cross,
              w_expand, b_expand, w_reduce, b_reduce, gain_feed, shift_feed):
    rows = w_query.shape[0]
    f = lax.axis_index("fsdp")
    x = tokens[0]
    mem = memory[0]

    vectors = (b_query, b_value, b_output, gain_attend, shift_attend, c_query, c_value, c_output,
               gain_cross, shift_cross, b_reduce, gain_feed, shift_feed)
    first = pack_first([w_query, w_key, w_value], vectors, b_expand)
    pack = pack_rows([w_reduce, w_expand, w_output, u_query, u_key, u_value, u_output])
    c1, c2, c3, steps = gather_line(x)
    if size == 8:
        r1, r2, r3 = gather_plane(first)
        wq, wk, wv = assemble(f, rows, 3, first, r1, r2, r3)
        n = first.shape[0]
        tables = [first, r1, r2[:n], r2[n:]] + [r3[i * n : (i + 1) * n] for i in range(4)]
        tables = jnp.stack([t[3 * rows : 3 * rows + N_VEC, :rows] for t in tables])
        c = lax.rem(f, 2)
        a, b = 2 + 2 * c, 4 - 2 * c
        offsets = jnp.stack([0 * c, a, b, 6 + 0 * c, 1 + 0 * c, b + 1, a + 1, 7 + 0 * c])
        pick = (jnp.arange(8)[:, None] == (offsets ^ f)[None, :]).astype(BF)
        tables = jnp.einsum("gd,dkl->gkl", pick, tables, preferred_element_type=F32)
    else:
        g = lax.all_gather(first, "fsdp", axis=0, tiled=False)
        wq, wk, wv = [g[:, i * rows : (i + 1) * rows].reshape(D, D) for i in range(3)]
        tables = g[:, 3 * rows : 3 * rows + N_VEC, :rows].astype(F32)
    vec = jnp.concatenate(
        [tables[:, :B_EXPAND].transpose(1, 0, 2).reshape(B_EXPAND, D), tables[:, B_EXPAND:].reshape(4, D)]
    )
    vec = jnp.pad(vec, ((0, VEC_ROWS - N_VEC), (0, 0)))

    everything = lax.all_gather(pack, "fsdp", axis=0, tiled=False)

    if size != 8:
        blocks = [everything[:, : 4 * rows].reshape(4, D, D)]
        for i in range(4, 13):
            blocks.append(everything[:, i * rows : (i + 1) * rows].reshape(1, D, D))
        everything = jnp.concatenate(blocks)
    bulk = Bulk(everything, size)

    def by_owner(stack, count):
        s = stack.reshape(count, size, rows, D)
        return s.transpose(1, 0, 2, 3).reshape(size, count * rows, D)

    def reduce(sums, tall, count, extra=None):
        if size == 8 and len(sums) == 2:
            return PlaneReduce(table, sums)
        if size == 8:
            return PlainReduce(table, sums[0])
        s = sums[0]
        blocks = [s[: 4 * D].reshape(size, 4 * rows, D), s[4 * D :]] if tall else [s]
        blocks[-1] = by_owner(blocks[-1], count)
        return PlainReduce(table, jnp.concatenate(blocks + ([] if extra is None else [extra]), 1))

    table = fold_table(f)
    f1 = f.reshape(1).astype(jnp.int32)
    q, k0, v0 = project([x, c1], True, wq, wk, wv, vec)
    k1, v1 = project([c2, c3], False, wq, wk, wv, vec)
    o, lse = attend(q, [k0, k1], [v0, v1])
    mem_x, mk, mv = project_memory(mem, gather_line_after(mem, steps, k1), bulk, vec)
    n1, r_one, low, cq = after_self(o, x, bulk, vec)
    ca, cross_lse = attend(cq, [mk], [mv])
    layer_out, d_two, d_catt, cross_delta, dvec_feed, *sums = feed(
        size, f1, ca, n1, cotangent[0], bulk, vec
    )
    feed_sum = reduce(sums, True, 5)

    m = 2 * mem.shape[0]
    def cross_back(g, i, acc, dtype):
        return attend_back(cq, g, cross_delta, cross_lse, mk, mv, i, m, bulk, acc, dtype)

    far, dqt, dk1, dv1 = cross_back(d_catt, 1, None, BF)
    far_in = over_seq(far, ENDS_OUT)
    near, dqt, dk0, dv0 = cross_back(after(d_catt, far), 0, dqt, F32)
    d_one, d_att, self_delta, dvec_mid, *sums = after_cross_back(
        size, f1, after(dqt, far_in), (dk0, dk1), (dv0, dv1), mem_x, low, o, d_two, n1, r_one, bulk, vec
    )
    mid_sum = reduce(sums, False, 4)
    far_mid = over_seq(after(add(far, far_in), d_att), MIDDLE)
    m = x.shape[0]

    def self_back(g, i, acc, dtype):
        k, v = ((k0, v0), (k1, v1))[i // 2]
        return attend_back(q, g, self_delta, lse, k, v, i % 2, m, (wk, wv), acc, dtype)

    p3, dqt, dk3, dv3 = self_back(d_att, 3, None, BF)
    e = over_seq(p3, ENDS_OUT)
    mid_sum.second(p3)
    half = m // 2
    p2, dqt, dk2, dv2 = self_back(after(d_att, p3, feed_sum.got[0], mid_sum.got[0]), 2, dqt, BF)
    feed_part = feed_sum.end()
    sum_feed = lax.psum(feed_part, "seq")
    cc = over_seq(p2, ENDS_OUT)
    mid_sum.third(p2)
    p1, dqt, dk1, dv1 = self_back(after(d_att, e, far_mid, p2, mid_sum.got[-2 if size == 8 else 0]), 1, dqt, BF)
    near_in = over_seq(after(add(near[half:], far_mid[half:]), p1), PAIRS)
    d = over_seq(after(add(p3, e), p1), MIDDLE)
    mid_part = mid_sum.end(p1)
    mid_in = over_seq(mid_part, PAIRS)
    p0, dqt, dk0, dv0 = self_back(after(d_att, cc, p1, mid_part), 0, dqt, F32)
    b = over_seq(after(add(p2, cc), p0), MIDDLE)
    mid_part = add(mid_part, after(mid_in, p0))
    dqt = after(dqt, d, near_in, mid_part, sum_feed)
    mid_in = over_seq(mid_part, ACROSS)
    grad_mem = near[:half] + near_in.astype(F32) + far_mid[:half].astype(F32)
    gq, *sums, vec_table = last(
        size, f1, dqt, (dk0, dk1, dk2, dk3), (dv0, dv1, dv2, dv3), (x, c1, c2, c3), dvec_feed, dvec_mid
    )
    extra = None
    if size != 8:
        extra = jnp.concatenate([
            vec_table[:B_EXPAND].reshape(B_EXPAND, size, rows).transpose(1, 0, 2),
            vec_table[B_EXPAND:N_VEC].reshape(size, 4, rows),
        ], 1)
        extra = jnp.pad(extra, ((0, 0), (0, VEC_ROWS - N_VEC), (0, D - rows))).astype(BF)
    late_sum = reduce(sums, False, 3, extra)
    tok_mine = own_rows(gq, p0, d_one, wq)
    a = over_seq(after(add(p1, d), gq), PAIRS)
    late_sum.second()
    late_sum.third()
    late = late_sum.end()
    got = over_seq(late, PAIRS)
    late = add(late, got)
    got = over_seq(late, ACROSS)
    sum_last = late.astype(F32) + got.astype(F32)
    sum_feed = sum_feed.astype(F32)
    sum_mid = mid_part.astype(F32) + mid_in.astype(F32)
    grad_tok = tok_mine + a.astype(F32) + b.astype(F32)

    if size == 8:
        c = lax.rem(f, 2)
        vecs = lax.dynamic_slice(sum_last, (3 * rows, c * rows), (B_EXPAND, rows))
        db_expand = lax.dynamic_slice(sum_last, (3 * rows + 16, c * 4 * rows), (1, 4 * rows)).reshape(4 * rows)
    else:
        vecs = sum_last[3 * rows : 3 * rows + N_VEC, :rows]
        db_expand = vecs[B_EXPAND:].reshape(4 * rows)
    dw_reduce = sum_feed[: 4 * rows]
    dw_expand = jnp.concatenate([sum_feed[(4 + j) * rows : (5 + j) * rows] for j in range(4)], 1)
    du_output = sum_feed[8 * rows :]
    du_query, du_key, du_value, dw_output = [sum_mid[i * rows : (i + 1) * rows] for i in range(4)]
    dw_query, dw_key, dw_value = [sum_last[i * rows : (i + 1) * rows] for i in range(3)]
    return (
        layer_out[None], grad_tok[None], grad_mem[None],
        dw_query, dw_key, dw_value, dw_output, vecs[0], vecs[1], vecs[2], vecs[3], vecs[4],
        du_query, du_key, du_value, du_output, vecs[5], vecs[6], vecs[7], vecs[8], vecs[9],
        dw_expand, db_expand, dw_reduce, vecs[10], vecs[11], vecs[12],
    )


def solution(mesh):
    rows = P("fsdp", "seq", None)
    mat, vec = P("fsdp", None), P("fsdp")
    weights = (mat,) * 4 + (vec,) * 5 + (mat,) * 4 + (vec,) * 5 + (mat, vec, mat, vec, vec, vec)
    return jax.shard_map(
        functools.partial(on_device, mesh.shape["fsdp"]),
        mesh=mesh,
        in_specs=(rows,) * 3 + weights,
        out_specs=(rows,) * 3 + weights,
        check_vma=False,
    )
```

```python
import functools

import jax
import jax.numpy as jnp
from jax import lax
from jax.experimental import pallas as pl
from jax.experimental.pallas import tpu as pltpu
from jax.sharding import PartitionSpec as P

HD = 64
D = 512
EPS = 1e-05
SCALE = HD ** (-0.5)
BF = jnp.bfloat16
F32 = jnp.float32

B_QUERY, B_VALUE, B_OUTPUT, GAIN_A, SHIFT_A = 0, 1, 2, 3, 4
C_QUERY, C_VALUE, C_OUTPUT, GAIN_B, SHIFT_B = 5, 6, 7, 8, 9
B_REDUCE, GAIN_C, SHIFT_C, B_EXPAND = 10, 11, 12, 13
N_VEC = 17
VEC_ROWS = 32

AT_EXPAND, AT_WO, AT_UQ, AT_UK, AT_UV, AT_UO = 4, 8, 9, 10, 11, 12


def dot(a, b, ca, cb):
    return lax.dot_general(a, b, (((ca,), (cb,)), ((), ())), preferred_element_type=F32)


def params(mib=14):
    return pltpu.CompilerParams(vmem_limit_bytes=mib << 20)


def cost(flops, nbytes, trans=0):
    return pl.CostEstimate(flops=flops // 100, bytes_accessed=nbytes // 100, transcendentals=0)


def shape(dims, dtype):
    return jax.ShapeDtypeStruct(dims, dtype)


def whole(x):
    nd = len(x.shape)
    return pl.BlockSpec(x.shape, lambda i: (0,) * nd, pipeline_mode=pl.Buffered(1))


def norm(hidden):
    centre = jnp.mean(hidden, axis=-1, keepdims=True)
    offset = hidden - centre
    spread = jnp.mean(offset * offset, axis=-1, keepdims=True)
    r = lax.rsqrt(spread + EPS)
    return offset * r, r


def norm_back(e, gain, n, r):
    t = e * gain
    return r * (t - jnp.mean(t, axis=-1, keepdims=True) - n * jnp.mean(t * n, axis=-1, keepdims=True))


def total(x):
    return jnp.sum(x, axis=0, keepdims=True)


def square(ref):
    return ref[...].reshape(-1, ref.shape[-1])


def smem():
    return pl.BlockSpec(memory_space=pltpu.SMEM)


def any_space():
    return pl.BlockSpec(memory_space=pltpu.HBM)


def in_hbm(*arrays):
    return [pltpu.with_memory_space_constraint(a, pltpu.HBM) for a in arrays]


class Bulk:
    def __init__(self, array, size):
        self.array = in_hbm(array)[0]
        self.by_owner = size == 8

    def scratch(self, wanted):
        shapes = []
        for count in (c for _, c in wanted):
            shapes.append(pltpu.VMEM((8, count * D // 8, D) if self.by_owner else (count, D, D), BF))
        return shapes + [pltpu.SemaphoreType.DMA((len(wanted),))]

    def copies(self, wanted, ref, scratch):
        out = []
        for i, (at, count) in enumerate(wanted):
            if self.by_owner:
                src = ref.at[:, pl.ds(at * D // 8, count * D // 8), :]
            else:
                src = ref.at[pl.ds(at, count)]
            out.append(pltpu.make_async_copy(src, scratch[i], scratch[-1].at[i]))
        return out


def sums_out(size, rows, count, late=False):
    if size == 8 and late:
        return [shape((4, rows, D), BF)] * 2
    if size == 8:
        return [shape((8, rows, D), BF)]
    return [shape((count * D, D), BF)]


class Outbox:
    def __init__(self, out, held, sems):
        self.out, self.held, self.sems = out, held, sems
        self.copies = []

    def send(self, block, at, value):
        v = value.astype(BF)
        if at is None:
            part = (pl.ds(2 * block, 2), pl.ds(0, D // 2))
            v = v.reshape(2, D // 2, D)
        else:
            part = (pl.ds(0, 8), pl.ds(at, D // 8))
            v = v.reshape(8, D // 8, D)
        self.held[part[0], part[1], :] = v
        copy = pltpu.make_async_copy(
            self.held.at[part[0], part[1]], self.out.at[part[0], part[1]], self.sems.at[len(self.copies)]
        )
        copy.start()
        self.copies.append(copy)

    def wait(self):
        for copy in self.copies:
            copy.wait()


def emit(size, f_ref, outs, block, at, value):
    if isinstance(outs, Outbox):
        outs.send(block, at, value)
        return
    value = value.astype(BF)
    if size != 8:
        outs[0][block * D : (block + 1) * D, :] = value
        return
    if len(outs) == 1:
        if at is None:
            outs[0][2 * block : 2 * block + 2, 0 : D // 2, :] = value.reshape(2, D // 2, D)
        else:
            outs[0][:, at : at + D // 8, :] = value.reshape(8, D // 8, D)
        return
    even = lax.rem(f_ref[0], 2) == 0
    if at is None:
        v = value.reshape(2, D // 2, D)
        outs[0][block, 0 : D // 2, :] = jnp.where(even, v[1], v[0])
        outs[1][block, 0 : D // 2, :] = jnp.where(even, v[0], v[1])
    else:
        v = value.reshape(4, 2, D // 8, D)
        outs[0][:, at : at + D // 8, :] = jnp.where(even, v[:, 1], v[:, 0])
        outs[1][:, at : at + D // 8, :] = jnp.where(even, v[:, 0], v[:, 1])


def head_rows(g, o):
    n = g.shape[0]
    t = (g.astype(F32) * o.astype(F32)).T
    s = jnp.sum(t.reshape(D // HD, HD, n), axis=1, keepdims=True)
    return jnp.broadcast_to(s, (D // HD, 8, n))


def assemble_kernel(rows, f_ref, own, r1, r2, r3, *rest):
    outs, sems = rest[:-1], rest[-1]
    f = f_ref[0]
    c = lax.rem(f, 2)
    a = 2 + 2 * c
    b = 4 - 2 * c
    n = own.shape[0]
    pieces = (
        (own, 0, 0), (r1, 0, a), (r2, 0, b), (r2, n, 6),
        (r3, 0, 1), (r3, n, b + 1), (r3, 2 * n, a + 1), (r3, 3 * n, 7),
    )
    copies = []
    for j, (src, base, off) in enumerate(pieces):
        at = pl.multiple_of(jnp.bitwise_xor(f, off) * rows, rows)
        for k, out in enumerate(outs):
            copy = pltpu.make_async_copy(
                src.at[pl.ds(base + k * rows, rows), :], out.at[pl.ds(at, rows), :], sems.at[j, k]
            )
            copy.start()
            copies.append(copy)
    for copy in copies:
        copy.wait()


def assemble(f, rows, count, own, r1, r2, r3):
    anyspec = pl.BlockSpec(memory_space=pl.ANY)
    return pl.pallas_call(
        functools.partial(assemble_kernel, rows),
        in_specs=[pl.BlockSpec(memory_space=pltpu.SMEM)] + [anyspec] * 4,
        out_shape=[shape((8 * rows, D), BF)] * count,
        scratch_shapes=[pltpu.SemaphoreType.DMA((8, count))],
        compiler_params=params(6),
        name="assemble",
    )(f.reshape(1).astype(jnp.int32), own, r1, r2, r3)


def project_kernel(x0, x1, wq, wk, wv, vec, q_ref, k_ref, v_ref):
    bv = vec[B_VALUE : B_VALUE + 1, :]
    m = x0.shape[0]
    q_ref[...] = (dot(x0[...], wq[...], 1, 0) + vec[B_QUERY : B_QUERY + 1, :]).astype(BF)
    for i, x in enumerate((x0, x1)):
        rows = pl.ds(i * m, m)
        k_ref[rows, :] = dot(x[...], wk[...], 1, 0).astype(BF)
        v_ref[rows, :] = (dot(x[...], wv[...], 1, 0) + bv).astype(BF)


def project(x0, x1, wq, wk, wv, vec):
    m = x0.shape[0]
    return pl.pallas_call(
        project_kernel,
        out_shape=[pltpu.HBM((m, D), BF), pltpu.HBM((2 * m, D), BF), pltpu.HBM((2 * m, D), BF)],
        compiler_params=params(),
        cost_estimate=cost(10 * m * D * D, 20 * m * D),
        name="project",
    )(*in_hbm(x0, x1), wq, wk, wv, vec)


def project_far_kernel(z_ref, b, c, d, e, wk, wv, vec, x_ref, k_ref, v_ref, sems):
    m = b.shape[0]
    middle = (z_ref[0] == 1) | (z_ref[0] == 2)

    def copies(first, second):
        return [pltpu.make_async_copy(first, x_ref.at[pl.ds(0, m), :], sems.at[0]),
                pltpu.make_async_copy(second, x_ref.at[pl.ds(m, m), :], sems.at[1])]

    @pl.when(middle)
    def _():
        for copy in copies(b, d):
            copy.start()
        for copy in copies(b, d):
            copy.wait()

    @pl.when(jnp.logical_not(middle))
    def _():
        for copy in copies(c, e):
            copy.start()
        for copy in copies(c, e):
            copy.wait()

    bv = vec[B_VALUE : B_VALUE + 1, :]
    for i in range(2):
        rows = pl.ds(i * m, m)
        x = x_ref[rows, :]
        k_ref[rows, :] = dot(x, wk[...], 1, 0).astype(BF)
        v_ref[rows, :] = (dot(x, wv[...], 1, 0) + bv).astype(BF)


def project_far(z, b, c, d, e, wk, wv, vec):
    n = 2 * b.shape[0]
    return pl.pallas_call(
        project_far_kernel,
        grid=(1,),
        in_specs=[smem()] + [any_space()] * 4 + [whole(wk), whole(wv), whole(vec)],
        out_specs=[pl.BlockSpec((n, D), lambda i: (0, 0), pipeline_mode=pl.Buffered(1))] * 3,
        out_shape=[pltpu.HBM((n, D), BF)] * 3,
        scratch_shapes=[pltpu.SemaphoreType.DMA((2,))],
        compiler_params=params(),
        cost_estimate=cost(4 * n * D * D, 10 * n * D),
        name="project_far",
    )(z, *in_hbm(b, c, d, e), wk, wv, vec)


def project_memory_kernel(bulk, z_ref, own, out, mid, inward, w_ref, vec, x_ref, k_ref, v_ref, uk, uv, sem, sems):
    loads = bulk.copies(((AT_UK, 1), (AT_UV, 1)), w_ref, (uk, uv, sem))
    for copy in loads:
        copy.start()
    m = own.shape[0]
    middle = (z_ref[0] == 1) | (z_ref[0] == 2)
    mine = pltpu.make_async_copy(own, x_ref.at[pl.ds(0, m), :], sems.at[0])
    mine.start()

    def near():
        return [pltpu.make_async_copy(out, x_ref.at[pl.ds(m, m), :], sems.at[1]),
                pltpu.make_async_copy(mid, x_ref.at[pl.ds(2 * m, 2 * m), :], sems.at[2])]

    def far():
        return [pltpu.make_async_copy(inward, x_ref.at[pl.ds(m, 3 * m), :], sems.at[3])]

    @pl.when(middle)
    def _():
        for copy in near():
            copy.start()
        for copy in near():
            copy.wait()

    @pl.when(jnp.logical_not(middle))
    def _():
        for copy in far():
            copy.start()
        for copy in far():
            copy.wait()

    mine.wait()
    for copy in loads:
        copy.wait()
    x = x_ref[...]
    k_ref[...] = dot(x, square(uk), 1, 0).astype(BF)
    v_ref[...] = (dot(x, square(uv), 1, 0) + vec[C_VALUE : C_VALUE + 1, :]).astype(BF)


def project_memory(z, own, out, mid, inward, bulk, vec):
    n = 4 * own.shape[0]
    return pl.pallas_call(
        functools.partial(project_memory_kernel, bulk),
        grid=(1,),
        in_specs=[smem()] + [any_space()] * 5 + [whole(vec)],
        out_specs=[pl.BlockSpec((n, D), lambda i: (0, 0), pipeline_mode=pl.Buffered(1))] * 3,
        out_shape=[pltpu.HBM((n, D), BF)] * 3,
        scratch_shapes=bulk.scratch(((AT_UK, 1), (AT_UV, 1))) + [pltpu.SemaphoreType.DMA((4,))],
        compiler_params=params(),
        cost_estimate=cost(4 * n * D * D, 10 * n * D),
        name="project_memory",
    )(z, *in_hbm(own, out, mid, inward), bulk.array, vec)


def attend_kernel(block, parts, q_ref, *refs):
    o_ref, lse_ref = refs[-2:]
    lane = lax.broadcasted_iota(jnp.int32, (block, 128), 1) < HD
    k = jnp.concatenate([r[...] for r in refs[:parts]])
    v = jnp.concatenate([r[...] for r in refs[parts : 2 * parts]])
    for i in range(q_ref.shape[0] // block):
        rows = pl.ds(i * block, block)
        q = q_ref[rows, :] * BF(SCALE)
        outs = []
        for a in range(2):
            qm = jnp.where(lane == (a == 0), q, jnp.zeros_like(q))
            s = dot(qm, k, 1, 1)
            top = jnp.max(s, axis=1, keepdims=True)
            p = jnp.exp(s - top)
            count = jnp.sum(p, axis=1, keepdims=True)
            outs.append(dot(p.astype(BF), v, 1, 0) / count)
            lse = jnp.broadcast_to(top + jnp.log(count), (block, 128))
            lse_ref[a, :, rows] = lse.T[:8]
        o_ref[rows, :] = jnp.where(lane, outs[0], outs[1]).astype(BF)


def attend(q, ks, vs):
    n, kv = q.shape[0], sum(k.shape[0] for k in ks)
    pairs = D // 128

    def cols(m):
        return pl.BlockSpec((m, 128), lambda h: (0, h))

    q, *kv_arrays = in_hbm(q, *ks, *vs)
    return pl.pallas_call(
        functools.partial(attend_kernel, 256, len(ks)),
        grid=(pairs,),
        in_specs=[cols(n)] + [cols(a.shape[0]) for a in ks] * 2,
        out_specs=[cols(n), pl.BlockSpec((2, 8, n), lambda h: (h, 0, 0))],
        out_shape=[shape((n, D), BF), pltpu.HBM((2 * pairs, 8, n), F32)],
        compiler_params=params(),
        cost_estimate=cost(16 * n * kv * D, 4 * kv * D, 8 * n * kv),
        name="attend",
    )(q, *kv_arrays)


def attend_back_kernel(first, bulk, q_ref, g_ref, delta_ref, lse_ref, k_ref, v_ref, *refs):
    h = pl.program_id(0)
    *refs, dk_all, dv_all, wk_ref, wv_ref, sem = refs
    if bulk is None:
        *weights, = refs[:2]
        refs = refs[2:]
        copies = [pltpu.make_async_copy(weights[i], (wk_ref, wv_ref)[i], sem.at[i]) for i in range(2)]
    else:
        copies = bulk.copies(((AT_UK, 1), (AT_UV, 1)), refs[0], (wk_ref, wv_ref, sem))
        refs = refs[1:]

    @pl.when(h == 0)
    def _():
        for copy in copies:
            copy.start()

    if not first:
        acc_ref, *refs = refs
    p_ref, dqt_ref, dk_ref, dv_ref = refs
    n = q_ref.shape[0]
    g = g_ref[...]
    q = q_ref[...] * BF(SCALE)
    k = k_ref[...]
    v = v_ref[...]
    lane = lax.broadcasted_iota(jnp.int32, (n, 128), 1) < HD
    zero = jnp.zeros_like(q)
    dk = jnp.zeros(k.shape, F32)
    dv = jnp.zeros(k.shape, F32)
    dqs = []
    for a in range(2):
        qm = jnp.where(lane == (a == 0), q, zero)
        gm = jnp.where(lane == (a == 0), g, zero)
        p = jnp.exp(dot(k, qm, 1, 1) - lse_ref[a, 0:1, :])
        dp = dot(v, gm, 1, 1)
        ds = (p * (dp - delta_ref[a, 0:1, :])).astype(BF)
        dv = dv + dot(p.astype(BF), gm, 1, 0)
        dk = dk + dot(ds, qm, 1, 0)
        dqs.append(dot(k, ds, 0, 0))
    top_half = lax.broadcasted_iota(jnp.int32, (128, n), 0) < HD
    dqt = jnp.where(top_half, dqs[0], dqs[1])
    if not first:
        dqt = dqt + acc_ref[...]
    dqt_ref[...] = dqt
    dk = dk.astype(BF)
    dv = dv.astype(BF)
    dk_ref[...] = dk
    dv_ref[...] = dv
    for i in range(D // 128):

        @pl.when(h == i)
        def _(i=i):
            dk_all[:, i * 128 : (i + 1) * 128] = dk
            dv_all[:, i * 128 : (i + 1) * 128] = dv

    @pl.when(h == pl.num_programs(0) - 1)
    def _():
        for copy in copies:
            copy.wait()
        p_ref[...] = (dot(dk_all[...], square(wk_ref), 1, 1) + dot(dv_all[...], square(wv_ref), 1, 1)).astype(
            p_ref.dtype
        )


def attend_back(q, g, delta, lse, k, v, at, m, weights, acc, dtype):
    n = q.shape[0]
    pairs = D // 128
    bulk = weights if isinstance(weights, Bulk) else None
    weights = weights if bulk is None else (bulk.array,)

    def cols(rows, i=0):
        return pl.BlockSpec((rows, 128), lambda h: (i, h))

    by_head = pl.BlockSpec((2, 8, n), lambda h: (h, 0, 0))
    acc_spec = pl.BlockSpec((128, n), lambda h: (h, 0))
    first = acc is None
    arrays = in_hbm(q, g, delta, lse, k, v, *weights, *([] if first else [acc]))
    shapes = [pltpu.VMEM((m, D), BF)] * 2
    shapes += bulk.scratch(((AT_UK, 1), (AT_UV, 1))) if bulk else (
        [pltpu.VMEM((D, D), BF)] * 2 + [pltpu.SemaphoreType.DMA((2,))]
    )
    return pl.pallas_call(
        functools.partial(attend_back_kernel, first, bulk),
        grid=(pairs,),
        in_specs=[cols(n), cols(n), by_head, by_head, cols(m, at), cols(m, at)]
        + [any_space()] * len(weights)
        + ([] if first else [acc_spec]),
        out_specs=[pl.BlockSpec((m, D), lambda h: (0, 0)), acc_spec, cols(m), cols(m)],
        out_shape=[shape((m, D), dtype), pltpu.HBM((D, n), F32), pltpu.HBM((m, D), BF), pltpu.HBM((m, D), BF)],
        scratch_shapes=shapes,
        compiler_params=params(),
        cost_estimate=cost(44 * n * m * D, 12 * m * D, 8 * n * m),
        name="attend_back",
    )(*arrays)


def after_self_kernel(bulk, o, x, w_ref, vec, n_ref, r_ref, low_ref, cq_ref, wo, uq, sem):
    copies = bulk.copies(((AT_WO, 1), (AT_UQ, 1)), w_ref, (wo, uq, sem))
    for copy in copies:
        copy.start()

    def v(i):
        return vec[i : i + 1, :]

    copies[0].wait()
    sum_one = x[...].astype(F32) + dot(o[...], square(wo), 1, 0) + v(B_OUTPUT)
    n, r = norm(sum_one)
    low = (n * v(GAIN_A) + v(SHIFT_A)).astype(BF)
    n_ref[...] = n
    r_ref[...] = jnp.broadcast_to(r, r_ref.shape)
    low_ref[...] = low
    copies[1].wait()
    cq_ref[...] = (dot(low, square(uq), 1, 0) + v(C_QUERY)).astype(BF)


def after_self(o, x, bulk, vec):
    m = x.shape[0]
    outs = [shape((m, D), F32), shape((m, 128), F32), shape((m, D), BF), pltpu.HBM((m, D), BF)]
    return pl.pallas_call(
        functools.partial(after_self_kernel, bulk),
        grid=(1,),
        in_specs=[whole(o), whole(x), any_space(), whole(vec)],
        out_specs=[whole(s) for s in outs],
        out_shape=outs,
        scratch_shapes=bulk.scratch(((AT_WO, 1), (AT_UQ, 1))),
        compiler_params=params(),
        cost_estimate=cost(4 * m * D * D, 12 * m * D),
        name="after_self",
    )(o, x, bulk.array, vec)


GELU_C = 0.7978845608028654
GELU_A = 0.044715


FEED_WEIGHTS = ((AT_UO, 1),) + tuple((AT_EXPAND + j, 1) for j in range(4)) + ((0, 4),)


def feed_kernel(size, bulk, f_ref, ca, n1, cot, w_ref, vec,
                out_ref, two_ref, catt_ref, delta_ref, dvec_ref, *refs):
    if size == 8:
        *refs, held, sems = refs
        sums = Outbox(refs[0], held, sems)
        uo, *expand, wred_ref, sem = refs[1:]
    else:
        sums, (uo, *expand, wred_ref, sem) = refs[:-7], refs[-7:]
    copies = bulk.copies(FEED_WEIGHTS, w_ref, (uo, *expand, wred_ref, sem))
    for copy in copies:
        copy.start()

    def v(i):
        return vec[i : i + 1, :]

    copies[0].wait()
    first = n1[...] * v(GAIN_A) + v(SHIFT_A)
    sum_two = first + dot(ca[...], square(uo), 1, 0) + v(C_OUTPUT)
    n2, r2 = norm(sum_two)
    second = n2 * v(GAIN_B) + v(SHIFT_B)
    low = second.astype(BF)
    sum_three = second + v(B_REDUCE)
    acts, slopes = [], []
    for copy in copies[1:]:
        copy.wait()
    wred = square(wred_ref)
    for j in range(4):
        pre = dot(low, square(expand[j]), 1, 0) + v(B_EXPAND + j)
        sq = pre * pre
        t = jnp.tanh(GELU_C * (pre + GELU_A * (sq * pre)))
        half = 0.5 * (1.0 + t)
        act = (pre * half).astype(BF)
        slope = half + 0.5 * pre * (1.0 - t * t) * (GELU_C * (1.0 + 3.0 * GELU_A * sq))
        acts.append(act)
        slopes.append(slope)
        sum_three = sum_three + dot(act, wred[j * D : (j + 1) * D], 1, 0)
    n3, r3 = norm(sum_three)
    out_ref[...] = (n3 * v(GAIN_C) + v(SHIFT_C)).astype(BF)
    e = cot[...].astype(F32)
    d_three = norm_back(e, v(GAIN_C), n3, r3)
    branch = d_three.astype(BF)
    dvec_ref[0:1, :] = total(branch.astype(F32))
    dvec_ref[1:2, :] = total(e * n3)
    dvec_ref[2:3, :] = total(e)
    second_grad = d_three
    for j in range(4):
        d_act = dot(branch, wred[j * D : (j + 1) * D], 1, 1)
        d_pre = (d_act * slopes[j]).astype(BF)
        dvec_ref[3 + j : 4 + j, :] = total(d_pre.astype(F32))
        emit(size, f_ref, sums, j, None, dot(acts[j], branch, 0, 0))
        emit(size, f_ref, sums, 4 + j, (4 + j) * D // 8, dot(low, d_pre, 0, 0))
        second_grad = second_grad + dot(d_pre, square(expand[j]), 1, 1)
    d_two = norm_back(second_grad, v(GAIN_B), n2, r2)
    two_ref[...] = d_two
    cross = d_two.astype(BF)
    dvec_ref[7:8, :] = total(second_grad * n2)
    dvec_ref[8:9, :] = total(second_grad)
    dvec_ref[9:10, :] = total(cross.astype(F32))
    emit(size, f_ref, sums, 8, D, dot(ca[...], cross, 0, 0))
    att = dot(cross, square(uo), 1, 1).astype(BF)
    catt_ref[...] = att
    delta_ref[...] = head_rows(att, ca[...])
    if size == 8:
        sums.wait()


def feed(size, f, ca, n1, cot, bulk, vec):
    m = ca.shape[0]
    outs = [
        shape((m, D), BF), shape((m, D), F32), pltpu.HBM((m, D), BF), pltpu.HBM((D // HD, 8, m), F32),
        shape((16, D), F32),
    ] + sums_out(size, 9 * D // 8, 9)
    specs = [whole(s) for s in outs]
    extra = []
    if size == 8:
        rows = 9 * D // 8
        outs[-1] = pltpu.HBM((8, rows, D), BF)
        specs[-1] = any_space()
        extra = [pltpu.VMEM((8, rows, D), BF), pltpu.SemaphoreType.DMA((9,))]
    return pl.pallas_call(
        functools.partial(feed_kernel, size, bulk),
        grid=(1,),
        in_specs=[smem(), whole(ca), whole(n1), whole(cot), any_space(), whole(vec)],
        out_specs=specs,
        out_shape=outs,
        scratch_shapes=bulk.scratch(FEED_WEIGHTS) + extra,
        compiler_params=params(34),
        cost_estimate=cost(2 * 27 * m * D * D, 24 * m * D * 4, 4 * m * D),
        name="feed",
    )(f, ca, n1, cot, bulk.array, vec)


def after_cross_back_kernel(size, bulk, f_ref, dqt, k0, k1, v0, v1, mem, low, o, two, n1, r1, w_ref, vec,
                            one_ref, att_ref, delta_ref, dvec_ref, *refs):
    sums, (uq, wo, sem) = refs[:-3], refs[-3:]
    copies = bulk.copies(((AT_UQ, 1), (AT_WO, 1)), w_ref, (uq, wo, sem))
    for copy in copies:
        copy.start()
    gain = vec[GAIN_A : GAIN_A + 1, :]
    gq = (dqt[...].T * SCALE).astype(BF)
    for copy in copies:
        copy.wait()
    first_grad = two[...] + dot(gq, square(uq), 1, 1)
    n = n1[...]
    d_one = norm_back(first_grad, gain, n, r1[:, 0:1])
    one_ref[...] = d_one
    low_one = d_one.astype(BF)
    att = dot(low_one, square(wo), 1, 1).astype(BF)
    att_ref[...] = att
    delta_ref[...] = head_rows(att, o[...])
    m = k0.shape[0]
    dvec_ref[0:1, :] = total(gq.astype(F32))
    dvec_ref[1:2, :] = total(first_grad * n)
    dvec_ref[2:3, :] = total(first_grad)
    dvec_ref[3:4, :] = total(low_one.astype(F32))
    dvec_ref[4:5, :] = total(v0[...].astype(F32)) + total(v1[...].astype(F32))
    r = D // 8
    emit(size, f_ref, sums, 0, 0, dot(low[...], gq, 0, 0))
    emit(size, f_ref, sums, 1, r, dot(mem[0:m, :], k0[...], 0, 0) + dot(mem[m:, :], k1[...], 0, 0))
    emit(size, f_ref, sums, 2, 2 * r, dot(mem[0:m, :], v0[...], 0, 0) + dot(mem[m:, :], v1[...], 0, 0))
    emit(size, f_ref, sums, 3, 3 * r, dot(o[...], low_one, 0, 0))


def after_cross_back(size, f, dqt, ks, vs, mem, low, o, two, n1, r1, bulk, vec):
    m = low.shape[0]
    arrays = in_hbm(dqt, *ks, *vs, mem) + [low, o, two, n1, r1]
    outs = [shape((m, D), F32), pltpu.HBM((m, D), BF), pltpu.HBM((D // HD, 8, m), F32), shape((8, D), F32)]
    outs += sums_out(size, 4 * D // 8, 4, True)
    return pl.pallas_call(
        functools.partial(after_cross_back_kernel, size, bulk),
        grid=(1,),
        in_specs=[smem()] + [whole(a) for a in arrays] + [any_space(), whole(vec)],
        out_specs=[whole(s) for s in outs],
        out_shape=outs,
        scratch_shapes=bulk.scratch(((AT_UQ, 1), (AT_WO, 1))),
        compiler_params=params(24),
        cost_estimate=cost(2 * 8 * m * D * D, 14 * m * D * 4),
        name="after_cross_back",
    )(f, *arrays, bulk.array, vec)


def last_kernel(size, count, f_ref, dqt, *refs):
    ks, vs = refs[:count], refs[count : 2 * count]
    x0, x1, x_far, feed, mid, gq_ref = refs[2 * count : 2 * count + 6]
    *sums, table = refs[2 * count + 6 :]
    m = x0.shape[0]
    xs = [x0[...], x1[...], x_far[0:m, :], x_far[m:, :]]
    gq = (dqt[...].T * SCALE).astype(BF)
    gq_ref[...] = gq
    r = D // 8
    emit(size, f_ref, sums, 0, 0, dot(xs[0], gq, 0, 0))
    for i, parts in ((1, ks), (2, vs)):
        acc = dot(xs[0], parts[0][...], 0, 0)
        for x, p in zip(xs[1:], parts[1:]):
            acc = acc + dot(x, p[...], 0, 0)
        emit(size, f_ref, sums, i, i * r, acc)
    table[...] = jnp.zeros_like(table)
    table[B_QUERY : B_QUERY + 1, :] = total(gq.astype(F32))
    dbv = total(vs[0][...].astype(F32))
    for v in vs[1:]:
        dbv = dbv + total(v[...].astype(F32))
    table[B_VALUE : B_VALUE + 1, :] = dbv
    for at, src, i in (
        (B_OUTPUT, mid, 3), (GAIN_A, mid, 1), (SHIFT_A, mid, 2), (C_QUERY, mid, 0), (C_VALUE, mid, 4),
        (C_OUTPUT, feed, 9), (GAIN_B, feed, 7), (SHIFT_B, feed, 8),
        (B_REDUCE, feed, 0), (GAIN_C, feed, 1), (SHIFT_C, feed, 2),
    ):
        table[at : at + 1, :] = src[i : i + 1, :]
    if size != 8:
        table[B_EXPAND : B_EXPAND + 4, :] = feed[3:7, :]
        return
    rows = table[0:16, :].astype(BF)
    for chip in range(4):
        wide = jnp.broadcast_to(feed[3 + chip : 4 + chip, :], (16, D)).astype(BF)
        for s in sums:
            s[chip, 3 * r : 3 * r + 16, :] = jnp.zeros((16, D), BF)
            s[chip, 3 * r : 3 * r + 16, 0:128] = rows[:, chip * 128 : (chip + 1) * 128]
            s[chip, 3 * r + 16 : 3 * r + 32, :] = wide


def last(size, f, dqt, ks, vs, xs, feed, mid):
    m = xs[0].shape[0]
    count = len(ks)
    arrays = [f, *in_hbm(dqt, *ks, *vs, *xs), feed, mid]
    outs = [shape((m, D), BF)] + sums_out(size, 3 * D // 8 + 32, 3, True) + [shape((VEC_ROWS, D), F32)]
    return pl.pallas_call(
        functools.partial(last_kernel, size, count),
        grid=(1,),
        in_specs=[smem()] + [whole(a) for a in arrays[1:]],
        out_specs=[whole(s) for s in outs],
        out_shape=outs,
        compiler_params=params(),
        cost_estimate=cost(2 * 9 * m * D * D, 14 * m * D * 2),
        name="last",
    )(*arrays)


def own_rows_kernel(gq, part, one, wq, out):
    out[...] = part[...] + one[...] + dot(gq[...], wq[...], 1, 1)


def own_rows(gq, part, one, wq):
    return pl.pallas_call(
        own_rows_kernel,
        out_shape=shape(part.shape, F32),
        compiler_params=params(),
        cost_estimate=cost(2 * part.shape[0] * D * D, 4 * part.shape[0] * D * 4),
        name="own_rows",
    )(gq, part, one, wq)


def fold_kernel(t_ref, *refs):
    acc = refs[0][...].astype(F32)
    for r in refs[1:-1]:
        acc = acc + r[...].astype(F32)
    refs[-1][...] = acc.astype(BF)


def fold(table, base, count, arrays):
    n = arrays[0].shape[1]
    width = len(arrays)

    def spec(k):
        return pl.BlockSpec((1, n, D), lambda j, t: (t[base + j * width + k], 0, 0))

    return pl.pallas_call(
        fold_kernel,
        grid_spec=pltpu.PrefetchScalarGridSpec(
            num_scalar_prefetch=1,
            grid=(count,),
            in_specs=[spec(k) for k in range(width)],
            out_specs=pl.BlockSpec((1, n, D), lambda j, t: (j, 0, 0)),
        ),
        out_shape=shape((count, n, D), BF),
        compiler_params=params(6),
        name="fold",
    )(table, *arrays)


def start_rows(arrays, out, sems):
    copies = []
    at = 0
    for ref in arrays:
        rows = ref.shape[0]
        for j in range(ref.shape[1] // D):
            copies.append(pltpu.make_async_copy(
                ref.at[:, pl.ds(j * D, D)], out.at[pl.ds(at, rows), :], sems.at[len(copies)]
            ))
            copies[-1].start()
            at += rows
    return copies


def pack_kernel(*refs):
    *arrays, out, sems = refs
    for copy in start_rows(arrays, out, sems):
        copy.wait()


def pack_plain(arrays):
    return jnp.concatenate([a[:, i : i + D] for a in arrays for i in range(0, a.shape[1], D)])


def pack_rows(arrays):
    if arrays[0].shape[0] % 16:
        return pack_plain(arrays)
    pieces = sum(a.shape[1] // D for a in arrays)
    rows = sum(a.shape[0] * a.shape[1] // D for a in arrays)
    return pl.pallas_call(
        pack_kernel,
        in_specs=[any_space()] * len(arrays),
        out_shape=shape((rows, D), BF),
        scratch_shapes=[pltpu.SemaphoreType.DMA((pieces,))],
        compiler_params=params(4),
        name="pack_rows",
    )(*in_hbm(*arrays))


def table_kernel(rows, count, *refs):
    arrays, refs = refs[:count], refs[count:]
    *vectors, expand, out, table, short, long, sems, vec_sems = refs
    copies = start_rows(arrays, out, sems)
    loads = [pltpu.make_async_copy(ref, short.at[i], vec_sems.at[i]) for i, ref in enumerate(vectors)]
    loads.append(pltpu.make_async_copy(expand, long, vec_sems.at[len(vectors)]))
    for load in loads:
        load.start()
    table[...] = jnp.zeros_like(table)
    for load in loads:
        load.wait()
    for i in range(len(vectors)):
        table[i : i + 1, 0:rows] = short[i].astype(F32)
    for j in range(4):
        table[B_EXPAND + j : B_EXPAND + j + 1, 0:rows] = long[:, j * rows : (j + 1) * rows].astype(F32)
    out[len(copies) * rows :, :] = table[...].astype(BF)
    for copy in copies:
        copy.wait()


def pack_first(arrays, vectors, expand):
    rows = vectors[0].shape[0]
    plain = rows % 16 != 0
    used = [] if plain else arrays
    vectors = [v.reshape(1, -1) for v in vectors]
    out = pl.pallas_call(
        functools.partial(table_kernel, rows, len(used)),
        in_specs=[any_space()] * (len(used) + len(vectors) + 1),
        out_shape=shape((len(used) * rows + VEC_ROWS, D), BF),
        scratch_shapes=[
            pltpu.VMEM((VEC_ROWS, D), F32), pltpu.VMEM((len(vectors), 1, rows), BF),
            pltpu.VMEM((1, 4 * rows), BF), pltpu.SemaphoreType.DMA((len(arrays),)),
            pltpu.SemaphoreType.DMA((len(vectors) + 1,)),
        ],
        compiler_params=params(4),
        name="pack_first",
    )(*in_hbm(*used, *vectors, expand.reshape(1, -1)))
    return pack_plain([*arrays, out]) if plain else out


ENDS_IN = ((1, 0), (2, 3))
ENDS_OUT = ((0, 1), (3, 2))
MIDDLE = ((1, 2), (2, 1))
PAIRS = ((0, 1), (1, 0), (2, 3), (3, 2))
ACROSS = ((0, 2), (2, 0), (1, 3), (3, 1))


def over_seq(x, pairs):
    return lax.ppermute(x, "seq", pairs)


def after(x, *deps):
    return lax.optimization_barrier((x,) + deps)[0]


def add(p, r):
    return (p.astype(F32) + r.astype(F32)).astype(BF)


def swap_core():
    return [(i, i ^ 1) for i in range(8)]


def swap_first():
    return [(i, i ^ (4 if i & 1 else 2)) for i in range(8)]


def swap_second():
    return [(i, i ^ (2 if i & 1 else 4)) for i in range(8)]


def gather_plane(own, deps, late):
    r1 = lax.ppermute(own, "fsdp", swap_first())
    both = after(jnp.concatenate([own, r1]), *deps)
    r2 = lax.ppermute(both, "fsdp", swap_second())
    r3 = lax.ppermute(after(jnp.concatenate([both, r2]), *late), "fsdp", swap_core())
    return r1, r2, r3


def fold_table(f):
    c = lax.rem(f, 2)
    x = lax.rem(f // 2, 2)
    y = f // 4
    even = c == 0
    send0 = jnp.where(even, 1 - x, 2 * (1 - y))
    send1 = jnp.where(even, 3 - x, 3 - 2 * y)
    keep0 = jnp.where(even, x, 2 * y)
    keep1 = jnp.where(even, 2 + x, 2 * y + 1)
    own = jnp.where(even, y, x)
    mine = jnp.where(own == 0, keep0, keep1)
    other = jnp.where(own == 0, keep1, keep0)
    zero = 0 * own
    return jnp.stack([send0, send0, send1, send1, other, other, 1 - own, mine, mine, own, zero]).astype(jnp.int32)


class PlaneReduce:
    def __init__(self, table, sums):
        self.table = table
        self.keep = sums[1]
        self.got = [lax.ppermute(sums[0], "fsdp", swap_core())]

    def second(self, *deps):
        out = fold(self.table, 0, 2, [after(self.keep, *deps), self.got[0]])
        self.got.append(lax.ppermute(out, "fsdp", swap_first()))

    def third(self, *deps):
        out = fold(self.table, 4, 1, [after(self.keep, *deps)] + self.got)
        self.got.append(lax.ppermute(out, "fsdp", swap_second()))

    def end(self, *deps):
        return fold(self.table, 7, 1, [after(self.keep, *deps)] + self.got)[0]


class PlainReduce:
    def __init__(self, table, sums):
        self.got = [lax.psum_scatter(sums, "fsdp", scatter_dimension=0, tiled=False)]

    def second(self, *deps):
        pass

    third = second

    def end(self, *deps):
        return self.got[0]


def on_device(size, tokens, memory, cotangent,
              w_query, w_key, w_value, w_output, b_query, b_value, b_output, gain_attend, shift_attend,
              u_query, u_key, u_value, u_output, c_query, c_value, c_output, gain_cross, shift_cross,
              w_expand, b_expand, w_reduce, b_reduce, gain_feed, shift_feed):
    rows = w_query.shape[0]
    f = lax.axis_index("fsdp")
    x = tokens[0]
    mem = memory[0]

    vectors = (b_query, b_value, b_output, gain_attend, shift_attend, c_query, c_value, c_output,
               gain_cross, shift_cross, b_reduce, gain_feed, shift_feed)
    first = pack_first([w_query, w_key, w_value], vectors, b_expand)
    pack = pack_rows([w_reduce, w_expand, w_output, u_query, u_key, u_value, u_output])
    c1 = over_seq(x, PAIRS)
    x_b = over_seq(x, MIDDLE)
    x_d = over_seq(c1, MIDDLE)
    x_c = over_seq(x_b, ENDS_IN)
    mem_out = over_seq(after(mem, c1, x_b), ENDS_OUT)
    if size == 8:
        r1, r2, r3 = gather_plane(first, (c1, x_b), (x_d, x_c, mem_out))
        wq, wk, wv = assemble(f, rows, 3, first, r1, r2, r3)
        n = first.shape[0]
        tables = [first, r1, r2[:n], r2[n:]] + [r3[i * n : (i + 1) * n] for i in range(4)]
        tables = jnp.stack([t[3 * rows : 3 * rows + N_VEC, :rows] for t in tables])
        c = lax.rem(f, 2)
        a, b = 2 + 2 * c, 4 - 2 * c
        offsets = jnp.stack([0 * c, a, b, 6 + 0 * c, 1 + 0 * c, b + 1, a + 1, 7 + 0 * c])
        pick = (jnp.arange(8)[:, None] == (offsets ^ f)[None, :]).astype(BF)
        tables = jnp.einsum("gd,dkl->gkl", pick, tables, preferred_element_type=F32)
    else:
        g = lax.all_gather(first, "fsdp", axis=0, tiled=False)
        wq, wk, wv = [g[:, i * rows : (i + 1) * rows].reshape(D, D) for i in range(3)]
        tables = g[:, 3 * rows : 3 * rows + N_VEC, :rows].astype(F32)
    vec = jnp.concatenate(
        [tables[:, :B_EXPAND].transpose(1, 0, 2).reshape(B_EXPAND, D), tables[:, B_EXPAND:].reshape(4, D)]
    )
    vec = jnp.pad(vec, ((0, VEC_ROWS - N_VEC), (0, 0)))

    everything = lax.all_gather(pack, "fsdp", axis=0, tiled=False)

    if size != 8:
        blocks = [everything[:, : 4 * rows].reshape(4, D, D)]
        for i in range(4, 13):
            blocks.append(everything[:, i * rows : (i + 1) * rows].reshape(1, D, D))
        everything = jnp.concatenate(blocks)
    bulk = Bulk(everything, size)

    def by_owner(stack, count):
        s = stack.reshape(count, size, rows, D)
        return s.transpose(1, 0, 2, 3).reshape(size, count * rows, D)

    def reduce(sums, tall, count, extra=None):
        if size == 8 and len(sums) == 2:
            return PlaneReduce(table, sums)
        if size == 8:
            return PlainReduce(table, sums[0])
        s = sums[0]
        blocks = [s[: 4 * D].reshape(size, 4 * rows, D), s[4 * D :]] if tall else [s]
        blocks[-1] = by_owner(blocks[-1], count)
        return PlainReduce(table, jnp.concatenate(blocks + ([] if extra is None else [extra]), 1))

    table = fold_table(f)
    f1 = f.reshape(1).astype(jnp.int32)
    z1 = lax.axis_index("seq").reshape(1).astype(jnp.int32)
    q, k0, v0 = project(x, c1, wq, wk, wv, vec)
    x_e = over_seq(x_d, ENDS_IN)
    mem_mid = over_seq(after(jnp.concatenate([mem, mem_out]), x_d), MIDDLE)
    x_far, k1, v1 = project_far(z1, x_b, x_c, x_d, after(x_e, k0), wk, wv, vec)
    mem_in = over_seq(jnp.concatenate([mem, after(mem_mid, x_far)]), ENDS_IN)
    o, lse = attend(q, [k0, k1], [v0, v1])
    n1, r_one, low, cq = after_self(o, x, bulk, vec)
    mem_x, mk, mv = project_memory(z1, mem, mem_out, mem_mid, after(mem_in, low), bulk, vec)
    ca, cross_lse = attend(cq, [mk], [mv])
    layer_out, d_two, d_catt, cross_delta, dvec_feed, *sums = feed(
        size, f1, ca, n1, cotangent[0], bulk, vec
    )
    feed_sum = reduce(sums, True, 5)

    m = 2 * mem.shape[0]
    def cross_back(g, i, acc, dtype):
        return attend_back(cq, g, cross_delta, cross_lse, mk, mv, i, m, bulk, acc, dtype)

    far, dqt, dk1, dv1 = cross_back(d_catt, 1, None, BF)
    far_in = over_seq(far, ENDS_OUT)
    near, dqt, dk0, dv0 = cross_back(after(d_catt, far), 0, dqt, F32)
    d_one, d_att, self_delta, dvec_mid, *sums = after_cross_back(
        size, f1, after(dqt, far_in), (dk0, dk1), (dv0, dv1), mem_x, low, o, d_two, n1, r_one, bulk, vec
    )
    mid_sum = reduce(sums, False, 4)
    far_mid = over_seq(after(add(far, far_in), d_att), MIDDLE)
    m = x.shape[0]

    def self_back(g, i, acc, dtype):
        k, v = ((k0, v0), (k1, v1))[i // 2]
        return attend_back(q, g, self_delta, lse, k, v, i % 2, m, (wk, wv), acc, dtype)

    p3, dqt, dk3, dv3 = self_back(d_att, 3, None, BF)
    e = over_seq(p3, ENDS_OUT)
    mid_sum.second(p3)
    half = m // 2
    p2, dqt, dk2, dv2 = self_back(after(d_att, p3, feed_sum.got[0], mid_sum.got[0]), 2, dqt, BF)
    feed_part = feed_sum.end()
    sum_feed = lax.psum(feed_part, "seq")
    cc = over_seq(p2, ENDS_OUT)
    mid_sum.third(p2)
    p1, dqt, dk1, dv1 = self_back(after(d_att, e, far_mid, p2, mid_sum.got[-2 if size == 8 else 0]), 1, dqt, BF)
    near_in = over_seq(after(add(near[half:], far_mid[half:]), p1), PAIRS)
    d = over_seq(after(add(p3, e), p1), MIDDLE)
    mid_part = mid_sum.end(p1)
    mid_in = over_seq(mid_part, PAIRS)
    p0, dqt, dk0, dv0 = self_back(after(d_att, cc, p1, mid_part), 0, dqt, F32)
    b = over_seq(after(add(p2, cc), p0), MIDDLE)
    mid_part = add(mid_part, after(mid_in, p0))
    dqt = after(dqt, d, mid_part, sum_feed)
    mid_in = over_seq(mid_part, ACROSS)
    gq, *sums, vec_table = last(
        size, f1, dqt, (dk0, dk1, dk2, dk3), (dv0, dv1, dv2, dv3), (x, c1, x_far), dvec_feed, dvec_mid
    )
    extra = None
    if size != 8:
        extra = jnp.concatenate([
            vec_table[:B_EXPAND].reshape(B_EXPAND, size, rows).transpose(1, 0, 2),
            vec_table[B_EXPAND:N_VEC].reshape(size, 4, rows),
        ], 1)
        extra = jnp.pad(extra, ((0, 0), (0, VEC_ROWS - N_VEC), (0, D - rows))).astype(BF)
    late_sum = reduce(sums, False, 3, extra)
    tok_mine = own_rows(gq, p0, d_one, wq)
    a = over_seq(after(add(p1, d), gq), PAIRS)
    late_sum.second()
    late_sum.third()
    late = late_sum.end()
    late_end = late
    got = over_seq(late, PAIRS)
    late = add(late, got)
    got = over_seq(late, ACROSS)
    sum_last = late.astype(F32) + got.astype(F32)
    sum_feed = sum_feed.astype(F32)
    sum_mid = mid_part.astype(F32) + mid_in.astype(F32)
    grad_tok = after(tok_mine, late_end) + a.astype(F32) + b.astype(F32)
    grad_mem = after(near[:half], late_end) + near_in.astype(F32) + far_mid[:half].astype(F32)
    sum_feed = after(sum_feed, late_end)

    if size == 8:
        c = lax.rem(f, 2)
        vecs = lax.dynamic_slice(sum_last, (3 * rows, c * rows), (B_EXPAND, rows))
        db_expand = lax.dynamic_slice(sum_last, (3 * rows + 16, c * 4 * rows), (1, 4 * rows)).reshape(4 * rows)
    else:
        vecs = sum_last[3 * rows : 3 * rows + N_VEC, :rows]
        db_expand = vecs[B_EXPAND:].reshape(4 * rows)
    dw_reduce = sum_feed[: 4 * rows]
    dw_expand = jnp.concatenate([sum_feed[(4 + j) * rows : (5 + j) * rows] for j in range(4)], 1)
    du_output = sum_feed[8 * rows :]
    du_query, du_key, du_value, dw_output = [sum_mid[i * rows : (i + 1) * rows] for i in range(4)]
    dw_query, dw_key, dw_value = [sum_last[i * rows : (i + 1) * rows] for i in range(3)]
    return (
        layer_out[None], grad_tok[None], grad_mem[None],
        dw_query, dw_key, dw_value, dw_output, vecs[0], vecs[1], vecs[2], vecs[3], vecs[4],
        du_query, du_key, du_value, du_output, vecs[5], vecs[6], vecs[7], vecs[8], vecs[9],
        dw_expand, db_expand, dw_reduce, vecs[10], vecs[11], vecs[12],
    )


def solution(mesh):
    rows = P("fsdp", "seq", None)
    mat, vec = P("fsdp", None), P("fsdp")
    weights = (mat,) * 4 + (vec,) * 5 + (mat,) * 4 + (vec,) * 5 + (mat, vec, mat, vec, vec, vec)
    return jax.shard_map(
        functools.partial(on_device, mesh.shape["fsdp"]),
        mesh=mesh,
        in_specs=(rows,) * 3 + weights,
        out_specs=(rows,) * 3 + weights,
        check_vma=False,
    )
```

```python
import functools

import jax
import jax.numpy as jnp
from jax import lax
from jax.experimental import pallas as pl
from jax.experimental.pallas import tpu as pltpu
from jax.sharding import PartitionSpec as P

HD = 64
D = 512
EPS = 1e-05
SCALE = HD ** (-0.5)
BF = jnp.bfloat16
F32 = jnp.float32

B_QUERY, B_VALUE, B_OUTPUT, GAIN_A, SHIFT_A = 0, 1, 2, 3, 4
C_QUERY, C_VALUE, C_OUTPUT, GAIN_B, SHIFT_B = 5, 6, 7, 8, 9
B_REDUCE, GAIN_C, SHIFT_C, B_EXPAND = 10, 11, 12, 13
N_VEC = 17
VEC_ROWS = 32

AT_EXPAND, AT_WO, AT_UQ, AT_UK, AT_UV, AT_UO = 4, 8, 9, 10, 11, 12


def dot(a, b, ca, cb):
    return lax.dot_general(a, b, (((ca,), (cb,)), ((), ())), preferred_element_type=F32)


def params(mib=14):
    return pltpu.CompilerParams(vmem_limit_bytes=mib << 20)


def cost(flops, nbytes, trans=0):
    return pl.CostEstimate(flops=flops // 100, bytes_accessed=nbytes // 100, transcendentals=0)


def shape(dims, dtype):
    return jax.ShapeDtypeStruct(dims, dtype)


def whole(x):
    nd = len(x.shape)
    return pl.BlockSpec(x.shape, lambda i: (0,) * nd, pipeline_mode=pl.Buffered(1))


def norm(hidden):
    centre = jnp.mean(hidden, axis=-1, keepdims=True)
    offset = hidden - centre
    spread = jnp.mean(offset * offset, axis=-1, keepdims=True)
    r = lax.rsqrt(spread + EPS)
    return offset * r, r


def norm_back(e, gain, n, r):
    t = e * gain
    return r * (t - jnp.mean(t, axis=-1, keepdims=True) - n * jnp.mean(t * n, axis=-1, keepdims=True))


def total(x):
    return jnp.sum(x, axis=0, keepdims=True)


def square(ref):
    return ref[...].reshape(-1, ref.shape[-1])


def smem():
    return pl.BlockSpec(memory_space=pltpu.SMEM)


def any_space():
    return pl.BlockSpec(memory_space=pltpu.HBM)


def in_hbm(*arrays):
    return [pltpu.with_memory_space_constraint(a, pltpu.HBM) for a in arrays]


class Bulk:
    def __init__(self, array, size):
        self.array = in_hbm(array)[0]
        self.by_owner = size == 8

    def scratch(self, wanted):
        shapes = []
        for count in (c for _, c in wanted):
            shapes.append(pltpu.VMEM((8, count * D // 8, D) if self.by_owner else (count, D, D), BF))
        return shapes + [pltpu.SemaphoreType.DMA((len(wanted),))]

    def copies(self, wanted, ref, scratch):
        out = []
        for i, (at, count) in enumerate(wanted):
            if self.by_owner:
                src = ref.at[:, pl.ds(at * D // 8, count * D // 8), :]
            else:
                src = ref.at[pl.ds(at, count)]
            out.append(pltpu.make_async_copy(src, scratch[i], scratch[-1].at[i]))
        return out


def sums_out(size, rows, count, late=False):
    if size == 8 and late:
        return [shape((4, rows, D), BF)] * 2
    if size == 8:
        return [shape((8, rows, D), BF)]
    return [shape((count * D, D), BF)]


class Outbox:
    def __init__(self, out, held, sems):
        self.out, self.held, self.sems = out, held, sems
        self.copies = []

    def send(self, block, at, value):
        v = value.astype(BF)
        if at is None:
            part = (pl.ds(2 * block, 2), pl.ds(0, D // 2))
            v = v.reshape(2, D // 2, D)
        else:
            part = (pl.ds(0, 8), pl.ds(at, D // 8))
            v = v.reshape(8, D // 8, D)
        self.held[part[0], part[1], :] = v
        copy = pltpu.make_async_copy(
            self.held.at[part[0], part[1]], self.out.at[part[0], part[1]], self.sems.at[len(self.copies)]
        )
        copy.start()
        self.copies.append(copy)

    def wait(self):
        for copy in self.copies:
            copy.wait()


def emit(size, f_ref, outs, block, at, value):
    if isinstance(outs, Outbox):
        outs.send(block, at, value)
        return
    value = value.astype(BF)
    if size != 8:
        outs[0][block * D : (block + 1) * D, :] = value
        return
    if len(outs) == 1:
        if at is None:
            outs[0][2 * block : 2 * block + 2, 0 : D // 2, :] = value.reshape(2, D // 2, D)
        else:
            outs[0][:, at : at + D // 8, :] = value.reshape(8, D // 8, D)
        return
    even = lax.rem(f_ref[0], 2) == 0
    if at is None:
        v = value.reshape(2, D // 2, D)
        outs[0][block, 0 : D // 2, :] = jnp.where(even, v[1], v[0])
        outs[1][block, 0 : D // 2, :] = jnp.where(even, v[0], v[1])
    else:
        v = value.reshape(4, 2, D // 8, D)
        outs[0][:, at : at + D // 8, :] = jnp.where(even, v[:, 1], v[:, 0])
        outs[1][:, at : at + D // 8, :] = jnp.where(even, v[:, 0], v[:, 1])


def head_rows(g, o):
    n = g.shape[0]
    t = (g.astype(F32) * o.astype(F32)).T
    s = jnp.sum(t.reshape(D // HD, HD, n), axis=1, keepdims=True)
    return jnp.broadcast_to(s, (D // HD, 8, n))


def assemble_kernel(rows, f_ref, own, r1, r2, r3, *rest):
    outs, sems = rest[:-1], rest[-1]
    f = f_ref[0]
    c = lax.rem(f, 2)
    a = 2 + 2 * c
    b = 4 - 2 * c
    n = own.shape[0]
    pieces = (
        (own, 0, 0), (r1, 0, a), (r2, 0, b), (r2, n, 6),
        (r3, 0, 1), (r3, n, b + 1), (r3, 2 * n, a + 1), (r3, 3 * n, 7),
    )
    copies = []
    for j, (src, base, off) in enumerate(pieces):
        at = pl.multiple_of(jnp.bitwise_xor(f, off) * rows, rows)
        for k, out in enumerate(outs):
            copy = pltpu.make_async_copy(
                src.at[pl.ds(base + k * rows, rows), :], out.at[pl.ds(at, rows), :], sems.at[j, k]
            )
            copy.start()
            copies.append(copy)
    for copy in copies:
        copy.wait()


def assemble(f, rows, count, own, r1, r2, r3):
    anyspec = pl.BlockSpec(memory_space=pl.ANY)
    return pl.pallas_call(
        functools.partial(assemble_kernel, rows),
        in_specs=[pl.BlockSpec(memory_space=pltpu.SMEM)] + [anyspec] * 4,
        out_shape=[shape((8 * rows, D), BF)] * count,
        scratch_shapes=[pltpu.SemaphoreType.DMA((8, count))],
        compiler_params=params(6),
        name="assemble",
    )(f.reshape(1).astype(jnp.int32), own, r1, r2, r3)


def project_kernel(x0, x1, wq, wk, wv, vec, q_ref, k_ref, v_ref):
    bv = vec[B_VALUE : B_VALUE + 1, :]
    m = x0.shape[0]
    q_ref[...] = (dot(x0[...], wq[...], 1, 0) + vec[B_QUERY : B_QUERY + 1, :]).astype(BF)
    for i, x in enumerate((x0, x1)):
        rows = pl.ds(i * m, m)
        k_ref[rows, :] = dot(x[...], wk[...], 1, 0).astype(BF)
        v_ref[rows, :] = (dot(x[...], wv[...], 1, 0) + bv).astype(BF)


def project(x0, x1, wq, wk, wv, vec):
    m = x0.shape[0]
    return pl.pallas_call(
        project_kernel,
        out_shape=[pltpu.HBM((m, D), BF), pltpu.HBM((2 * m, D), BF), pltpu.HBM((2 * m, D), BF)],
        compiler_params=params(),
        cost_estimate=cost(10 * m * D * D, 20 * m * D),
        name="project",
    )(*in_hbm(x0, x1), wq, wk, wv, vec)


def project_far_kernel(z_ref, b, c, d, e, wk, wv, vec, x_ref, k_ref, v_ref, sems):
    m = b.shape[0]
    middle = (z_ref[0] == 1) | (z_ref[0] == 2)

    def copies(first, second):
        return [pltpu.make_async_copy(first, x_ref.at[pl.ds(0, m), :], sems.at[0]),
                pltpu.make_async_copy(second, x_ref.at[pl.ds(m, m), :], sems.at[1])]

    @pl.when(middle)
    def _():
        for copy in copies(b, d):
            copy.start()
        for copy in copies(b, d):
            copy.wait()

    @pl.when(jnp.logical_not(middle))
    def _():
        for copy in copies(c, e):
            copy.start()
        for copy in copies(c, e):
            copy.wait()

    bv = vec[B_VALUE : B_VALUE + 1, :]
    for i in range(2):
        rows = pl.ds(i * m, m)
        x = x_ref[rows, :]
        k_ref[rows, :] = dot(x, wk[...], 1, 0).astype(BF)
        v_ref[rows, :] = (dot(x, wv[...], 1, 0) + bv).astype(BF)


def project_far(z, b, c, d, e, wk, wv, vec):
    n = 2 * b.shape[0]
    return pl.pallas_call(
        project_far_kernel,
        grid=(1,),
        in_specs=[smem()] + [any_space()] * 4 + [whole(wk), whole(wv), whole(vec)],
        out_specs=[pl.BlockSpec((n, D), lambda i: (0, 0), pipeline_mode=pl.Buffered(1))] * 3,
        out_shape=[pltpu.HBM((n, D), BF)] * 3,
        scratch_shapes=[pltpu.SemaphoreType.DMA((2,))],
        compiler_params=params(),
        cost_estimate=cost(4 * n * D * D, 10 * n * D),
        name="project_far",
    )(z, *in_hbm(b, c, d, e), wk, wv, vec)


def project_memory_kernel(bulk, z_ref, own, out, mid, inward, w_ref, vec, x_ref, k_ref, v_ref, uk, uv, sem, sems):
    loads = bulk.copies(((AT_UK, 1), (AT_UV, 1)), w_ref, (uk, uv, sem))
    for copy in loads:
        copy.start()
    m = own.shape[0]
    middle = (z_ref[0] == 1) | (z_ref[0] == 2)
    mine = pltpu.make_async_copy(own, x_ref.at[pl.ds(0, m), :], sems.at[0])
    mine.start()

    def near():
        return [pltpu.make_async_copy(out, x_ref.at[pl.ds(m, m), :], sems.at[1]),
                pltpu.make_async_copy(mid, x_ref.at[pl.ds(2 * m, 2 * m), :], sems.at[2])]

    def far():
        return [pltpu.make_async_copy(inward, x_ref.at[pl.ds(m, 3 * m), :], sems.at[3])]

    @pl.when(middle)
    def _():
        for copy in near():
            copy.start()
        for copy in near():
            copy.wait()

    @pl.when(jnp.logical_not(middle))
    def _():
        for copy in far():
            copy.start()
        for copy in far():
            copy.wait()

    mine.wait()
    for copy in loads:
        copy.wait()
    x = x_ref[...]
    k_ref[...] = dot(x, square(uk), 1, 0).astype(BF)
    v_ref[...] = (dot(x, square(uv), 1, 0) + vec[C_VALUE : C_VALUE + 1, :]).astype(BF)


def project_memory(z, own, out, mid, inward, bulk, vec):
    n = 4 * own.shape[0]
    return pl.pallas_call(
        functools.partial(project_memory_kernel, bulk),
        grid=(1,),
        in_specs=[smem()] + [any_space()] * 5 + [whole(vec)],
        out_specs=[pl.BlockSpec((n, D), lambda i: (0, 0), pipeline_mode=pl.Buffered(1))] * 3,
        out_shape=[pltpu.HBM((n, D), BF)] * 3,
        scratch_shapes=bulk.scratch(((AT_UK, 1), (AT_UV, 1))) + [pltpu.SemaphoreType.DMA((4,))],
        compiler_params=params(),
        cost_estimate=cost(4 * n * D * D, 10 * n * D),
        name="project_memory",
    )(z, *in_hbm(own, out, mid, inward), bulk.array, vec)


def attend_kernel(block, parts, q_ref, *refs):
    o_ref, lse_ref = refs[-2:]
    lane = lax.broadcasted_iota(jnp.int32, (block, 128), 1) < HD
    k, v = refs[0][...], refs[parts][...]
    if parts > 1:
        k = jnp.concatenate([r[...] for r in refs[:parts]])
        v = jnp.concatenate([r[...] for r in refs[parts : 2 * parts]])
    items = [(i, a) for i in range(q_ref.shape[0] // block) for a in range(2)]

    def score(item):
        i, a = item
        q = q_ref[pl.ds(i * block, block), :] * BF(SCALE)
        return dot(jnp.where(lane == (a == 0), q, jnp.zeros_like(q)), k, 1, 1)

    outs = []
    s = score(items[0])
    for j in range(len(items)):
        ahead = score(items[j + 1]) if j + 1 < len(items) else None
        top = jnp.max(s, axis=1, keepdims=True)
        p = jnp.exp(s - top)
        outs.append((dot(p.astype(BF), v, 1, 0), top, jnp.sum(p, axis=1, keepdims=True)))
        s = ahead
    for i in range(q_ref.shape[0] // block):
        rows = pl.ds(i * block, block)
        o, top, count = [jnp.where(lane, x, y) for x, y in zip(outs[2 * i], outs[2 * i + 1])]
        o_ref[rows, :] = (o / count).astype(BF)
        lse = (top + jnp.log(count)).T
        for a in range(2):
            lse_ref[a, :, rows] = lse[HD * a : HD * a + 8]


def attend(q, ks, vs):
    n, kv = q.shape[0], sum(k.shape[0] for k in ks)
    pairs = D // 128

    def cols(m):
        return pl.BlockSpec((m, 128), lambda h: (0, h))

    q, *kv_arrays = in_hbm(q, *ks, *vs)
    return pl.pallas_call(
        functools.partial(attend_kernel, 256, len(ks)),
        grid=(pairs,),
        in_specs=[cols(n)] + [cols(a.shape[0]) for a in ks] * 2,
        out_specs=[cols(n), pl.BlockSpec((2, 8, n), lambda h: (h, 0, 0))],
        out_shape=[shape((n, D), BF), pltpu.HBM((2 * pairs, 8, n), F32)],
        compiler_params=params(),
        cost_estimate=cost(16 * n * kv * D, 4 * kv * D, 8 * n * kv),
        name="attend",
    )(q, *kv_arrays)


def attend_back_kernel(first, bulk, q_ref, g_ref, delta_ref, lse_ref, k_ref, v_ref, *refs):
    h = pl.program_id(0)
    *refs, dk_all, dv_all, wk_ref, wv_ref, sem = refs
    if bulk is None:
        *weights, = refs[:2]
        refs = refs[2:]
        copies = [pltpu.make_async_copy(weights[i], (wk_ref, wv_ref)[i], sem.at[i]) for i in range(2)]
    else:
        copies = bulk.copies(((AT_UK, 1), (AT_UV, 1)), refs[0], (wk_ref, wv_ref, sem))
        refs = refs[1:]

    @pl.when(h == 0)
    def _():
        for copy in copies:
            copy.start()

    if not first:
        acc_ref, *refs = refs
    p_ref, dqt_ref, dk_ref, dv_ref = refs
    n = q_ref.shape[0]
    g = g_ref[...]
    q = q_ref[...] * BF(SCALE)
    k = k_ref[...]
    v = v_ref[...]
    lane = lax.broadcasted_iota(jnp.int32, (n, 128), 1) < HD
    zero = jnp.zeros_like(q)
    dk = jnp.zeros(k.shape, F32)
    dv = jnp.zeros(k.shape, F32)
    dqs = []
    for a in range(2):
        qm = jnp.where(lane == (a == 0), q, zero)
        gm = jnp.where(lane == (a == 0), g, zero)
        p = jnp.exp(dot(k, qm, 1, 1) - lse_ref[a, 0:1, :])
        dp = dot(v, gm, 1, 1)
        ds = (p * (dp - delta_ref[a, 0:1, :])).astype(BF)
        dv = dv + dot(p.astype(BF), gm, 1, 0)
        dk = dk + dot(ds, qm, 1, 0)
        dqs.append(dot(k, ds, 0, 0))
    top_half = lax.broadcasted_iota(jnp.int32, (128, n), 0) < HD
    dqt = jnp.where(top_half, dqs[0], dqs[1])
    if not first:
        dqt = dqt + acc_ref[...]
    dqt_ref[...] = dqt
    dk = dk.astype(BF)
    dv = dv.astype(BF)
    dk_ref[...] = dk
    dv_ref[...] = dv
    for i in range(D // 128):

        @pl.when(h == i)
        def _(i=i):
            dk_all[:, i * 128 : (i + 1) * 128] = dk
            dv_all[:, i * 128 : (i + 1) * 128] = dv

    @pl.when(h == pl.num_programs(0) - 1)
    def _():
        for copy in copies:
            copy.wait()
        p_ref[...] = (dot(dk_all[...], square(wk_ref), 1, 1) + dot(dv_all[...], square(wv_ref), 1, 1)).astype(
            p_ref.dtype
        )


def attend_back(q, g, delta, lse, k, v, at, m, weights, acc, dtype):
    n = q.shape[0]
    pairs = D // 128
    bulk = weights if isinstance(weights, Bulk) else None
    weights = weights if bulk is None else (bulk.array,)

    def cols(rows, i=0):
        return pl.BlockSpec((rows, 128), lambda h: (i, h))

    by_head = pl.BlockSpec((2, 8, n), lambda h: (h, 0, 0))
    acc_spec = pl.BlockSpec((128, n), lambda h: (h, 0))
    first = acc is None
    arrays = in_hbm(q, g, delta, lse, k, v, *weights, *([] if first else [acc]))
    shapes = [pltpu.VMEM((m, D), BF)] * 2
    shapes += bulk.scratch(((AT_UK, 1), (AT_UV, 1))) if bulk else (
        [pltpu.VMEM((D, D), BF)] * 2 + [pltpu.SemaphoreType.DMA((2,))]
    )
    return pl.pallas_call(
        functools.partial(attend_back_kernel, first, bulk),
        grid=(pairs,),
        in_specs=[cols(n), cols(n), by_head, by_head, cols(m, at), cols(m, at)]
        + [any_space()] * len(weights)
        + ([] if first else [acc_spec]),
        out_specs=[pl.BlockSpec((m, D), lambda h: (0, 0)), acc_spec, cols(m), cols(m)],
        out_shape=[shape((m, D), dtype), pltpu.HBM((D, n), F32), pltpu.HBM((m, D), BF), pltpu.HBM((m, D), BF)],
        scratch_shapes=shapes,
        compiler_params=params(),
        cost_estimate=cost(44 * n * m * D, 12 * m * D, 8 * n * m),
        name="attend_back",
    )(*arrays)


def after_self_kernel(bulk, o, x, w_ref, vec, n_ref, r_ref, low_ref, cq_ref, wo, uq, sem):
    copies = bulk.copies(((AT_WO, 1), (AT_UQ, 1)), w_ref, (wo, uq, sem))
    for copy in copies:
        copy.start()

    def v(i):
        return vec[i : i + 1, :]

    copies[0].wait()
    sum_one = x[...].astype(F32) + dot(o[...], square(wo), 1, 0) + v(B_OUTPUT)
    n, r = norm(sum_one)
    low = (n * v(GAIN_A) + v(SHIFT_A)).astype(BF)
    n_ref[...] = n
    r_ref[...] = jnp.broadcast_to(r, r_ref.shape)
    low_ref[...] = low
    copies[1].wait()
    cq_ref[...] = (dot(low, square(uq), 1, 0) + v(C_QUERY)).astype(BF)


def after_self(o, x, bulk, vec):
    m = x.shape[0]
    outs = [shape((m, D), F32), shape((m, 128), F32), shape((m, D), BF), pltpu.HBM((m, D), BF)]
    return pl.pallas_call(
        functools.partial(after_self_kernel, bulk),
        grid=(1,),
        in_specs=[whole(o), whole(x), any_space(), whole(vec)],
        out_specs=[whole(s) for s in outs],
        out_shape=outs,
        scratch_shapes=bulk.scratch(((AT_WO, 1), (AT_UQ, 1))),
        compiler_params=params(),
        cost_estimate=cost(4 * m * D * D, 12 * m * D),
        name="after_self",
    )(o, x, bulk.array, vec)


GELU_C = 0.7978845608028654
GELU_A = 0.044715


FEED_WEIGHTS = ((AT_UO, 1),) + tuple((AT_EXPAND + j, 1) for j in range(4)) + ((0, 4),)


def feed_kernel(size, bulk, f_ref, ca, n1, cot, w_ref, vec,
                out_ref, two_ref, catt_ref, delta_ref, dvec_ref, *refs):
    if size == 8:
        *refs, held, sems = refs
        sums = Outbox(refs[0], held, sems)
        uo, *expand, wred_ref, sem = refs[1:]
    else:
        sums, (uo, *expand, wred_ref, sem) = refs[:-7], refs[-7:]
    copies = bulk.copies(FEED_WEIGHTS, w_ref, (uo, *expand, wred_ref, sem))
    for copy in copies:
        copy.start()

    def v(i):
        return vec[i : i + 1, :]

    copies[0].wait()
    first = n1[...] * v(GAIN_A) + v(SHIFT_A)
    sum_two = first + dot(ca[...], square(uo), 1, 0) + v(C_OUTPUT)
    n2, r2 = norm(sum_two)
    second = n2 * v(GAIN_B) + v(SHIFT_B)
    low = second.astype(BF)
    sum_three = second + v(B_REDUCE)
    acts, slopes = [], []
    for copy in copies[1:]:
        copy.wait()
    wred = square(wred_ref)
    pres = [dot(low, square(w), 1, 0) for w in expand]
    for j in range(4):
        pre = pres[j] + v(B_EXPAND + j)
        sq = pre * pre
        t = jnp.tanh(GELU_C * (pre + GELU_A * (sq * pre)))
        half = 0.5 * (1.0 + t)
        act = (pre * half).astype(BF)
        slope = half + 0.5 * pre * (1.0 - t * t) * (GELU_C * (1.0 + 3.0 * GELU_A * sq))
        acts.append(act)
        slopes.append(slope)
        sum_three = sum_three + dot(act, wred[j * D : (j + 1) * D], 1, 0)
    n3, r3 = norm(sum_three)
    out_ref[...] = (n3 * v(GAIN_C) + v(SHIFT_C)).astype(BF)
    e = cot[...].astype(F32)
    d_three = norm_back(e, v(GAIN_C), n3, r3)
    branch = d_three.astype(BF)
    dvec_ref[0:1, :] = total(branch.astype(F32))
    dvec_ref[1:2, :] = total(e * n3)
    dvec_ref[2:3, :] = total(e)
    second_grad = d_three
    d_acts = [dot(branch, wred[j * D : (j + 1) * D], 1, 1) for j in range(4)]
    for j in range(4):
        d_pre = (d_acts[j] * slopes[j]).astype(BF)
        dvec_ref[3 + j : 4 + j, :] = total(d_pre.astype(F32))
        emit(size, f_ref, sums, j, None, dot(acts[j], branch, 0, 0))
        emit(size, f_ref, sums, 4 + j, (4 + j) * D // 8, dot(low, d_pre, 0, 0))
        second_grad = second_grad + dot(d_pre, square(expand[j]), 1, 1)
    d_two = norm_back(second_grad, v(GAIN_B), n2, r2)
    two_ref[...] = d_two
    cross = d_two.astype(BF)
    dvec_ref[7:8, :] = total(second_grad * n2)
    dvec_ref[8:9, :] = total(second_grad)
    dvec_ref[9:10, :] = total(cross.astype(F32))
    emit(size, f_ref, sums, 8, D, dot(ca[...], cross, 0, 0))
    att = dot(cross, square(uo), 1, 1).astype(BF)
    catt_ref[...] = att
    delta_ref[...] = head_rows(att, ca[...])
    if size == 8:
        sums.wait()


def feed(size, f, ca, n1, cot, bulk, vec):
    m = ca.shape[0]
    outs = [
        shape((m, D), BF), shape((m, D), F32), pltpu.HBM((m, D), BF), pltpu.HBM((D // HD, 8, m), F32),
        shape((16, D), F32),
    ] + sums_out(size, 9 * D // 8, 9)
    specs = [whole(s) for s in outs]
    extra = []
    if size == 8:
        rows = 9 * D // 8
        outs[-1] = pltpu.HBM((8, rows, D), BF)
        specs[-1] = any_space()
        extra = [pltpu.VMEM((8, rows, D), BF), pltpu.SemaphoreType.DMA((9,))]
    return pl.pallas_call(
        functools.partial(feed_kernel, size, bulk),
        grid=(1,),
        in_specs=[smem(), whole(ca), whole(n1), whole(cot), any_space(), whole(vec)],
        out_specs=specs,
        out_shape=outs,
        scratch_shapes=bulk.scratch(FEED_WEIGHTS) + extra,
        compiler_params=params(44),
        cost_estimate=cost(2 * 27 * m * D * D, 24 * m * D * 4, 4 * m * D),
        name="feed",
    )(f, ca, n1, cot, bulk.array, vec)


def after_cross_back_kernel(size, bulk, f_ref, dqt, k0, k1, v0, v1, mem, low, o, two, n1, r1, w_ref, vec,
                            one_ref, att_ref, delta_ref, dvec_ref, *refs):
    sums, (uq, wo, sem) = refs[:-3], refs[-3:]
    copies = bulk.copies(((AT_UQ, 1), (AT_WO, 1)), w_ref, (uq, wo, sem))
    for copy in copies:
        copy.start()
    gain = vec[GAIN_A : GAIN_A + 1, :]
    gq = (dqt[...].T * SCALE).astype(BF)
    for copy in copies:
        copy.wait()
    first_grad = two[...] + dot(gq, square(uq), 1, 1)
    n = n1[...]
    d_one = norm_back(first_grad, gain, n, r1[:, 0:1])
    one_ref[...] = d_one
    low_one = d_one.astype(BF)
    att = dot(low_one, square(wo), 1, 1).astype(BF)
    att_ref[...] = att
    delta_ref[...] = head_rows(att, o[...])
    m = k0.shape[0]
    dvec_ref[0:1, :] = total(gq.astype(F32))
    dvec_ref[1:2, :] = total(first_grad * n)
    dvec_ref[2:3, :] = total(first_grad)
    dvec_ref[3:4, :] = total(low_one.astype(F32))
    dvec_ref[4:5, :] = total(v0[...].astype(F32)) + total(v1[...].astype(F32))
    r = D // 8
    emit(size, f_ref, sums, 0, 0, dot(low[...], gq, 0, 0))
    emit(size, f_ref, sums, 1, r, dot(mem[0:m, :], k0[...], 0, 0) + dot(mem[m:, :], k1[...], 0, 0))
    emit(size, f_ref, sums, 2, 2 * r, dot(mem[0:m, :], v0[...], 0, 0) + dot(mem[m:, :], v1[...], 0, 0))
    emit(size, f_ref, sums, 3, 3 * r, dot(o[...], low_one, 0, 0))


def after_cross_back(size, f, dqt, ks, vs, mem, low, o, two, n1, r1, bulk, vec):
    m = low.shape[0]
    arrays = in_hbm(dqt, *ks, *vs, mem) + [low, o, two, n1, r1]
    outs = [shape((m, D), F32), pltpu.HBM((m, D), BF), pltpu.HBM((D // HD, 8, m), F32), shape((8, D), F32)]
    outs += sums_out(size, 4 * D // 8, 4, True)
    return pl.pallas_call(
        functools.partial(after_cross_back_kernel, size, bulk),
        grid=(1,),
        in_specs=[smem()] + [whole(a) for a in arrays] + [any_space(), whole(vec)],
        out_specs=[whole(s) for s in outs],
        out_shape=outs,
        scratch_shapes=bulk.scratch(((AT_UQ, 1), (AT_WO, 1))),
        compiler_params=params(24),
        cost_estimate=cost(2 * 8 * m * D * D, 14 * m * D * 4),
        name="after_cross_back",
    )(f, *arrays, bulk.array, vec)


def last_kernel(size, count, f_ref, dqt, *refs):
    ks, vs = refs[:count], refs[count : 2 * count]
    x0, x1, x_far, feed, mid, gq_ref = refs[2 * count : 2 * count + 6]
    *sums, table = refs[2 * count + 6 :]
    m = x0.shape[0]
    xs = [x0[...], x1[...], x_far[0:m, :], x_far[m:, :]]
    gq = (dqt[...].T * SCALE).astype(BF)
    gq_ref[...] = gq
    r = D // 8
    emit(size, f_ref, sums, 0, 0, dot(xs[0], gq, 0, 0))
    for i, parts in ((1, ks), (2, vs)):
        acc = dot(xs[0], parts[0][...], 0, 0)
        for x, p in zip(xs[1:], parts[1:]):
            acc = acc + dot(x, p[...], 0, 0)
        emit(size, f_ref, sums, i, i * r, acc)
    table[...] = jnp.zeros_like(table)
    table[B_QUERY : B_QUERY + 1, :] = total(gq.astype(F32))
    dbv = total(vs[0][...].astype(F32))
    for v in vs[1:]:
        dbv = dbv + total(v[...].astype(F32))
    table[B_VALUE : B_VALUE + 1, :] = dbv
    for at, src, i in (
        (B_OUTPUT, mid, 3), (GAIN_A, mid, 1), (SHIFT_A, mid, 2), (C_QUERY, mid, 0), (C_VALUE, mid, 4),
        (C_OUTPUT, feed, 9), (GAIN_B, feed, 7), (SHIFT_B, feed, 8),
        (B_REDUCE, feed, 0), (GAIN_C, feed, 1), (SHIFT_C, feed, 2),
    ):
        table[at : at + 1, :] = src[i : i + 1, :]
    if size != 8:
        table[B_EXPAND : B_EXPAND + 4, :] = feed[3:7, :]
        return
    rows = table[0:16, :].astype(BF)
    for chip in range(4):
        wide = jnp.broadcast_to(feed[3 + chip : 4 + chip, :], (16, D)).astype(BF)
        for s in sums:
            s[chip, 3 * r : 3 * r + 16, :] = jnp.zeros((16, D), BF)
            s[chip, 3 * r : 3 * r + 16, 0:128] = rows[:, chip * 128 : (chip + 1) * 128]
            s[chip, 3 * r + 16 : 3 * r + 32, :] = wide


def last(size, f, dqt, ks, vs, xs, feed, mid):
    m = xs[0].shape[0]
    count = len(ks)
    arrays = [f, *in_hbm(dqt, *ks, *vs, *xs), feed, mid]
    outs = [shape((m, D), BF)] + sums_out(size, 3 * D // 8 + 32, 3, True) + [shape((VEC_ROWS, D), F32)]
    return pl.pallas_call(
        functools.partial(last_kernel, size, count),
        grid=(1,),
        in_specs=[smem()] + [whole(a) for a in arrays[1:]],
        out_specs=[whole(s) for s in outs],
        out_shape=outs,
        compiler_params=params(),
        cost_estimate=cost(2 * 9 * m * D * D, 14 * m * D * 2),
        name="last",
    )(*arrays)


def own_rows_kernel(gq, part, one, wq, out):
    out[...] = part[...] + one[...] + dot(gq[...], wq[...], 1, 1)


def own_rows(gq, part, one, wq):
    return pl.pallas_call(
        own_rows_kernel,
        out_shape=shape(part.shape, F32),
        compiler_params=params(),
        cost_estimate=cost(2 * part.shape[0] * D * D, 4 * part.shape[0] * D * 4),
        name="own_rows",
    )(gq, part, one, wq)


def fold_kernel(t_ref, *refs):
    acc = refs[0][...].astype(F32)
    for r in refs[1:-1]:
        acc = acc + r[...].astype(F32)
    refs[-1][...] = acc.astype(BF)


def fold(table, base, count, arrays):
    n = arrays[0].shape[1]
    width = len(arrays)

    def spec(k):
        return pl.BlockSpec((1, n, D), lambda j, t: (t[base + j * width + k], 0, 0))

    return pl.pallas_call(
        fold_kernel,
        grid_spec=pltpu.PrefetchScalarGridSpec(
            num_scalar_prefetch=1,
            grid=(count,),
            in_specs=[spec(k) for k in range(width)],
            out_specs=pl.BlockSpec((1, n, D), lambda j, t: (j, 0, 0)),
        ),
        out_shape=shape((count, n, D), BF),
        compiler_params=params(6),
        name="fold",
    )(table, *arrays)


def start_rows(arrays, out, sems):
    copies = []
    at = 0
    for ref in arrays:
        rows = ref.shape[0]
        for j in range(ref.shape[1] // D):
            copies.append(pltpu.make_async_copy(
                ref.at[:, pl.ds(j * D, D)], out.at[pl.ds(at, rows), :], sems.at[len(copies)]
            ))
            copies[-1].start()
            at += rows
    return copies


def pack_kernel(*refs):
    *arrays, out, sems = refs
    for copy in start_rows(arrays, out, sems):
        copy.wait()


def pack_plain(arrays):
    return jnp.concatenate([a[:, i : i + D] for a in arrays for i in range(0, a.shape[1], D)])


def pack_rows(arrays):
    if arrays[0].shape[0] % 16:
        return pack_plain(arrays)
    pieces = sum(a.shape[1] // D for a in arrays)
    rows = sum(a.shape[0] * a.shape[1] // D for a in arrays)
    return pl.pallas_call(
        pack_kernel,
        in_specs=[any_space()] * len(arrays),
        out_shape=shape((rows, D), BF),
        scratch_shapes=[pltpu.SemaphoreType.DMA((pieces,))],
        compiler_params=params(4),
        name="pack_rows",
    )(*in_hbm(*arrays))


def table_kernel(rows, count, *refs):
    arrays, refs = refs[:count], refs[count:]
    *vectors, expand, out, table, short, long, sems, vec_sems = refs
    copies = start_rows(arrays, out, sems)
    loads = [pltpu.make_async_copy(ref, short.at[i], vec_sems.at[i]) for i, ref in enumerate(vectors)]
    loads.append(pltpu.make_async_copy(expand, long, vec_sems.at[len(vectors)]))
    for load in loads:
        load.start()
    table[...] = jnp.zeros_like(table)
    for load in loads:
        load.wait()
    for i in range(len(vectors)):
        table[i : i + 1, 0:rows] = short[i].astype(F32)
    for j in range(4):
        table[B_EXPAND + j : B_EXPAND + j + 1, 0:rows] = long[:, j * rows : (j + 1) * rows].astype(F32)
    out[len(copies) * rows :, :] = table[...].astype(BF)
    for copy in copies:
        copy.wait()


def pack_first(arrays, vectors, expand):
    rows = vectors[0].shape[0]
    plain = rows % 16 != 0
    used = [] if plain else arrays
    vectors = [v.reshape(1, -1) for v in vectors]
    out = pl.pallas_call(
        functools.partial(table_kernel, rows, len(used)),
        in_specs=[any_space()] * (len(used) + len(vectors) + 1),
        out_shape=shape((len(used) * rows + VEC_ROWS, D), BF),
        scratch_shapes=[
            pltpu.VMEM((VEC_ROWS, D), F32), pltpu.VMEM((len(vectors), 1, rows), BF),
            pltpu.VMEM((1, 4 * rows), BF), pltpu.SemaphoreType.DMA((len(arrays),)),
            pltpu.SemaphoreType.DMA((len(vectors) + 1,)),
        ],
        compiler_params=params(4),
        name="pack_first",
    )(*in_hbm(*used, *vectors, expand.reshape(1, -1)))
    return pack_plain([*arrays, out]) if plain else out


ENDS_IN = ((1, 0), (2, 3))
ENDS_OUT = ((0, 1), (3, 2))
MIDDLE = ((1, 2), (2, 1))
PAIRS = ((0, 1), (1, 0), (2, 3), (3, 2))
ACROSS = ((0, 2), (2, 0), (1, 3), (3, 1))


def over_seq(x, pairs):
    return lax.ppermute(x, "seq", pairs)


def after(x, *deps):
    return lax.optimization_barrier((x,) + deps)[0]


def add(p, r):
    return (p.astype(F32) + r.astype(F32)).astype(BF)


def swap_core():
    return [(i, i ^ 1) for i in range(8)]


def swap_first():
    return [(i, i ^ (4 if i & 1 else 2)) for i in range(8)]


def swap_second():
    return [(i, i ^ (2 if i & 1 else 4)) for i in range(8)]


def gather_plane(own, deps, late):
    r1 = lax.ppermute(own, "fsdp", swap_first())
    both = after(jnp.concatenate([own, r1]), *deps)
    r2 = lax.ppermute(both, "fsdp", swap_second())
    r3 = lax.ppermute(after(jnp.concatenate([both, r2]), *late), "fsdp", swap_core())
    return r1, r2, r3


def fold_table(f):
    c = lax.rem(f, 2)
    x = lax.rem(f // 2, 2)
    y = f // 4
    even = c == 0
    send0 = jnp.where(even, 1 - x, 2 * (1 - y))
    send1 = jnp.where(even, 3 - x, 3 - 2 * y)
    keep0 = jnp.where(even, x, 2 * y)
    keep1 = jnp.where(even, 2 + x, 2 * y + 1)
    own = jnp.where(even, y, x)
    mine = jnp.where(own == 0, keep0, keep1)
    other = jnp.where(own == 0, keep1, keep0)
    zero = 0 * own
    return jnp.stack([send0, send0, send1, send1, other, other, 1 - own, mine, mine, own, zero]).astype(jnp.int32)


class PlaneReduce:
    def __init__(self, table, sums):
        self.table = table
        self.keep = sums[1]
        self.got = [lax.ppermute(sums[0], "fsdp", swap_core())]

    def second(self, *deps):
        out = fold(self.table, 0, 2, [after(self.keep, *deps), self.got[0]])
        self.got.append(lax.ppermute(out, "fsdp", swap_first()))

    def third(self, *deps):
        out = fold(self.table, 4, 1, [after(self.keep, *deps)] + self.got)
        self.got.append(lax.ppermute(out, "fsdp", swap_second()))

    def end(self, *deps):
        return fold(self.table, 7, 1, [after(self.keep, *deps)] + self.got)[0]


class PlainReduce:
    def __init__(self, table, sums):
        self.got = [lax.psum_scatter(sums, "fsdp", scatter_dimension=0, tiled=False)]

    def second(self, *deps):
        pass

    third = second

    def end(self, *deps):
        return self.got[0]


def on_device(size, tokens, memory, cotangent,
              w_query, w_key, w_value, w_output, b_query, b_value, b_output, gain_attend, shift_attend,
              u_query, u_key, u_value, u_output, c_query, c_value, c_output, gain_cross, shift_cross,
              w_expand, b_expand, w_reduce, b_reduce, gain_feed, shift_feed):
    rows = w_query.shape[0]
    f = lax.axis_index("fsdp")
    x = tokens[0]
    mem = memory[0]

    vectors = (b_query, b_value, b_output, gain_attend, shift_attend, c_query, c_value, c_output,
               gain_cross, shift_cross, b_reduce, gain_feed, shift_feed)
    first = pack_first([w_query, w_key, w_value], vectors, b_expand)
    pack = pack_rows([w_reduce, w_expand, w_output, u_query, u_key, u_value, u_output])
    c1 = over_seq(x, PAIRS)
    x_b = over_seq(x, MIDDLE)
    x_d = over_seq(c1, MIDDLE)
    x_c = over_seq(x_b, ENDS_IN)
    mem_out = over_seq(after(mem, c1, x_b), ENDS_OUT)
    if size == 8:
        r1, r2, r3 = gather_plane(first, (c1, x_b), (x_d, x_c, mem_out))
        wq, wk, wv = assemble(f, rows, 3, first, r1, r2, r3)
        n = first.shape[0]
        tables = [first, r1, r2[:n], r2[n:]] + [r3[i * n : (i + 1) * n] for i in range(4)]
        tables = jnp.stack([t[3 * rows : 3 * rows + N_VEC, :rows] for t in tables])
        c = lax.rem(f, 2)
        a, b = 2 + 2 * c, 4 - 2 * c
        offsets = jnp.stack([0 * c, a, b, 6 + 0 * c, 1 + 0 * c, b + 1, a + 1, 7 + 0 * c])
        pick = (jnp.arange(8)[:, None] == (offsets ^ f)[None, :]).astype(BF)
        tables = jnp.einsum("gd,dkl->gkl", pick, tables, preferred_element_type=F32)
    else:
        g = lax.all_gather(first, "fsdp", axis=0, tiled=False)
        wq, wk, wv = [g[:, i * rows : (i + 1) * rows].reshape(D, D) for i in range(3)]
        tables = g[:, 3 * rows : 3 * rows + N_VEC, :rows].astype(F32)
    vec = jnp.concatenate(
        [tables[:, :B_EXPAND].transpose(1, 0, 2).reshape(B_EXPAND, D), tables[:, B_EXPAND:].reshape(4, D)]
    )
    vec = jnp.pad(vec, ((0, VEC_ROWS - N_VEC), (0, 0)))

    everything = lax.all_gather(pack, "fsdp", axis=0, tiled=False)

    if size != 8:
        blocks = [everything[:, : 4 * rows].reshape(4, D, D)]
        for i in range(4, 13):
            blocks.append(everything[:, i * rows : (i + 1) * rows].reshape(1, D, D))
        everything = jnp.concatenate(blocks)
    bulk = Bulk(everything, size)

    def by_owner(stack, count):
        s = stack.reshape(count, size, rows, D)
        return s.transpose(1, 0, 2, 3).reshape(size, count * rows, D)

    def reduce(sums, tall, count, extra=None):
        if size == 8 and len(sums) == 2:
            return PlaneReduce(table, sums)
        if size == 8:
            return PlainReduce(table, sums[0])
        s = sums[0]
        blocks = [s[: 4 * D].reshape(size, 4 * rows, D), s[4 * D :]] if tall else [s]
        blocks[-1] = by_owner(blocks[-1], count)
        return PlainReduce(table, jnp.concatenate(blocks + ([] if extra is None else [extra]), 1))

    table = fold_table(f)
    f1 = f.reshape(1).astype(jnp.int32)
    z1 = lax.axis_index("seq").reshape(1).astype(jnp.int32)
    q, k0, v0 = project(x, c1, wq, wk, wv, vec)
    x_e = over_seq(x_d, ENDS_IN)
    mem_mid = over_seq(after(jnp.concatenate([mem, mem_out]), x_d), MIDDLE)
    x_far, k1, v1 = project_far(z1, x_b, x_c, x_d, after(x_e, k0), wk, wv, vec)
    mem_in = over_seq(jnp.concatenate([mem, after(mem_mid, x_far)]), ENDS_IN)
    o, lse = attend(q, [k0, k1], [v0, v1])
    n1, r_one, low, cq = after_self(o, x, bulk, vec)
    mem_x, mk, mv = project_memory(z1, mem, mem_out, mem_mid, after(mem_in, low), bulk, vec)
    ca, cross_lse = attend(cq, [mk], [mv])
    layer_out, d_two, d_catt, cross_delta, dvec_feed, *sums = feed(
        size, f1, ca, n1, cotangent[0], bulk, vec
    )
    feed_sum = reduce(sums, True, 5)

    m = 2 * mem.shape[0]
    def cross_back(g, i, acc, dtype):
        return attend_back(cq, g, cross_delta, cross_lse, mk, mv, i, m, bulk, acc, dtype)

    far, dqt, dk1, dv1 = cross_back(d_catt, 1, None, BF)
    far_in = over_seq(far, ENDS_OUT)
    near, dqt, dk0, dv0 = cross_back(after(d_catt, far), 0, dqt, F32)
    d_one, d_att, self_delta, dvec_mid, *sums = after_cross_back(
        size, f1, after(dqt, far_in), (dk0, dk1), (dv0, dv1), mem_x, low, o, d_two, n1, r_one, bulk, vec
    )
    mid_sum = reduce(sums, False, 4)
    far_mid = over_seq(after(add(far, far_in), d_att), MIDDLE)
    m = x.shape[0]

    def self_back(g, i, acc, dtype):
        k, v = ((k0, v0), (k1, v1))[i // 2]
        return attend_back(q, g, self_delta, lse, k, v, i % 2, m, (wk, wv), acc, dtype)

    p3, dqt, dk3, dv3 = self_back(d_att, 3, None, BF)
    e = over_seq(p3, ENDS_OUT)
    mid_sum.second(p3)
    half = m // 2
    p2, dqt, dk2, dv2 = self_back(after(d_att, p3, feed_sum.got[0], mid_sum.got[0]), 2, dqt, BF)
    feed_part = feed_sum.end()
    sum_feed = lax.psum(feed_part, "seq")
    cc = over_seq(p2, ENDS_OUT)
    mid_sum.third(p2)
    p1, dqt, dk1, dv1 = self_back(after(d_att, e, far_mid, p2, mid_sum.got[-2 if size == 8 else 0]), 1, dqt, BF)
    near_in = over_seq(after(add(near[half:], far_mid[half:]), p1), PAIRS)
    d = over_seq(after(add(p3, e), p1), MIDDLE)
    mid_part = mid_sum.end(p1)
    mid_in = over_seq(mid_part, PAIRS)
    p0, dqt, dk0, dv0 = self_back(after(d_att, cc, p1, mid_part), 0, dqt, F32)
    b = over_seq(after(add(p2, cc), p0), MIDDLE)
    mid_part = add(mid_part, after(mid_in, p0))
    dqt = after(dqt, d, mid_part, sum_feed)
    mid_in = over_seq(mid_part, ACROSS)
    gq, *sums, vec_table = last(
        size, f1, dqt, (dk0, dk1, dk2, dk3), (dv0, dv1, dv2, dv3), (x, c1, x_far), dvec_feed, dvec_mid
    )
    extra = None
    if size != 8:
        extra = jnp.concatenate([
            vec_table[:B_EXPAND].reshape(B_EXPAND, size, rows).transpose(1, 0, 2),
            vec_table[B_EXPAND:N_VEC].reshape(size, 4, rows),
        ], 1)
        extra = jnp.pad(extra, ((0, 0), (0, VEC_ROWS - N_VEC), (0, D - rows))).astype(BF)
    late_sum = reduce(sums, False, 3, extra)
    tok_mine = own_rows(gq, p0, d_one, wq)
    a = over_seq(after(add(p1, d), gq), PAIRS)
    late_sum.second()
    late_sum.third()
    late = late_sum.end()
    late_end = late
    got = over_seq(late, PAIRS)
    late = add(late, got)
    got = over_seq(late, ACROSS)
    sum_last = late.astype(F32) + got.astype(F32)
    sum_feed = sum_feed.astype(F32)
    sum_mid = mid_part.astype(F32) + mid_in.astype(F32)
    grad_tok = after(tok_mine, late_end) + a.astype(F32) + b.astype(F32)
    grad_mem = after(near[:half], late_end) + near_in.astype(F32) + far_mid[:half].astype(F32)
    sum_feed = after(sum_feed, late_end)

    if size == 8:
        c = lax.rem(f, 2)
        vecs = lax.dynamic_slice(sum_last, (3 * rows, c * rows), (B_EXPAND, rows))
        db_expand = lax.dynamic_slice(sum_last, (3 * rows + 16, c * 4 * rows), (1, 4 * rows)).reshape(4 * rows)
    else:
        vecs = sum_last[3 * rows : 3 * rows + N_VEC, :rows]
        db_expand = vecs[B_EXPAND:].reshape(4 * rows)
    dw_reduce = sum_feed[: 4 * rows]
    dw_expand = jnp.concatenate([sum_feed[(4 + j) * rows : (5 + j) * rows] for j in range(4)], 1)
    du_output = sum_feed[8 * rows :]
    du_query, du_key, du_value, dw_output = [sum_mid[i * rows : (i + 1) * rows] for i in range(4)]
    dw_query, dw_key, dw_value = [sum_last[i * rows : (i + 1) * rows] for i in range(3)]
    return (
        layer_out[None], grad_tok[None], grad_mem[None],
        dw_query, dw_key, dw_value, dw_output, vecs[0], vecs[1], vecs[2], vecs[3], vecs[4],
        du_query, du_key, du_value, du_output, vecs[5], vecs[6], vecs[7], vecs[8], vecs[9],
        dw_expand, db_expand, dw_reduce, vecs[10], vecs[11], vecs[12],
    )


def solution(mesh):
    rows = P("fsdp", "seq", None)
    mat, vec = P("fsdp", None), P("fsdp")
    weights = (mat,) * 4 + (vec,) * 5 + (mat,) * 4 + (vec,) * 5 + (mat, vec, mat, vec, vec, vec)
    return jax.shard_map(
        functools.partial(on_device, mesh.shape["fsdp"]),
        mesh=mesh,
        in_specs=(rows,) * 3 + weights,
        out_specs=(rows,) * 3 + weights,
        check_vma=False,
    )
```

```python
import functools

import jax
import jax.numpy as jnp
from jax import lax
from jax.experimental import pallas as pl
from jax.experimental.pallas import tpu as pltpu
from jax.sharding import PartitionSpec as P

HD = 64
D = 512
EPS = 1e-05
SCALE = HD ** (-0.5)
BF = jnp.bfloat16
F32 = jnp.float32

B_QUERY, B_VALUE, B_OUTPUT, GAIN_A, SHIFT_A = 0, 1, 2, 3, 4
C_QUERY, C_VALUE, C_OUTPUT, GAIN_B, SHIFT_B = 5, 6, 7, 8, 9
B_REDUCE, GAIN_C, SHIFT_C, B_EXPAND = 10, 11, 12, 13
N_VEC = 17
VEC_ROWS = 32

AT_EXPAND, AT_WO, AT_UQ, AT_UK, AT_UV, AT_UO = 4, 8, 9, 10, 11, 12


def dot(a, b, ca, cb):
    return lax.dot_general(a, b, (((ca,), (cb,)), ((), ())), preferred_element_type=F32)


def params(mib=14):
    return pltpu.CompilerParams(vmem_limit_bytes=mib << 20)


def cost(flops, nbytes, trans=0):
    return pl.CostEstimate(flops=flops // 100, bytes_accessed=nbytes // 100, transcendentals=0)


def shape(dims, dtype):
    return jax.ShapeDtypeStruct(dims, dtype)


def whole(x):
    nd = len(x.shape)
    return pl.BlockSpec(x.shape, lambda i: (0,) * nd, pipeline_mode=pl.Buffered(1))


def norm(hidden):
    centre = jnp.mean(hidden, axis=-1, keepdims=True)
    offset = hidden - centre
    spread = jnp.mean(offset * offset, axis=-1, keepdims=True)
    r = lax.rsqrt(spread + EPS)
    return offset * r, r


def norm_back(e, gain, n, r):
    t = e * gain
    return r * (t - jnp.mean(t, axis=-1, keepdims=True) - n * jnp.mean(t * n, axis=-1, keepdims=True))


def total(x):
    return jnp.sum(x, axis=0, keepdims=True)


def square(ref):
    return ref[...].reshape(-1, ref.shape[-1])


def smem():
    return pl.BlockSpec(memory_space=pltpu.SMEM)


def any_space():
    return pl.BlockSpec(memory_space=pltpu.HBM)


def in_hbm(*arrays):
    return [pltpu.with_memory_space_constraint(a, pltpu.HBM) for a in arrays]


class Bulk:
    def __init__(self, array, size):
        self.array = in_hbm(array)[0]
        self.by_owner = size == 8

    def scratch(self, wanted):
        shapes = []
        for count in (c for _, c in wanted):
            shapes.append(pltpu.VMEM((8, count * D // 8, D) if self.by_owner else (count, D, D), BF))
        return shapes + [pltpu.SemaphoreType.DMA((len(wanted),))]

    def copies(self, wanted, ref, scratch):
        out = []
        for i, (at, count) in enumerate(wanted):
            if self.by_owner:
                src = ref.at[:, pl.ds(at * D // 8, count * D // 8), :]
            else:
                src = ref.at[pl.ds(at, count)]
            out.append(pltpu.make_async_copy(src, scratch[i], scratch[-1].at[i]))
        return out


def sums_out(size, rows, count, late=False):
    if size == 8 and late:
        return [shape((4, rows, D), BF)] * 2
    if size == 8:
        return [shape((8, rows, D), BF)]
    return [shape((count * D, D), BF)]


class Outbox:
    def __init__(self, out, held, sems):
        self.out, self.held, self.sems = out, held, sems
        self.copies = []

    def send(self, block, at, value):
        v = value.astype(BF)
        if at is None:
            part = (pl.ds(2 * block, 2), pl.ds(0, D // 2))
            v = v.reshape(2, D // 2, D)
        else:
            part = (pl.ds(0, 8), pl.ds(at, D // 8))
            v = v.reshape(8, D // 8, D)
        self.held[part[0], part[1], :] = v
        copy = pltpu.make_async_copy(
            self.held.at[part[0], part[1]], self.out.at[part[0], part[1]], self.sems.at[len(self.copies)]
        )
        copy.start()
        self.copies.append(copy)

    def wait(self):
        for copy in self.copies:
            copy.wait()


def emit(size, f_ref, outs, block, at, value):
    if isinstance(outs, Outbox):
        outs.send(block, at, value)
        return
    value = value.astype(BF)
    if size != 8:
        outs[0][block * D : (block + 1) * D, :] = value
        return
    if len(outs) == 1:
        if at is None:
            outs[0][2 * block : 2 * block + 2, 0 : D // 2, :] = value.reshape(2, D // 2, D)
        else:
            outs[0][:, at : at + D // 8, :] = value.reshape(8, D // 8, D)
        return
    even = lax.rem(f_ref[0], 2) == 0
    if at is None:
        v = value.reshape(2, D // 2, D)
        outs[0][block, 0 : D // 2, :] = jnp.where(even, v[1], v[0])
        outs[1][block, 0 : D // 2, :] = jnp.where(even, v[0], v[1])
    else:
        v = value.reshape(4, 2, D // 8, D)
        outs[0][:, at : at + D // 8, :] = jnp.where(even, v[:, 1], v[:, 0])
        outs[1][:, at : at + D // 8, :] = jnp.where(even, v[:, 0], v[:, 1])


def head_rows(g, o):
    n = g.shape[0]
    t = (g.astype(F32) * o.astype(F32)).T
    s = jnp.sum(t.reshape(D // HD, HD, n), axis=1, keepdims=True)
    return jnp.broadcast_to(s, (D // HD, 8, n))


def assemble_kernel(rows, f_ref, own, r1, r2, r3, *rest):
    outs, sems = rest[:-1], rest[-1]
    f = f_ref[0]
    c = lax.rem(f, 2)
    a = 2 + 2 * c
    b = 4 - 2 * c
    n = own.shape[0]
    pieces = (
        (own, 0, 0), (r1, 0, a), (r2, 0, b), (r2, n, 6),
        (r3, 0, 1), (r3, n, b + 1), (r3, 2 * n, a + 1), (r3, 3 * n, 7),
    )
    copies = []
    for j, (src, base, off) in enumerate(pieces):
        at = pl.multiple_of(jnp.bitwise_xor(f, off) * rows, rows)
        for k, out in enumerate(outs):
            copy = pltpu.make_async_copy(
                src.at[pl.ds(base + k * rows, rows), :], out.at[pl.ds(at, rows), :], sems.at[j, k]
            )
            copy.start()
            copies.append(copy)
    for copy in copies:
        copy.wait()


def assemble(f, rows, count, own, r1, r2, r3):
    anyspec = pl.BlockSpec(memory_space=pl.ANY)
    return pl.pallas_call(
        functools.partial(assemble_kernel, rows),
        in_specs=[pl.BlockSpec(memory_space=pltpu.SMEM)] + [anyspec] * 4,
        out_shape=[shape((8 * rows, D), BF)] * count,
        scratch_shapes=[pltpu.SemaphoreType.DMA((8, count))],
        compiler_params=params(6),
        name="assemble",
    )(f.reshape(1).astype(jnp.int32), own, r1, r2, r3)


def project_kernel(x0, x1, wq, wk, wv, vec, q_ref, k_ref, v_ref):
    bv = vec[B_VALUE : B_VALUE + 1, :]
    m = x0.shape[0]
    q_ref[...] = (dot(x0[...], wq[...], 1, 0) + vec[B_QUERY : B_QUERY + 1, :]).astype(BF)
    for i, x in enumerate((x0, x1)):
        rows = pl.ds(i * m, m)
        k_ref[rows, :] = dot(x[...], wk[...], 1, 0).astype(BF)
        v_ref[rows, :] = (dot(x[...], wv[...], 1, 0) + bv).astype(BF)


def project(x0, x1, wq, wk, wv, vec):
    m = x0.shape[0]
    return pl.pallas_call(
        project_kernel,
        out_shape=[pltpu.HBM((m, D), BF), pltpu.HBM((2 * m, D), BF), pltpu.HBM((2 * m, D), BF)],
        compiler_params=params(),
        cost_estimate=cost(10 * m * D * D, 20 * m * D),
        name="project",
    )(*in_hbm(x0, x1), wq, wk, wv, vec)


def project_far_kernel(z_ref, b, c, d, e, wk, wv, vec, x_ref, k_ref, v_ref, sems):
    m = b.shape[0]
    middle = (z_ref[0] == 1) | (z_ref[0] == 2)

    def copies(first, second):
        return [pltpu.make_async_copy(first, x_ref.at[pl.ds(0, m), :], sems.at[0]),
                pltpu.make_async_copy(second, x_ref.at[pl.ds(m, m), :], sems.at[1])]

    @pl.when(middle)
    def _():
        for copy in copies(b, d):
            copy.start()
        for copy in copies(b, d):
            copy.wait()

    @pl.when(jnp.logical_not(middle))
    def _():
        for copy in copies(c, e):
            copy.start()
        for copy in copies(c, e):
            copy.wait()

    bv = vec[B_VALUE : B_VALUE + 1, :]
    for i in range(2):
        rows = pl.ds(i * m, m)
        x = x_ref[rows, :]
        k_ref[rows, :] = dot(x, wk[...], 1, 0).astype(BF)
        v_ref[rows, :] = (dot(x, wv[...], 1, 0) + bv).astype(BF)


def project_far(z, b, c, d, e, wk, wv, vec):
    n = 2 * b.shape[0]
    return pl.pallas_call(
        project_far_kernel,
        grid=(1,),
        in_specs=[smem()] + [any_space()] * 4 + [whole(wk), whole(wv), whole(vec)],
        out_specs=[pl.BlockSpec((n, D), lambda i: (0, 0), pipeline_mode=pl.Buffered(1))] * 3,
        out_shape=[pltpu.HBM((n, D), BF)] * 3,
        scratch_shapes=[pltpu.SemaphoreType.DMA((2,))],
        compiler_params=params(),
        cost_estimate=cost(4 * n * D * D, 10 * n * D),
        name="project_far",
    )(z, *in_hbm(b, c, d, e), wk, wv, vec)


def project_memory_kernel(bulk, z_ref, own, near, mid, inward, w_ref, vec, x_ref, k_ref, v_ref, uk, uv, sem, sems):
    loads = bulk.copies(((AT_UK, 1), (AT_UV, 1)), w_ref, (uk, uv, sem))
    for copy in loads:
        copy.start()
    m = own.shape[0]
    middle = (z_ref[0] == 1) | (z_ref[0] == 2)
    mine = pltpu.make_async_copy(own, x_ref.at[pl.ds(0, m), :], sems.at[0])
    mine.start()
    next_to = pltpu.make_async_copy(near, x_ref.at[pl.ds(m, m), :], sems.at[1])
    next_to.start()
    rest = x_ref.at[pl.ds(2 * m, 2 * m), :]

    @pl.when(middle)
    def _():
        copy = pltpu.make_async_copy(mid, rest, sems.at[2])
        copy.start()
        copy.wait()

    @pl.when(jnp.logical_not(middle))
    def _():
        copy = pltpu.make_async_copy(inward, rest, sems.at[3])
        copy.start()
        copy.wait()

    next_to.wait()
    mine.wait()
    for copy in loads:
        copy.wait()
    x = x_ref[...]
    k_ref[...] = dot(x, square(uk), 1, 0).astype(BF)
    v_ref[...] = (dot(x, square(uv), 1, 0) + vec[C_VALUE : C_VALUE + 1, :]).astype(BF)


def project_memory(z, own, near, mid, inward, bulk, vec):
    n = 4 * own.shape[0]
    return pl.pallas_call(
        functools.partial(project_memory_kernel, bulk),
        grid=(1,),
        in_specs=[smem()] + [any_space()] * 5 + [whole(vec)],
        out_specs=[pl.BlockSpec((n, D), lambda i: (0, 0), pipeline_mode=pl.Buffered(1))] * 3,
        out_shape=[pltpu.HBM((n, D), BF)] * 3,
        scratch_shapes=bulk.scratch(((AT_UK, 1), (AT_UV, 1))) + [pltpu.SemaphoreType.DMA((4,))],
        compiler_params=params(),
        cost_estimate=cost(4 * n * D * D, 10 * n * D),
        name="project_memory",
    )(z, *in_hbm(own, near, mid, inward), bulk.array, vec)


def attend_kernel(block, parts, q_ref, *refs):
    o_ref, lse_ref = refs[-2:]
    lane = lax.broadcasted_iota(jnp.int32, (block, 128), 1) < HD
    k, v = refs[0][...], refs[parts][...]
    if parts > 1:
        k = jnp.concatenate([r[...] for r in refs[:parts]])
        v = jnp.concatenate([r[...] for r in refs[parts : 2 * parts]])
    items = [(i, a) for i in range(q_ref.shape[0] // block) for a in range(2)]

    def score(item):
        i, a = item
        q = q_ref[pl.ds(i * block, block), :] * BF(SCALE)
        return dot(jnp.where(lane == (a == 0), q, jnp.zeros_like(q)), k, 1, 1)

    outs = []
    s = score(items[0])
    for j in range(len(items)):
        ahead = score(items[j + 1]) if j + 1 < len(items) else None
        top = jnp.max(s, axis=1, keepdims=True)
        p = jnp.exp(s - top)
        outs.append((dot(p.astype(BF), v, 1, 0), top, jnp.sum(p, axis=1, keepdims=True)))
        s = ahead
    for i in range(q_ref.shape[0] // block):
        rows = pl.ds(i * block, block)
        o, top, count = [jnp.where(lane, x, y) for x, y in zip(outs[2 * i], outs[2 * i + 1])]
        o_ref[rows, :] = (o / count).astype(BF)
        lse = (top + jnp.log(count)).T
        for a in range(2):
            lse_ref[a, :, rows] = lse[HD * a : HD * a + 8]


def attend(q, ks, vs):
    n, kv = q.shape[0], sum(k.shape[0] for k in ks)
    pairs = D // 128

    def cols(m):
        return pl.BlockSpec((m, 128), lambda h: (0, h))

    q, *kv_arrays = in_hbm(q, *ks, *vs)
    return pl.pallas_call(
        functools.partial(attend_kernel, 256, len(ks)),
        grid=(pairs,),
        in_specs=[cols(n)] + [cols(a.shape[0]) for a in ks] * 2,
        out_specs=[cols(n), pl.BlockSpec((2, 8, n), lambda h: (h, 0, 0))],
        out_shape=[shape((n, D), BF), pltpu.HBM((2 * pairs, 8, n), F32)],
        compiler_params=params(),
        cost_estimate=cost(16 * n * kv * D, 4 * kv * D, 8 * n * kv),
        name="attend",
    )(q, *kv_arrays)


def attend_back_kernel(first, bulk, q_ref, g_ref, delta_ref, lse_ref, k_ref, v_ref, *refs):
    h = pl.program_id(0)
    *refs, dk_all, dv_all, wk_ref, wv_ref, sem = refs
    if bulk is None:
        *weights, = refs[:2]
        refs = refs[2:]
        copies = [pltpu.make_async_copy(weights[i], (wk_ref, wv_ref)[i], sem.at[i]) for i in range(2)]
    else:
        copies = bulk.copies(((AT_UK, 1), (AT_UV, 1)), refs[0], (wk_ref, wv_ref, sem))
        refs = refs[1:]

    @pl.when(h == 0)
    def _():
        for copy in copies:
            copy.start()

    if not first:
        acc_ref, *refs = refs
    p_ref, dqt_ref, dk_ref, dv_ref = refs
    n = q_ref.shape[0]
    g = g_ref[...]
    q = q_ref[...] * BF(SCALE)
    k = k_ref[...]
    v = v_ref[...]
    lane = lax.broadcasted_iota(jnp.int32, (n, 128), 1) < HD
    zero = jnp.zeros_like(q)
    dk = jnp.zeros(k.shape, F32)
    dv = jnp.zeros(k.shape, F32)
    dqs = []
    for a in range(2):
        qm = jnp.where(lane == (a == 0), q, zero)
        gm = jnp.where(lane == (a == 0), g, zero)
        p = jnp.exp(dot(k, qm, 1, 1) - lse_ref[a, 0:1, :])
        dp = dot(v, gm, 1, 1)
        ds = (p * (dp - delta_ref[a, 0:1, :])).astype(BF)
        dv = dv + dot(p.astype(BF), gm, 1, 0)
        dk = dk + dot(ds, qm, 1, 0)
        dqs.append(dot(k, ds, 0, 0))
    top_half = lax.broadcasted_iota(jnp.int32, (128, n), 0) < HD
    dqt = jnp.where(top_half, dqs[0], dqs[1])
    if not first:
        dqt = dqt + acc_ref[...]
    dqt_ref[...] = dqt
    dk = dk.astype(BF)
    dv = dv.astype(BF)
    dk_ref[...] = dk
    dv_ref[...] = dv
    for i in range(D // 128):

        @pl.when(h == i)
        def _(i=i):
            dk_all[:, i * 128 : (i + 1) * 128] = dk
            dv_all[:, i * 128 : (i + 1) * 128] = dv

    @pl.when(h == pl.num_programs(0) - 1)
    def _():
        for copy in copies:
            copy.wait()
        p_ref[...] = (dot(dk_all[...], square(wk_ref), 1, 1) + dot(dv_all[...], square(wv_ref), 1, 1)).astype(
            p_ref.dtype
        )


def attend_back(q, g, delta, lse, k, v, at, m, weights, acc, dtype):
    n = q.shape[0]
    pairs = D // 128
    bulk = weights if isinstance(weights, Bulk) else None
    weights = weights if bulk is None else (bulk.array,)

    def cols(rows, i=0):
        return pl.BlockSpec((rows, 128), lambda h: (i, h))

    by_head = pl.BlockSpec((2, 8, n), lambda h: (h, 0, 0))
    acc_spec = pl.BlockSpec((128, n), lambda h: (h, 0))
    first = acc is None
    arrays = in_hbm(q, g, delta, lse, k, v, *weights, *([] if first else [acc]))
    shapes = [pltpu.VMEM((m, D), BF)] * 2
    shapes += bulk.scratch(((AT_UK, 1), (AT_UV, 1))) if bulk else (
        [pltpu.VMEM((D, D), BF)] * 2 + [pltpu.SemaphoreType.DMA((2,))]
    )
    return pl.pallas_call(
        functools.partial(attend_back_kernel, first, bulk),
        grid=(pairs,),
        in_specs=[cols(n), cols(n), by_head, by_head, cols(m, at), cols(m, at)]
        + [any_space()] * len(weights)
        + ([] if first else [acc_spec]),
        out_specs=[pl.BlockSpec((m, D), lambda h: (0, 0)), acc_spec, cols(m), cols(m)],
        out_shape=[shape((m, D), dtype), pltpu.HBM((D, n), F32), pltpu.HBM((m, D), BF), pltpu.HBM((m, D), BF)],
        scratch_shapes=shapes,
        compiler_params=params(),
        cost_estimate=cost(44 * n * m * D, 12 * m * D, 8 * n * m),
        name="attend_back",
    )(*arrays)


def after_self_kernel(bulk, o, x, w_ref, vec, n_ref, r_ref, low_ref, cq_ref, wo, uq, sem):
    copies = bulk.copies(((AT_WO, 1), (AT_UQ, 1)), w_ref, (wo, uq, sem))
    for copy in copies:
        copy.start()

    def v(i):
        return vec[i : i + 1, :]

    copies[0].wait()
    sum_one = x[...].astype(F32) + dot(o[...], square(wo), 1, 0) + v(B_OUTPUT)
    n, r = norm(sum_one)
    low = (n * v(GAIN_A) + v(SHIFT_A)).astype(BF)
    n_ref[...] = n
    r_ref[...] = jnp.broadcast_to(r, r_ref.shape)
    low_ref[...] = low
    copies[1].wait()
    cq_ref[...] = (dot(low, square(uq), 1, 0) + v(C_QUERY)).astype(BF)


def after_self(o, x, bulk, vec):
    m = x.shape[0]
    outs = [shape((m, D), F32), shape((m, 128), F32), shape((m, D), BF), pltpu.HBM((m, D), BF)]
    return pl.pallas_call(
        functools.partial(after_self_kernel, bulk),
        grid=(1,),
        in_specs=[whole(o), whole(x), any_space(), whole(vec)],
        out_specs=[whole(s) for s in outs],
        out_shape=outs,
        scratch_shapes=bulk.scratch(((AT_WO, 1), (AT_UQ, 1))),
        compiler_params=params(),
        cost_estimate=cost(4 * m * D * D, 12 * m * D),
        name="after_self",
    )(o, x, bulk.array, vec)


GELU_C = 0.7978845608028654
GELU_A = 0.044715


FEED_WEIGHTS = ((AT_UO, 1),) + tuple((AT_EXPAND + j, 1) for j in range(4)) + ((0, 4),)


def feed_kernel(size, bulk, f_ref, ca, n1, cot, w_ref, vec,
                out_ref, two_ref, catt_ref, delta_ref, dvec_ref, *refs):
    if size == 8:
        *refs, held, sems = refs
        sums = Outbox(refs[0], held, sems)
        uo, *expand, wred_ref, sem = refs[1:]
    else:
        sums, (uo, *expand, wred_ref, sem) = refs[:-7], refs[-7:]
    copies = bulk.copies(FEED_WEIGHTS, w_ref, (uo, *expand, wred_ref, sem))
    for copy in copies:
        copy.start()

    def v(i):
        return vec[i : i + 1, :]

    copies[0].wait()
    first = n1[...] * v(GAIN_A) + v(SHIFT_A)
    sum_two = first + dot(ca[...], square(uo), 1, 0) + v(C_OUTPUT)
    n2, r2 = norm(sum_two)
    second = n2 * v(GAIN_B) + v(SHIFT_B)
    low = second.astype(BF)
    sum_three = second + v(B_REDUCE)
    acts, slopes = [], []
    for copy in copies[1:]:
        copy.wait()
    wred = square(wred_ref)
    pres = [dot(low, square(w), 1, 0) for w in expand]
    for j in range(4):
        pre = pres[j] + v(B_EXPAND + j)
        sq = pre * pre
        t = jnp.tanh(GELU_C * (pre + GELU_A * (sq * pre)))
        half = 0.5 * (1.0 + t)
        act = (pre * half).astype(BF)
        slope = half + 0.5 * pre * (1.0 - t * t) * (GELU_C * (1.0 + 3.0 * GELU_A * sq))
        acts.append(act)
        slopes.append(slope)
        sum_three = sum_three + dot(act, wred[j * D : (j + 1) * D], 1, 0)
    n3, r3 = norm(sum_three)
    out_ref[...] = (n3 * v(GAIN_C) + v(SHIFT_C)).astype(BF)
    e = cot[...].astype(F32)
    d_three = norm_back(e, v(GAIN_C), n3, r3)
    branch = d_three.astype(BF)
    dvec_ref[0:1, :] = total(branch.astype(F32))
    dvec_ref[1:2, :] = total(e * n3)
    dvec_ref[2:3, :] = total(e)
    second_grad = d_three
    d_acts = [dot(branch, wred[j * D : (j + 1) * D], 1, 1) for j in range(4)]
    for j in range(4):
        d_pre = (d_acts[j] * slopes[j]).astype(BF)
        dvec_ref[3 + j : 4 + j, :] = total(d_pre.astype(F32))
        emit(size, f_ref, sums, j, None, dot(acts[j], branch, 0, 0))
        emit(size, f_ref, sums, 4 + j, (4 + j) * D // 8, dot(low, d_pre, 0, 0))
        second_grad = second_grad + dot(d_pre, square(expand[j]), 1, 1)
    d_two = norm_back(second_grad, v(GAIN_B), n2, r2)
    two_ref[...] = d_two
    cross = d_two.astype(BF)
    dvec_ref[7:8, :] = total(second_grad * n2)
    dvec_ref[8:9, :] = total(second_grad)
    dvec_ref[9:10, :] = total(cross.astype(F32))
    att = dot(cross, square(uo), 1, 1).astype(BF)
    catt_ref[...] = att
    delta_ref[...] = head_rows(att, ca[...])
    if size == 8:
        sums.wait()


def feed(size, f, ca, n1, cot, bulk, vec):
    m = ca.shape[0]
    outs = [
        shape((m, D), BF), shape((m, D), F32), pltpu.HBM((m, D), BF), pltpu.HBM((D // HD, 8, m), F32),
        shape((16, D), F32),
    ] + sums_out(size, D, 8)
    specs = [whole(s) for s in outs]
    extra = []
    if size == 8:
        rows = D
        outs[-1] = pltpu.HBM((8, rows, D), BF)
        specs[-1] = any_space()
        extra = [pltpu.VMEM((8, rows, D), BF), pltpu.SemaphoreType.DMA((8,))]
    return pl.pallas_call(
        functools.partial(feed_kernel, size, bulk),
        grid=(1,),
        in_specs=[smem(), whole(ca), whole(n1), whole(cot), any_space(), whole(vec)],
        out_specs=specs,
        out_shape=outs,
        scratch_shapes=bulk.scratch(FEED_WEIGHTS) + extra,
        compiler_params=params(44),
        cost_estimate=cost(2 * 27 * m * D * D, 24 * m * D * 4, 4 * m * D),
        name="feed",
    )(f, ca, n1, cot, bulk.array, vec)


def after_cross_back_kernel(size, bulk, f_ref, dqt, k0, k1, v0, v1, mem, low, o, two, ca, n1, r1, w_ref, vec,
                            one_ref, att_ref, delta_ref, dvec_ref, *refs):
    sums, (uq, wo, sem) = refs[:-3], refs[-3:]
    copies = bulk.copies(((AT_UQ, 1), (AT_WO, 1)), w_ref, (uq, wo, sem))
    for copy in copies:
        copy.start()
    gain = vec[GAIN_A : GAIN_A + 1, :]
    gq = (dqt[...].T * SCALE).astype(BF)
    for copy in copies:
        copy.wait()
    first_grad = two[...] + dot(gq, square(uq), 1, 1)
    n = n1[...]
    d_one = norm_back(first_grad, gain, n, r1[:, 0:1])
    one_ref[...] = d_one
    low_one = d_one.astype(BF)
    att = dot(low_one, square(wo), 1, 1).astype(BF)
    att_ref[...] = att
    delta_ref[...] = head_rows(att, o[...])
    m = k0.shape[0]
    dvec_ref[0:1, :] = total(gq.astype(F32))
    dvec_ref[1:2, :] = total(first_grad * n)
    dvec_ref[2:3, :] = total(first_grad)
    dvec_ref[3:4, :] = total(low_one.astype(F32))
    dvec_ref[4:5, :] = total(v0[...].astype(F32)) + total(v1[...].astype(F32))
    r = D // 8
    emit(size, f_ref, sums, 0, 0, dot(low[...], gq, 0, 0))
    emit(size, f_ref, sums, 1, r, dot(mem[0:m, :], k0[...], 0, 0) + dot(mem[m:, :], k1[...], 0, 0))
    emit(size, f_ref, sums, 2, 2 * r, dot(mem[0:m, :], v0[...], 0, 0) + dot(mem[m:, :], v1[...], 0, 0))
    emit(size, f_ref, sums, 3, 3 * r, dot(o[...], low_one, 0, 0))
    emit(size, f_ref, sums, 4, 4 * r, dot(ca[...], two[...].astype(BF), 0, 0))


def after_cross_back(size, f, dqt, ks, vs, mem, low, o, two, ca, n1, r1, bulk, vec):
    m = low.shape[0]
    arrays = in_hbm(dqt, *ks, *vs, mem) + [low, o, two, ca, n1, r1]
    outs = [shape((m, D), F32), pltpu.HBM((m, D), BF), pltpu.HBM((D // HD, 8, m), F32), shape((8, D), F32)]
    outs += sums_out(size, 5 * D // 8, 5, True)
    return pl.pallas_call(
        functools.partial(after_cross_back_kernel, size, bulk),
        grid=(1,),
        in_specs=[smem()] + [whole(a) for a in arrays] + [any_space(), whole(vec)],
        out_specs=[whole(s) for s in outs],
        out_shape=outs,
        scratch_shapes=bulk.scratch(((AT_UQ, 1), (AT_WO, 1))),
        compiler_params=params(24),
        cost_estimate=cost(2 * 8 * m * D * D, 14 * m * D * 4),
        name="after_cross_back",
    )(f, *arrays, bulk.array, vec)


def last_kernel(size, count, f_ref, dqt, *refs):
    ks, vs = refs[:count], refs[count : 2 * count]
    x0, x1, x_far, feed, mid, gq_ref = refs[2 * count : 2 * count + 6]
    *sums, table = refs[2 * count + 6 :]
    m = x0.shape[0]
    xs = [x0[...], x1[...], x_far[0:m, :], x_far[m:, :]]
    gq = (dqt[...].T * SCALE).astype(BF)
    gq_ref[...] = gq
    r = D // 8
    emit(size, f_ref, sums, 0, 0, dot(xs[0], gq, 0, 0))
    for i, parts in ((1, ks), (2, vs)):
        acc = dot(xs[0], parts[0][...], 0, 0)
        for x, p in zip(xs[1:], parts[1:]):
            acc = acc + dot(x, p[...], 0, 0)
        emit(size, f_ref, sums, i, i * r, acc)
    table[...] = jnp.zeros_like(table)
    table[B_QUERY : B_QUERY + 1, :] = total(gq.astype(F32))
    dbv = total(vs[0][...].astype(F32))
    for v in vs[1:]:
        dbv = dbv + total(v[...].astype(F32))
    table[B_VALUE : B_VALUE + 1, :] = dbv
    for at, src, i in (
        (B_OUTPUT, mid, 3), (GAIN_A, mid, 1), (SHIFT_A, mid, 2), (C_QUERY, mid, 0), (C_VALUE, mid, 4),
        (C_OUTPUT, feed, 9), (GAIN_B, feed, 7), (SHIFT_B, feed, 8),
        (B_REDUCE, feed, 0), (GAIN_C, feed, 1), (SHIFT_C, feed, 2),
    ):
        table[at : at + 1, :] = src[i : i + 1, :]
    if size != 8:
        table[B_EXPAND : B_EXPAND + 4, :] = feed[3:7, :]
        return
    rows = table[0:16, :].astype(BF)
    for chip in range(4):
        wide = jnp.broadcast_to(feed[3 + chip : 4 + chip, :], (16, D)).astype(BF)
        for s in sums:
            s[chip, 3 * r : 3 * r + 16, :] = jnp.zeros((16, D), BF)
            s[chip, 3 * r : 3 * r + 16, 0:128] = rows[:, chip * 128 : (chip + 1) * 128]
            s[chip, 3 * r + 16 : 3 * r + 32, :] = wide


def last(size, f, dqt, ks, vs, xs, feed, mid):
    m = xs[0].shape[0]
    count = len(ks)
    arrays = [f, *in_hbm(dqt, *ks, *vs, *xs), feed, mid]
    outs = [shape((m, D), BF)] + sums_out(size, 3 * D // 8 + 32, 3, True) + [shape((VEC_ROWS, D), F32)]
    return pl.pallas_call(
        functools.partial(last_kernel, size, count),
        grid=(1,),
        in_specs=[smem()] + [whole(a) for a in arrays[1:]],
        out_specs=[whole(s) for s in outs],
        out_shape=outs,
        compiler_params=params(),
        cost_estimate=cost(2 * 9 * m * D * D, 14 * m * D * 2),
        name="last",
    )(*arrays)


def own_rows_kernel(gq, part, one, wq, out):
    out[...] = part[...] + one[...] + dot(gq[...], wq[...], 1, 1)


def own_rows(gq, part, one, wq):
    return pl.pallas_call(
        own_rows_kernel,
        out_shape=shape(part.shape, F32),
        compiler_params=params(),
        cost_estimate=cost(2 * part.shape[0] * D * D, 4 * part.shape[0] * D * 4),
        name="own_rows",
    )(gq, part, one, wq)


def fold_kernel(t_ref, *refs):
    acc = refs[0][...].astype(F32)
    for r in refs[1:-1]:
        acc = acc + r[...].astype(F32)
    refs[-1][...] = acc.astype(BF)


def fold(table, base, count, arrays):
    n = arrays[0].shape[1]
    width = len(arrays)

    def spec(k):
        return pl.BlockSpec((1, n, D), lambda j, t: (t[base + j * width + k], 0, 0))

    return pl.pallas_call(
        fold_kernel,
        grid_spec=pltpu.PrefetchScalarGridSpec(
            num_scalar_prefetch=1,
            grid=(count,),
            in_specs=[spec(k) for k in range(width)],
            out_specs=pl.BlockSpec((1, n, D), lambda j, t: (j, 0, 0)),
        ),
        out_shape=shape((count, n, D), BF),
        compiler_params=params(6),
        name="fold",
    )(table, *arrays)


def start_rows(arrays, out, sems):
    copies = []
    at = 0
    for ref in arrays:
        rows = ref.shape[0]
        for j in range(ref.shape[1] // D):
            copies.append(pltpu.make_async_copy(
                ref.at[:, pl.ds(j * D, D)], out.at[pl.ds(at, rows), :], sems.at[len(copies)]
            ))
            copies[-1].start()
            at += rows
    return copies


def pack_kernel(*refs):
    *arrays, out, sems = refs
    for copy in start_rows(arrays, out, sems):
        copy.wait()


def pack_plain(arrays):
    return jnp.concatenate([a[:, i : i + D] for a in arrays for i in range(0, a.shape[1], D)])


def pack_rows(arrays):
    if arrays[0].shape[0] % 16:
        return pack_plain(arrays)
    pieces = sum(a.shape[1] // D for a in arrays)
    rows = sum(a.shape[0] * a.shape[1] // D for a in arrays)
    return pl.pallas_call(
        pack_kernel,
        in_specs=[any_space()] * len(arrays),
        out_shape=shape((rows, D), BF),
        scratch_shapes=[pltpu.SemaphoreType.DMA((pieces,))],
        compiler_params=params(4),
        name="pack_rows",
    )(*in_hbm(*arrays))


def table_kernel(rows, count, *refs):
    arrays, refs = refs[:count], refs[count:]
    *vectors, expand, out, table, short, long, sems, vec_sems = refs
    copies = start_rows(arrays, out, sems)
    loads = [pltpu.make_async_copy(ref, short.at[i], vec_sems.at[i]) for i, ref in enumerate(vectors)]
    loads.append(pltpu.make_async_copy(expand, long, vec_sems.at[len(vectors)]))
    for load in loads:
        load.start()
    table[...] = jnp.zeros_like(table)
    for load in loads:
        load.wait()
    for i in range(len(vectors)):
        table[i : i + 1, 0:rows] = short[i].astype(F32)
    for j in range(4):
        table[B_EXPAND + j : B_EXPAND + j + 1, 0:rows] = long[:, j * rows : (j + 1) * rows].astype(F32)
    out[len(copies) * rows :, :] = table[...].astype(BF)
    for copy in copies:
        copy.wait()


def pack_first(arrays, vectors, expand):
    rows = vectors[0].shape[0]
    plain = rows % 16 != 0
    used = [] if plain else arrays
    vectors = [v.reshape(1, -1) for v in vectors]
    out = pl.pallas_call(
        functools.partial(table_kernel, rows, len(used)),
        in_specs=[any_space()] * (len(used) + len(vectors) + 1),
        out_shape=shape((len(used) * rows + VEC_ROWS, D), BF),
        scratch_shapes=[
            pltpu.VMEM((VEC_ROWS, D), F32), pltpu.VMEM((len(vectors), 1, rows), BF),
            pltpu.VMEM((1, 4 * rows), BF), pltpu.SemaphoreType.DMA((len(arrays),)),
            pltpu.SemaphoreType.DMA((len(vectors) + 1,)),
        ],
        compiler_params=params(4),
        name="pack_first",
    )(*in_hbm(*used, *vectors, expand.reshape(1, -1)))
    return pack_plain([*arrays, out]) if plain else out


ENDS_IN = ((1, 0), (2, 3))
ENDS_OUT = ((0, 1), (3, 2))
MIDDLE = ((1, 2), (2, 1))
PAIRS = ((0, 1), (1, 0), (2, 3), (3, 2))
ACROSS = ((0, 2), (2, 0), (1, 3), (3, 1))


def over_seq(x, pairs):
    return lax.ppermute(x, "seq", pairs)


def after(x, *deps):
    return lax.optimization_barrier((x,) + deps)[0]


def add(p, r):
    return (p.astype(F32) + r.astype(F32)).astype(BF)


def swap_core():
    return [(i, i ^ 1) for i in range(8)]


def swap_first():
    return [(i, i ^ (4 if i & 1 else 2)) for i in range(8)]


def swap_second():
    return [(i, i ^ (2 if i & 1 else 4)) for i in range(8)]


def gather_plane(own, deps, late):
    r1 = lax.ppermute(own, "fsdp", swap_first())
    both = after(jnp.concatenate([own, r1]), *deps)
    r2 = lax.ppermute(both, "fsdp", swap_second())
    r3 = lax.ppermute(after(jnp.concatenate([both, r2]), *late), "fsdp", swap_core())
    return r1, r2, r3


def fold_table(f):
    c = lax.rem(f, 2)
    x = lax.rem(f // 2, 2)
    y = f // 4
    even = c == 0
    send0 = jnp.where(even, 1 - x, 2 * (1 - y))
    send1 = jnp.where(even, 3 - x, 3 - 2 * y)
    keep0 = jnp.where(even, x, 2 * y)
    keep1 = jnp.where(even, 2 + x, 2 * y + 1)
    own = jnp.where(even, y, x)
    mine = jnp.where(own == 0, keep0, keep1)
    other = jnp.where(own == 0, keep1, keep0)
    zero = 0 * own
    return jnp.stack([send0, send0, send1, send1, other, other, 1 - own, mine, mine, own, zero]).astype(jnp.int32)


class PlaneReduce:
    def __init__(self, table, sums):
        self.table = table
        self.keep = sums[1]
        self.got = [lax.ppermute(sums[0], "fsdp", swap_core())]

    def second(self, *deps):
        out = fold(self.table, 0, 2, [after(self.keep, *deps), self.got[0]])
        self.got.append(lax.ppermute(out, "fsdp", swap_first()))

    def third(self, *deps):
        out = fold(self.table, 4, 1, [after(self.keep, *deps)] + self.got)
        self.got.append(lax.ppermute(out, "fsdp", swap_second()))

    def end(self, *deps):
        return fold(self.table, 7, 1, [after(self.keep, *deps)] + self.got)[0]


class PlainReduce:
    def __init__(self, table, sums):
        self.got = [lax.psum_scatter(sums, "fsdp", scatter_dimension=0, tiled=False)]

    def second(self, *deps):
        pass

    third = second

    def end(self, *deps):
        return self.got[0]


def on_device(size, tokens, memory, cotangent,
              w_query, w_key, w_value, w_output, b_query, b_value, b_output, gain_attend, shift_attend,
              u_query, u_key, u_value, u_output, c_query, c_value, c_output, gain_cross, shift_cross,
              w_expand, b_expand, w_reduce, b_reduce, gain_feed, shift_feed):
    rows = w_query.shape[0]
    f = lax.axis_index("fsdp")
    x = tokens[0]
    mem = memory[0]

    vectors = (b_query, b_value, b_output, gain_attend, shift_attend, c_query, c_value, c_output,
               gain_cross, shift_cross, b_reduce, gain_feed, shift_feed)
    first = pack_first([w_query, w_key, w_value], vectors, b_expand)
    pack = pack_rows([w_reduce, w_expand, w_output, u_query, u_key, u_value, u_output])
    c1 = over_seq(x, PAIRS)
    x_b = over_seq(x, MIDDLE)
    x_d = over_seq(c1, MIDDLE)
    x_c = over_seq(x_b, ENDS_IN)
    mem_near = over_seq(after(mem, c1, x_b), PAIRS)
    if size == 8:
        r1, r2, r3 = gather_plane(first, (c1, x_b), (x_d, x_c, mem_near))
        wq, wk, wv = assemble(f, rows, 3, first, r1, r2, r3)
        n = first.shape[0]
        tables = [first, r1, r2[:n], r2[n:]] + [r3[i * n : (i + 1) * n] for i in range(4)]
        tables = jnp.stack([t[3 * rows : 3 * rows + N_VEC, :rows] for t in tables])
        c = lax.rem(f, 2)
        a, b = 2 + 2 * c, 4 - 2 * c
        offsets = jnp.stack([0 * c, a, b, 6 + 0 * c, 1 + 0 * c, b + 1, a + 1, 7 + 0 * c])
        pick = (jnp.arange(8)[:, None] == (offsets ^ f)[None, :]).astype(BF)
        tables = jnp.einsum("gd,dkl->gkl", pick, tables, preferred_element_type=F32)
    else:
        g = lax.all_gather(first, "fsdp", axis=0, tiled=False)
        wq, wk, wv = [g[:, i * rows : (i + 1) * rows].reshape(D, D) for i in range(3)]
        tables = g[:, 3 * rows : 3 * rows + N_VEC, :rows].astype(F32)
    vec = jnp.concatenate(
        [tables[:, :B_EXPAND].transpose(1, 0, 2).reshape(B_EXPAND, D), tables[:, B_EXPAND:].reshape(4, D)]
    )
    vec = jnp.pad(vec, ((0, VEC_ROWS - N_VEC), (0, 0)))

    everything = lax.all_gather(pack, "fsdp", axis=0, tiled=False)

    if size != 8:
        blocks = [everything[:, : 4 * rows].reshape(4, D, D)]
        for i in range(4, 13):
            blocks.append(everything[:, i * rows : (i + 1) * rows].reshape(1, D, D))
        everything = jnp.concatenate(blocks)
    bulk = Bulk(everything, size)

    def by_owner(stack, count):
        s = stack.reshape(count, size, rows, D)
        return s.transpose(1, 0, 2, 3).reshape(size, count * rows, D)

    def reduce(sums, tall, count, extra=None):
        if size == 8 and len(sums) == 2:
            return PlaneReduce(table, sums)
        if size == 8:
            return PlainReduce(table, sums[0])
        s = sums[0]
        blocks = [s[: 4 * D].reshape(size, 4 * rows, D), s[4 * D :]] if tall else [s]
        blocks[-1] = by_owner(blocks[-1], count)
        return PlainReduce(table, jnp.concatenate(blocks + ([] if extra is None else [extra]), 1))

    table = fold_table(f)
    f1 = f.reshape(1).astype(jnp.int32)
    z1 = lax.axis_index("seq").reshape(1).astype(jnp.int32)
    q, k0, v0 = project(x, c1, wq, wk, wv, vec)
    x_e = over_seq(x_d, ENDS_IN)
    mem_mid = over_seq(after(jnp.concatenate([mem, mem_near]), x_d), MIDDLE)
    x_far, k1, v1 = project_far(z1, x_b, x_c, x_d, after(x_e, k0), wk, wv, vec)
    mem_in = over_seq(after(mem_mid, x_far), ENDS_IN)
    o, lse = attend(q, [k0, k1], [v0, v1])
    n1, r_one, low, cq = after_self(o, x, bulk, vec)
    mem_x, mk, mv = project_memory(z1, mem, mem_near, mem_mid, after(mem_in, low), bulk, vec)
    ca, cross_lse = attend(cq, [mk], [mv])
    layer_out, d_two, d_catt, cross_delta, dvec_feed, *sums = feed(
        size, f1, ca, n1, cotangent[0], bulk, vec
    )
    feed_sum = reduce(sums, True, 4)

    m = 2 * mem.shape[0]
    def cross_back(g, i, acc, dtype):
        return attend_back(cq, g, cross_delta, cross_lse, mk, mv, i, m, bulk, acc, dtype)

    far, dqt, dk1, dv1 = cross_back(d_catt, 1, None, BF)
    far_in = over_seq(far, ENDS_OUT)
    near, dqt, dk0, dv0 = cross_back(after(d_catt, far), 0, dqt, F32)
    d_one, d_att, self_delta, dvec_mid, *sums = after_cross_back(
        size, f1, after(dqt, far_in), (dk0, dk1), (dv0, dv1), mem_x, low, o, d_two, ca, n1, r_one, bulk, vec
    )
    mid_sum = reduce(sums, False, 5)
    far_mid = over_seq(after(add(far, far_in), d_att), MIDDLE)
    m = x.shape[0]

    def self_back(g, i, acc, dtype):
        k, v = ((k0, v0), (k1, v1))[i // 2]
        return attend_back(q, g, self_delta, lse, k, v, i % 2, m, (wk, wv), acc, dtype)

    p3, dqt, dk3, dv3 = self_back(d_att, 3, None, BF)
    e = over_seq(p3, ENDS_OUT)
    mid_sum.second(p3)
    half = m // 2
    p2, dqt, dk2, dv2 = self_back(after(d_att, p3, feed_sum.got[0], mid_sum.got[0]), 2, dqt, BF)
    feed_part = feed_sum.end()
    sum_feed = lax.psum(feed_part, "seq")
    cc = over_seq(p2, ENDS_OUT)
    mid_sum.third(p2)
    p1, dqt, dk1, dv1 = self_back(after(d_att, e, far_mid, p2, mid_sum.got[-2 if size == 8 else 0]), 1, dqt, BF)
    near_in = over_seq(after(add(near[half:], far_mid[half:]), p1), PAIRS)
    d = over_seq(after(add(p3, e), p1), MIDDLE)
    mid_part = mid_sum.end(p1)
    mid_in = over_seq(mid_part, PAIRS)
    p0, dqt, dk0, dv0 = self_back(after(d_att, cc, p1, mid_part), 0, dqt, F32)
    b = over_seq(after(add(p2, cc), p0), MIDDLE)
    mid_part = add(mid_part, after(mid_in, p0))
    dqt = after(dqt, d, mid_part, sum_feed)
    mid_in = over_seq(mid_part, ACROSS)
    gq, *sums, vec_table = last(
        size, f1, dqt, (dk0, dk1, dk2, dk3), (dv0, dv1, dv2, dv3), (x, c1, x_far), dvec_feed, dvec_mid
    )
    extra = None
    if size != 8:
        extra = jnp.concatenate([
            vec_table[:B_EXPAND].reshape(B_EXPAND, size, rows).transpose(1, 0, 2),
            vec_table[B_EXPAND:N_VEC].reshape(size, 4, rows),
        ], 1)
        extra = jnp.pad(extra, ((0, 0), (0, VEC_ROWS - N_VEC), (0, D - rows))).astype(BF)
    late_sum = reduce(sums, False, 3, extra)
    tok_mine = own_rows(gq, p0, d_one, wq)
    a = over_seq(after(add(p1, d), gq), PAIRS)
    late_sum.second()
    late_sum.third()
    late = late_sum.end()
    late_end = late
    got = over_seq(late, PAIRS)
    late = add(late, got)
    got = over_seq(late, ACROSS)
    sum_last = late.astype(F32) + got.astype(F32)
    sum_feed = sum_feed.astype(F32)
    sum_mid = mid_part.astype(F32) + mid_in.astype(F32)
    grad_tok = after(tok_mine, late_end) + a.astype(F32) + b.astype(F32)
    grad_mem = after(near[:half], late_end) + near_in.astype(F32) + far_mid[:half].astype(F32)
    sum_feed = after(sum_feed, late_end)

    if size == 8:
        c = lax.rem(f, 2)
        vecs = lax.dynamic_slice(sum_last, (3 * rows, c * rows), (B_EXPAND, rows))
        db_expand = lax.dynamic_slice(sum_last, (3 * rows + 16, c * 4 * rows), (1, 4 * rows)).reshape(4 * rows)
    else:
        vecs = sum_last[3 * rows : 3 * rows + N_VEC, :rows]
        db_expand = vecs[B_EXPAND:].reshape(4 * rows)
    dw_reduce = sum_feed[: 4 * rows]
    dw_expand = jnp.concatenate([sum_feed[(4 + j) * rows : (5 + j) * rows] for j in range(4)], 1)
    du_query, du_key, du_value, dw_output, du_output = [sum_mid[i * rows : (i + 1) * rows] for i in range(5)]
    dw_query, dw_key, dw_value = [sum_last[i * rows : (i + 1) * rows] for i in range(3)]
    return (
        layer_out[None], grad_tok[None], grad_mem[None],
        dw_query, dw_key, dw_value, dw_output, vecs[0], vecs[1], vecs[2], vecs[3], vecs[4],
        du_query, du_key, du_value, du_output, vecs[5], vecs[6], vecs[7], vecs[8], vecs[9],
        dw_expand, db_expand, dw_reduce, vecs[10], vecs[11], vecs[12],
    )


def solution(mesh):
    rows = P("fsdp", "seq", None)
    mat, vec = P("fsdp", None), P("fsdp")
    weights = (mat,) * 4 + (vec,) * 5 + (mat,) * 4 + (vec,) * 5 + (mat, vec, mat, vec, vec, vec)
    return jax.shard_map(
        functools.partial(on_device, mesh.shape["fsdp"]),
        mesh=mesh,
        in_specs=(rows,) * 3 + weights,
        out_specs=(rows,) * 3 + weights,
        check_vma=False,
    )
```
